32 devices in a mesh: row: 8 (over z, x), col: 4 (over y, core).
Axes of the slice: x: 2, y: 2, z: 4, core: 2. Of those that a mesh axis runs over, the one named last changes fastest.
Arguments:
- tokens: bfloat16 [4096, 768], P(('row', 'col')), may hold values from -6 to 6
- w_qkv: bfloat16 [768, 3, 768], P('row', None, 'col'), may hold values from -0.21875 to 0.21875
- w_out: bfloat16 [768, 768], P('col', 'row'), may hold values from -2.5 to 2.5
- w_gate_up: bfloat16 [768, 2, 3072], P('row', None, 'col'), may hold values from -0.21875 to 0.21875
- w_down: bfloat16 [3072, 768], P('col', 'row'), may hold values from -0.109375 to 0.109375
- gain1: float32 [768], replicated, may hold values from 0.1 to 1.9
- bias1: float32 [768], replicated, may hold values from -1.8 to 1.8
- gain2: float32 [768], replicated, may hold values from 0.1 to 1.9
- bias2: float32 [768], replicated, may hold values from -1.8 to 1.8
- cotangent: bfloat16 [4096, 768], P(('row', 'col')), may hold values from -6 to 6
- seq_lengths: int32 [3], replicated, may hold values from 512 to 2048, as said below
- packed_order: int32 [4096], replicated, may hold values from 0 to 4095, each once
Outputs:
- output: bfloat16 [4096, 768], P(('row', 'col'))
- grad_tokens: float32 [4096, 768], P(('row', 'col'))
- grad_w_qkv: float32 [768, 3, 768], P('row', None, 'col')
- grad_w_out: float32 [768, 768], P('col', 'row')
- grad_w_gate_up: float32 [768, 2, 3072], P('row', None, 'col')
- grad_w_down: float32 [3072, 768], P('col', 'row')
- grad_gain1: float32 [768], replicated
- grad_bias1: float32 [768], replicated
- grad_gain2: float32 [768], replicated
- grad_bias2: float32 [768], replicated
The draws below stay inside these ranges and needn't reach their ends.
Inputs may be any that keep to these rules, and one draw needn't show every extreme that they name: `seq_lengths`: 3 lengths that sum to 4096; the longest is exactly 2048.
All inputs are finite; a program needn't handle non-finite values.
Results may differ from the reference program's by a relative error of at most 0.024.
Values may be sent and summed in bfloat16 or wider, within the bound.
No kernel may reach another device: no remote copies, remote signals or barrier semaphores. Data moves between devices by JAX's collectives and lax.ppermute only.
A program may use at most 512 MiB of HBM per device.

```python
import math
import jax
import jax.numpy as jnp
from jax import lax

D = 768
HEADS = 12
FF = 3072
HEAD = 64
TOKENS = 4096
SEQS = 3
LONGEST = 2048


def draw_seq_lengths(key, part):
    others = SEQS - 1
    longest = LONGEST
    remain = TOKENS - longest
    base = TOKENS // (4 * others)
    extra = remain - others * base
    keys_two = jax.random.split(key, 2)
    shares = jax.random.randint(keys_two[0], (others,), 500, 1001).astype(jnp.int32)
    running = jnp.cumsum(shares).astype(jnp.int32)
    bounds = extra * running // running[-1]
    pieces = bounds - jnp.concatenate([jnp.zeros((1,), jnp.int32), bounds[:-1]])
    lengths = jnp.concatenate([jnp.full((1,), longest, jnp.int32), base + pieces]).astype(jnp.int32)
    order = jax.random.permutation(keys_two[1], SEQS)
    return lengths[order].astype(jnp.int32)


def block_levels(own_key, extent, cuts, smallest, top_value):
    level, own = 1.0, jax.random.fold_in(own_key, 6)
    for dim, shards_of in cuts:
        draws = jnp.exp(jax.random.uniform(jax.random.fold_in(own, dim), (shards_of,), jnp.float32, smallest / len(cuts), top_value / len(cuts)))
        level = level * jnp.repeat(draws, extent[dim] // shards_of).reshape([-1 if axis == dim else 1 for axis in range(len(extent))])
    return level


def normal_values(own_key, dims, deviation, bound, cuts=(), kind=jnp.bfloat16):
    values = deviation * jax.random.normal(own_key, dims, jnp.float32)
    if cuts:
        values = values * block_levels(own_key, dims, cuts, -0.22, 0.18)
    return jnp.clip(values, -bound, bound).astype(kind)


def setup_inputs(seed: int = 0) -> dict:
    arg_keys = jax.random.split(jax.random.key(seed), 13)
    return {
        "tokens": normal_values(arg_keys[0], (TOKENS, D), 1.0, 6.0, ((0, 32),)),
        "w_qkv": normal_values(arg_keys[1], (D, 3, D), D ** -0.5, 0.21875, ((0, 8), (2, 4))),
        "w_out": normal_values(arg_keys[2], (D, D), (max(1, D * 32 // TOKENS)) ** -0.5, 2.5, ((0, 4), (1, 8))),
        "w_gate_up": normal_values(arg_keys[3], (D, 2, FF), D ** -0.5, 0.21875, ((0, 8), (2, 4))),
        "w_down": normal_values(arg_keys[4], (FF, D), FF ** -0.5, 0.109375, ((0, 4), (1, 8))),
        "gain1": jnp.clip(1.0 + 0.18 * jax.random.normal(arg_keys[5], (D,), jnp.float32), 0.1, 1.9),
        "bias1": normal_values(arg_keys[6], (D,), 0.3, 1.8, (), jnp.float32),
        "gain2": jnp.clip(1.0 + 0.18 * jax.random.normal(arg_keys[7], (D,), jnp.float32), 0.1, 1.9),
        "bias2": normal_values(arg_keys[8], (D,), 0.3, 1.8, (), jnp.float32),
        "cotangent": normal_values(arg_keys[9], (TOKENS, D), 1.0, 6.0, ((0, 32),)),
        "seq_lengths": draw_seq_lengths(jax.random.fold_in(arg_keys[12], 71), 0),
        "packed_order": jax.random.permutation(arg_keys[11], TOKENS).astype(jnp.int32),
    }


@jax.custom_vjp
def low(v):
    return lax.optimization_barrier(v.astype(jnp.bfloat16)).astype(jnp.float32)

@jax.custom_vjp
def low_back(v):
    return v

def low_keep(v):
    return (low(v), None)

def low_pass(kept, grad):
    return (grad,)

def back_keep(v):
    return (v, None)

def back_low(kept, grad):
    return (low(grad),)
low.defvjp(low_keep, low_pass)
low_back.defvjp(back_keep, back_low)
HIGH = lax.Precision.HIGHEST
ROPE_BASE = 1000.0
NORM_EPS = 1e-12
MASKED = -1e+30

def token_layout(seq_lengths, packed_order):
    seq_ends = jnp.cumsum(seq_lengths).astype(jnp.int32)
    seq_starts = seq_ends - seq_lengths
    seq_id = lax.optimization_barrier(jnp.sum((packed_order[:, None] >= seq_ends[None, :]).astype(jnp.int32), axis=1))
    member = seq_id[:, None] == jnp.arange(seq_lengths.shape[0], dtype=jnp.int32)[None, :]
    start_of = lax.optimization_barrier(jnp.sum(jnp.where(member, seq_starts[None, :], 0), axis=1))
    return (seq_id.astype(jnp.int32), (packed_order - start_of).astype(jnp.int32))

def rope_tables(positions, head):
    half = head // 2
    freqs = ROPE_BASE ** (-jnp.arange(half, dtype=jnp.float32) * 2.0 / head)
    angles = positions.astype(jnp.float32)[:, None] * freqs[None, :]
    return (jnp.cos(angles), jnp.sin(angles))

def rotate(field, cosine, sine):
    half = field.shape[-1] // 2
    first = field[..., :half]
    second = field[..., half:]
    cos_b = cosine[:, None, :]
    sin_b = sine[:, None, :]
    return jnp.concatenate([first * cos_b - second * sin_b, second * cos_b + first * sin_b], axis=-1)

def layer_norm(values, gain, bias):
    centered = values - lax.optimization_barrier(jnp.mean(values, axis=-1, keepdims=True))
    inverse = lax.rsqrt(lax.optimization_barrier(jnp.mean(centered * centered, axis=-1, keepdims=True)) + NORM_EPS)
    return centered * inverse * gain + bias

def forward(tokens, w_qkv, w_out, w_gate_up, w_down, gain1, bias1, gain2, bias2, seq_id, cosine, sine):
    count = tokens.shape[0]
    scale = 1.0 / math.sqrt(HEAD)
    mixed = low_back(jnp.einsum('td,dce->tce', tokens, w_qkv, precision=HIGH))
    queries = low(rotate(mixed[:, 0].reshape(count, HEADS, HEAD), cosine, sine))
    keys = low(rotate(mixed[:, 1].reshape(count, HEADS, HEAD), cosine, sine))
    values = low(mixed[:, 2].reshape(count, HEADS, HEAD))
    block = math.gcd(count, 512)
    query_blocks = queries.reshape(count // block, block, HEADS, HEAD)
    seg_blocks = seq_id.reshape(count // block, block)

    def attend(pair):
        query_rows, seg_rows = pair
        scores = jnp.einsum('qhd,khd->hqk', query_rows, keys, precision=HIGH) * scale
        scores = low_back(scores)
        same = seg_rows[:, None] == seq_id[None, :]
        scores = jnp.where(same[None], scores, MASKED)
        weights = jax.nn.softmax(scores, axis=-1)
        return jnp.einsum('hqk,khd->qhd', low(weights), values, precision=HIGH)
    context = lax.map(jax.checkpoint(attend), (query_blocks, seg_blocks)).reshape(count, D)
    context = low_back(low(context))
    attn = low_back(jnp.dot(context, w_out, precision=HIGH))
    hidden1 = layer_norm(tokens + attn, gain1, bias1)
    gate_up = low_back(jnp.einsum('td,dcf->tcf', low(hidden1), w_gate_up, precision=HIGH))
    inner = low(jax.nn.silu(gate_up[:, 1]) * gate_up[:, 0])
    ffn = low_back(jnp.dot(inner, w_down, precision=HIGH))
    return layer_norm(hidden1 + ffn, gain2, bias2)

def reference(tokens, w_qkv, w_out, w_gate_up, w_down, gain1, bias1, gain2, bias2, cotangent, seq_lengths, packed_order):
    seq_id, positions = token_layout(seq_lengths, packed_order)
    cosine, sine = rope_tables(positions, HEAD)
    floats = tuple((arr.astype(jnp.float32) for arr in (tokens, w_qkv, w_out, w_gate_up, w_down, gain1, bias1, gain2, bias2)))

    def run(tok_in, wq_in, wo_in, wgu_in, wd_in, g1_in, b1_in, g2_in, b2_in):
        return forward(tok_in, wq_in, wo_in, wgu_in, wd_in, g1_in, b1_in, g2_in, b2_in, seq_id, cosine, sine)
    result, pullback = jax.vjp(run, *floats)
    grads = pullback(cotangent.astype(jnp.float32))
    return (result.astype(jnp.bfloat16), grads[0], grads[1], grads[2], grads[3], grads[4], grads[5], grads[6], grads[7], grads[8])
```

```python
import functools
import math

import jax
import jax.numpy as jnp
from jax import lax
from jax.experimental import pallas as pl
from jax.experimental.pallas import tpu as pltpu
from jax.sharding import PartitionSpec as P

HEAD = 64
ROPE_BASE = 1000.0
NORM_EPS = 1e-12
FAR = -(2.0**100)
LOWEST = -1e30
AUX = 16
BF = jnp.bfloat16
F32 = jnp.float32

CYCLE = (0, 2, 4, 6, 7, 5, 3, 1)
OFFSETS = (0, 2, 1, 3)


def dot(a, b, contract, out=F32):
    return lax.dot_general(a, b, (contract, ((), ())), preferred_element_type=out)


NN = ((1,), (0,))
NT = ((1,), (1,))
TN = ((0,), (0,))


def forward_hop(v):
    n = len(CYCLE)
    return lax.ppermute(v, "row", [(CYCLE[i], CYCLE[(i + 1) % n]) for i in range(n)])


def backward_hop(v):
    n = len(CYCLE)
    return lax.ppermute(v, "row", [(CYCLE[(i + 1) % n], CYCLE[i]) for i in range(n)])


def col_swap(v, mask):
    count = lax.axis_size("col")
    return lax.ppermute(v, "col", [(i, i ^ mask) for i in range(count)])


def row_swap(v, mask):
    count = lax.axis_size("row")
    return lax.ppermute(v, "row", [(i, i ^ mask) for i in range(count)])


def cycle_place():
    row = lax.axis_index("row")
    return sum(jnp.where(row == CYCLE[i], i, 0) for i in range(len(CYCLE))).astype(jnp.int32)


def cycle_row(place):
    place = lax.rem(place + 2 * len(CYCLE), len(CYCLE))
    return sum(jnp.where(place == i, CYCLE[i], 0) for i in range(len(CYCLE))).astype(jnp.int32)


STEPS = (0, -1, 1, -2, 2, -3, 3, 4)


def cycle_gather(block):
    half = block.shape[0] // 2
    ahead = back = block
    out = [block]
    for _ in range(3):
        ahead, back = forward_hop(ahead), backward_hop(back)
        out += [ahead, back]
    far = jnp.concatenate([forward_hop(ahead[:half]), backward_hop(back[half:])], axis=0)
    return out + [far]


def cycle_scatter(full, place):
    count = full.shape[0] // len(CYCLE)
    half = count // 2

    def part(step, begin=0, size=count):
        return lax.dynamic_slice_in_dim(full, cycle_row(place + step) * count + begin, size, 0)

    def add(v, step):
        return (v.astype(F32) + part(step).astype(F32)).astype(BF)

    ahead = forward_hop(part(4, 0, half).astype(BF))
    back = backward_hop(part(4, half, half).astype(BF))
    third, fifth = part(3), part(5)
    ahead = jnp.concatenate(
        [(ahead.astype(F32) + third[:half].astype(F32)).astype(BF), third[half:].astype(BF)], axis=0
    )
    back = jnp.concatenate(
        [fifth[:half].astype(BF), (back.astype(F32) + fifth[half:].astype(F32)).astype(BF)], axis=0
    )
    for step in (2, 1):
        ahead, back = add(forward_hop(ahead), step), add(backward_hop(back), -step)
    ahead, back = forward_hop(ahead), backward_hop(back)
    return part(0).astype(F32) + ahead.astype(F32) + back.astype(F32)


def row_scatter(full, place):
    if place is None:
        return lax.psum_scatter(full.astype(F32), "row", scatter_dimension=0, tiled=True)
    return cycle_scatter(full, place)


def col_gather(v):
    pair = jnp.concatenate([v, col_swap(v, 2)], axis=0)
    return jnp.concatenate([pair, col_swap(pair, 1)], axis=0)


def col_scatter(full):
    half = full.shape[0] // 2
    quarter = half // 2
    other = col_swap(full[half:], 1)
    far = full[quarter:half].astype(F32) + other[quarter:].astype(F32)
    near = full[:quarter].astype(F32) + other[:quarter].astype(F32)
    return near + col_swap(far.astype(BF), 2).astype(F32)


def sum_everywhere(v):
    for axis, swap in (("col", col_swap), ("row", row_swap)):
        mask = 1
        while mask < lax.axis_size(axis):
            v = v + swap(v, mask)
            mask *= 2
    return v


def whole(shape):
    return pl.BlockSpec(shape, lambda *_: (0,) * len(shape))


def assemble_kernel(turned, order, *refs):
    pieces, out = refs[: len(CYCLE)], refs[len(CYCLE)]
    target = refs[len(CYCLE) + 1] if turned else out
    count = pieces[0].shape[0]
    for i, piece in enumerate(pieces):
        target[pl.ds(pl.multiple_of(order[i] * count, count), count), :] = piece[...]
    if turned:
        out[...] = target[...].T


def assemble(pieces, order, turned):
    count, width = pieces[0].shape
    total = count * len(pieces)
    shape = (width, total) if turned else (total, width)
    return pl.pallas_call(
        functools.partial(assemble_kernel, turned),
        grid_spec=pltpu.PrefetchScalarGridSpec(
            num_scalar_prefetch=1,
            grid=(1,),
            in_specs=[whole(pieces[0].shape)] * len(pieces),
            out_specs=whole(shape),
            scratch_shapes=[pltpu.VMEM((total, width), BF)] if turned else [],
        ),
        out_shape=jax.ShapeDtypeStruct(shape, BF),
        name="assemble",
    )(order, *pieces)


def project_kernel(heads, *refs):
    x_refs, (weight, turn, marks, q_out, k_out, v_out) = refs[:-6], refs[-6:]
    x = jnp.concatenate([r[...] for r in x_refs], axis=0)
    mixed = dot(weight[...], x, NT)
    half = HEAD // 2
    cosine, sine = turn[:half, :], turn[half:, :]
    width = heads * HEAD
    key_marks, query_marks = marks[:AUX, :], marks[AUX : 2 * AUX, :]
    ones = marks[2 * AUX :, :]
    for h in range(heads):
        for base, out, scale, tail in (
            (0, q_out, 1.0 / math.sqrt(HEAD), query_marks),
            (width, k_out, None, key_marks),
        ):
            at = base + h * HEAD
            first, second = mixed[at : at + half], mixed[at + half : at + HEAD]
            turned = jnp.concatenate(
                [first * cosine - second * sine, second * cosine + first * sine], axis=0
            )
            if scale is not None:
                turned = turned * scale
            out[h, :HEAD, :] = turned.astype(BF)
            out[h, HEAD:, :] = tail
        at = 2 * width + h * HEAD
        v_out[h, :HEAD, :] = mixed[at : at + HEAD].astype(BF)
        v_out[h, HEAD:, :] = ones


def project(pieces, weight, turn, marks, heads):
    tokens = sum(p.shape[0] for p in pieces)
    shape = jax.ShapeDtypeStruct((heads, HEAD + AUX, tokens), BF)
    args = (*pieces, weight, turn, marks)
    flops = 2 * weight.shape[0] * weight.shape[1] * tokens
    return pl.pallas_call(
        functools.partial(project_kernel, heads),
        grid=(1,),
        in_specs=[whole(a.shape) for a in args],
        out_specs=[whole(shape.shape)] * 3,
        out_shape=[shape] * 3,
        cost_estimate=pl.CostEstimate(flops=flops, bytes_accessed=2**22, transcendentals=0),
        name="project",
    )(*args)


def attend_kernel(heads, tile, q, k, v, top_in, sum_in, acc_in, top, total, acc):
    tokens = q.shape[2]
    for h in range(heads):
        for t in range(0, tokens, tile):
            cols = slice(t, t + tile)
            scores = dot(k[h], q[h, :, cols], TN)
            old = top_in[h : h + 1, cols]
            new = jnp.maximum(old, jnp.max(scores, axis=0, keepdims=True))
            keep = jnp.exp(old - new)
            weights = jnp.exp(scores - new)
            top[h : h + 1, cols] = new
            total[h : h + 1, cols] = sum_in[h : h + 1, cols] * keep + jnp.sum(
                weights, axis=0, keepdims=True
            )
            acc[h, :, cols] = acc_in[h, :, cols] * keep + dot(v[h, :HEAD, :], weights.astype(BF), NN)


def attend(q, k, v, state, heads):
    tokens = q.shape[2]
    args = (q, k, v, *state)
    scores = heads * tokens * k.shape[2]
    return pl.pallas_call(
        functools.partial(attend_kernel, heads, min(256, tokens)),
        grid=(1,),
        in_specs=[whole(a.shape) for a in args],
        out_specs=[whole(s.shape) for s in state],
        out_shape=[jax.ShapeDtypeStruct(s.shape, F32) for s in state],
        cost_estimate=pl.CostEstimate(
            flops=4 * scores * 256, bytes_accessed=2**21, transcendentals=scores
        ),
        name="attend",
    )(*args)


def query_grad_kernel(heads, tile, q, g, k, v, out):
    @pl.when(pl.program_id(0) == 0)
    def _():
        out[...] = jnp.zeros_like(out)

    tokens = q.shape[2]
    for h in range(heads):
        for t in range(0, tokens, tile):
            cols = slice(t, t + tile)
            probs = jnp.exp(dot(k[0, h], q[h, :, cols], TN))
            slope = dot(v[0, h], g[h, :, cols], TN)
            grads = (probs * slope).astype(BF)
            out[h, :, cols] += dot(k[0, h, :HEAD, :], grads, NN)


def query_grad(q, g, keys, values, heads):
    chunks, _, rows, count = keys.shape
    tokens = q.shape[2]
    scores = heads * tokens * count * chunks
    each = pl.BlockSpec((1, heads, rows, count), lambda i: (i, 0, 0, 0))
    return pl.pallas_call(
        functools.partial(query_grad_kernel, heads, min(256, tokens)),
        grid=(chunks,),
        in_specs=[whole(q.shape), whole(g.shape), each, each],
        out_specs=whole((heads, HEAD, tokens)),
        out_shape=jax.ShapeDtypeStruct((heads, HEAD, tokens), F32),
        cost_estimate=pl.CostEstimate(
            flops=6 * scores * 256, bytes_accessed=2**22, transcendentals=scores
        ),
        name="query_grad",
    )(q, g, keys, values)


def key_grad_kernel(heads, tile, q, g, k, v, dk_in, dv_in, dk, dv):
    tokens = k.shape[2]
    for h in range(heads):
        for t in range(0, tokens, tile):
            cols = slice(t, t + tile)
            probs = jnp.exp(dot(q[h], k[h, :, cols], TN))
            slope = dot(g[h], v[h, :, cols], TN)
            grads = (probs * slope).astype(BF)
            dv[h, :, cols] = dv_in[h, :, cols] + dot(g[h, :HEAD, :], probs.astype(BF), NN)
            dk[h, :, cols] = dk_in[h, :, cols] + dot(q[h, :HEAD, :], grads, NN)


def key_grad(q, g, k, v, sums, heads):
    args = (q, g, k, v, *sums)
    scores = heads * q.shape[2] * k.shape[2]
    return pl.pallas_call(
        functools.partial(key_grad_kernel, heads, min(256, k.shape[2])),
        grid=(1,),
        in_specs=[whole(a.shape) for a in args],
        out_specs=[whole(s.shape) for s in sums],
        out_shape=[jax.ShapeDtypeStruct(s.shape, F32) for s in sums],
        cost_estimate=pl.CostEstimate(
            flops=8 * scores * 256, bytes_accessed=2**21, transcendentals=scores
        ),
        name="key_grad",
    )(*args)


def norm_forward(values, gain, bias):
    centered = values - jnp.mean(values, axis=-1, keepdims=True)
    inverse = lax.rsqrt(jnp.mean(centered * centered, axis=-1, keepdims=True) + NORM_EPS)
    normed = centered * inverse
    return (normed * gain + bias, normed, inverse)


def norm_backward(grad_out, normed, inverse, gain):
    scaled = grad_out * gain
    grad_in = inverse * (
        scaled
        - jnp.mean(scaled, axis=-1, keepdims=True)
        - normed * jnp.mean(scaled * normed, axis=-1, keepdims=True)
    )
    return (grad_in, jnp.sum(grad_out * normed, axis=0), jnp.sum(grad_out, axis=0))


def three_parts(v):
    high = lax.reduce_precision(v, 8, 7)
    rest = v - high
    middle = lax.reduce_precision(rest, 8, 7)
    low = lax.reduce_precision(rest - middle, 8, 7)
    return [p.astype(BF) for p in (high, middle, low)]


def slot_tables(seq_lengths, packed_order, chunk_rows, col, local):
    cols = lax.axis_size("col")
    blocks = packed_order.reshape(-1, local)
    wanted = (chunk_rows[:, None] * cols + jnp.stack([col ^ o for o in OFFSETS])[None, :]).reshape(-1)
    index = jnp.arange(blocks.shape[0], dtype=jnp.int32)
    slots = jnp.sum(
        jnp.where(wanted[:, None, None] == index[None, :, None], blocks[None], 0), axis=1
    ).reshape(chunk_rows.shape[0], cols * local)
    ends = jnp.cumsum(seq_lengths)
    starts = ends - seq_lengths
    count = seq_lengths.shape[0]
    seq = sum((slots >= ends[s]).astype(jnp.int32) for s in range(count))
    start = sum(jnp.where(seq == s, starts[s], 0) for s in range(count))
    positions = (slots - start).astype(F32)
    half = HEAD // 2
    freqs = ROPE_BASE ** (-jnp.arange(half, dtype=F32) * 2.0 / HEAD)
    angles = positions[:, None, :] * freqs[None, :, None]
    turn = jnp.concatenate([jnp.cos(angles), jnp.sin(angles)], axis=1)
    member = seq[:, None, :] == jnp.arange(8, dtype=jnp.int32)[None, :, None]
    shape = (slots.shape[0], 3, slots.shape[1])
    ones, zeros = jnp.ones(shape, F32), jnp.zeros(shape, F32)
    blank = jnp.zeros((slots.shape[0], AUX - 14, slots.shape[1]), F32)
    key_marks = jnp.concatenate([jnp.where(member, 1.0, 0.0), ones, zeros, blank], axis=1)
    query_marks = jnp.concatenate([jnp.where(member, 0.0, FAR), zeros, zeros, blank], axis=1)
    plain = jnp.concatenate([jnp.zeros_like(key_marks[:, :11]), ones, blank], axis=1)
    marks = jnp.concatenate([key_marks, query_marks, plain], axis=1).astype(BF)
    return turn, marks


def local(
    tokens,
    w_qkv,
    w_out,
    w_gate_up,
    w_down,
    gain1,
    bias1,
    gain2,
    bias2,
    cotangent,
    seq_lengths,
    packed_order,
):
    rows = lax.axis_size("row")
    row, col = lax.axis_index("row"), lax.axis_index("col")
    ring = rows == len(CYCLE)
    own, features = tokens.shape
    group = own * lax.axis_size("col")
    share = w_qkv.shape[0]
    width = w_qkv.shape[2]
    heads = width // HEAD
    hidden_units = w_gate_up.shape[2]
    place = cycle_place() if ring else None

    early = jnp.concatenate([w_qkv.reshape(share, 3 * width), w_out.T], axis=1)
    late = jnp.concatenate([w_gate_up.reshape(share, 2 * hidden_units), w_down.T], axis=1)

    if ring:
        chunk_rows = jnp.stack([cycle_row(place + s) for s in STEPS])
        early_full = assemble(cycle_gather(early), chunk_rows, True)
    else:
        chunk_rows = jnp.arange(rows, dtype=jnp.int32)
        early_full = lax.all_gather(early, "row", axis=0, tiled=True).T
    w_mix, full_out = early_full[: 3 * width], early_full[3 * width :]

    turn, marks = slot_tables(seq_lengths, packed_order, chunk_rows, col, own)

    side = col_swap(tokens, 2)
    own_pieces = [tokens, side, col_swap(tokens, 1), col_swap(side, 1)]
    token_block = jnp.concatenate(own_pieces, axis=0)

    empty = (
        jnp.full((heads, group), LOWEST, F32),
        jnp.zeros((heads, group), F32),
        jnp.zeros((heads, HEAD, group), F32),
    )
    if ring:
        gathered = cycle_gather(tokens)
        parts = []
        state = empty
        for i, piece in enumerate(gathered):
            if i == 0:
                pieces = own_pieces
            else:
                beside = col_swap(piece, 2)
                pieces = [piece, beside, col_swap(piece, 1), col_swap(beside, 1)]
            q, k, v = project(pieces, w_mix, turn[i], marks[i], heads)
            parts.append((q, k, v))
            state = attend(parts[0][0], k, v, state, heads)
        own_q, own_k, own_v = parts[0]
        all_q, all_k, all_v = (jnp.stack(p) for p in zip(*parts))
    else:
        own_turn = lax.dynamic_index_in_dim(turn, row, 0, keepdims=False)
        own_marks = lax.dynamic_index_in_dim(marks, row, 0, keepdims=False)
        own_q, own_k, own_v = project([token_block], w_mix, own_turn, own_marks, heads)
        blocks = lax.all_gather(token_block, "row", axis=0, tiled=False)

        def step(state, part):
            block, chunk_turn, chunk_marks = part
            q, k, v = project([block], w_mix, chunk_turn, chunk_marks, heads)
            return tuple(attend(own_q, k, v, state, heads)), (q, k, v)

        state, (all_q, all_k, all_v) = lax.scan(step, empty, (blocks, turn, marks))
    top, total, acc = state
    context = acc / total[:, None, :]
    log_total = top + jnp.log(total)
    context_bf = context.astype(BF).reshape(width, group)

    if ring:
        late, _ = lax.optimization_barrier((late, gathered[5]))
        late_full = assemble(cycle_gather(late), chunk_rows, False)
    else:
        late_full = lax.all_gather(late, "row", axis=0, tiled=True)
    w_gu, w_dn = late_full[:, : 2 * hidden_units], late_full[:, 2 * hidden_units :]

    attn_out = col_scatter(dot(context_bf, full_out, TN).astype(BF))
    residual1 = tokens.astype(F32) + attn_out
    hidden1, normed1, inverse1 = norm_forward(residual1, gain1, bias1)
    hidden_block = col_gather(hidden1.astype(BF))
    gate_up = dot(hidden_block, w_gu, NN)
    up, gate = gate_up[:, :hidden_units], gate_up[:, hidden_units:]
    sigma = jax.nn.sigmoid(gate)
    inner = (gate * sigma * up).astype(BF)
    ffn_out = col_scatter(dot(inner, w_dn, NT).astype(BF))
    residual2 = hidden1 + ffn_out
    result, normed2, inverse2 = norm_forward(residual2, gain2, bias2)
    grad_res2, grad_gain2, grad_bias2 = norm_backward(
        cotangent.astype(F32), normed2, inverse2, gain2
    )
    grad_ffn = col_gather(grad_res2.astype(BF))
    grad_inner = dot(grad_ffn, w_dn, NN)
    grad_up = grad_inner * gate * sigma
    grad_gate = grad_inner * up * sigma * (1.0 + gate * (1.0 - sigma))
    grad_gate_up = jnp.concatenate([grad_up, grad_gate], axis=1).astype(BF)
    grad_hidden1 = grad_res2 + col_scatter(dot(grad_gate_up, w_gu, NT).astype(BF))
    grad_dn = row_scatter(dot(grad_ffn, inner, TN).astype(BF), place)
    grad_gu = row_scatter(dot(hidden_block, grad_gate_up, TN).astype(BF), place)
    grad_res1, grad_gain1, grad_bias1 = norm_backward(grad_hidden1, normed1, inverse1, gain1)
    grad_attn = col_gather(grad_res1.astype(BF))
    grad_context = dot(full_out, grad_attn, NT).astype(BF)
    grad_out = row_scatter(dot(grad_attn, context_bf, ((0,), (1,))).astype(BF), place)

    grad_heads = grad_context.reshape(heads, HEAD, group)
    delta = jnp.sum(grad_heads.astype(F32) * context, axis=1)
    terms = jnp.stack(three_parts(-log_total) + three_parts(-delta), axis=1)
    blank8 = jnp.zeros((heads, 8, group), BF)
    blank2 = jnp.zeros((heads, AUX - 14, group), BF)
    package = jnp.concatenate([grad_heads, blank8, terms, blank2], axis=1)

    def with_terms(q, g):
        tail = q[..., HEAD:, :] + jnp.concatenate(
            [jnp.zeros_like(g[..., :8, :]), g[..., HEAD + 8 : HEAD + 11, :], jnp.zeros_like(g[..., : AUX - 11, :])],
            axis=-2,
        )
        return jnp.concatenate([q[..., :HEAD, :], tail], axis=-2)

    grad_query = query_grad(with_terms(own_q, package), package, all_k, all_v, heads)
    sums = (jnp.zeros((heads, HEAD, group), F32),) * 2
    flat = package.reshape(heads * (HEAD + AUX), group)
    if ring:
        for i, g in enumerate(cycle_gather(flat)):
            g = g.reshape(package.shape)
            sums = key_grad(with_terms(parts[i][0], g), g, own_k, own_v, sums, heads)
    else:
        packages = lax.all_gather(flat, "row", axis=0, tiled=False)

        def key_step(sums, part):
            q, g = part
            g = g.reshape(package.shape)
            return tuple(key_grad(with_terms(q, g), g, own_k, own_v, sums, heads)), None

        sums, _ = lax.scan(key_step, sums, (all_q, packages))
    grad_key, grad_value = sums
    own_turn = turn[0] if ring else lax.dynamic_index_in_dim(turn, row, 0, keepdims=False)
    half = HEAD // 2
    cosine, sine = own_turn[None, :half], own_turn[None, half:]

    def turn_back(v):
        first, second = v[:, :half], v[:, half:]
        return jnp.concatenate(
            [first * cosine + second * sine, second * cosine - first * sine], axis=1
        )

    scale = 1.0 / math.sqrt(HEAD)
    grad_mixed = (
        jnp.concatenate([turn_back(grad_query * scale), turn_back(grad_key), grad_value], axis=0)
        .astype(BF)
        .reshape(3 * width, group)
    )
    grad_tokens = grad_res1 + col_scatter(dot(grad_mixed, w_mix, TN).astype(BF))
    grad_mix = row_scatter(dot(token_block, grad_mixed, ((0,), (1,))).astype(BF), place)
    norms = sum_everywhere(jnp.stack([grad_gain1, grad_bias1, grad_gain2, grad_bias2]))
    return (
        result.astype(BF),
        grad_tokens,
        grad_mix.reshape(share, 3, width),
        grad_out.T,
        grad_gu.reshape(share, 2, hidden_units),
        grad_dn.T,
        norms[0],
        norms[1],
        norms[2],
        norms[3],
    )


def solution(mesh):
    placed = (
        P(("row", "col"), None),
        P("row", None, "col"),
        P("col", "row"),
        P("row", None, "col"),
        P("col", "row"),
        P(),
        P(),
        P(),
        P(),
        P(("row", "col"), None),
        P(),
        P(),
    )
    return jax.shard_map(
        local,
        mesh=mesh,
        in_specs=placed,
        out_specs=(
            P(("row", "col"), None),
            P(("row", "col"), None),
            P("row", None, "col"),
            P("col", "row"),
            P("row", None, "col"),
            P("col", "row"),
            P(),
            P(),
            P(),
            P(),
        ),
        check_vma=False,
    )
```

```python
import functools
import math

import jax
import jax.numpy as jnp
from jax import lax
from jax.experimental import pallas as pl
from jax.experimental.pallas import tpu as pltpu
from jax.sharding import PartitionSpec as P

HEAD = 64
ROPE_BASE = 1000.0
NORM_EPS = 1e-12
FAR = -(2.0**100)
LOWEST = -1e30
AUX = 16
BF = jnp.bfloat16
F32 = jnp.float32

CYCLE = (0, 2, 4, 6, 7, 5, 3, 1)
OFFSETS = (0, 2, 1, 3)


def dot(a, b, contract, out=F32):
    return lax.dot_general(a, b, (contract, ((), ())), preferred_element_type=out)


NN = ((1,), (0,))
NT = ((1,), (1,))
TN = ((0,), (0,))


def forward_hop(v):
    n = len(CYCLE)
    return lax.ppermute(v, "row", [(CYCLE[i], CYCLE[(i + 1) % n]) for i in range(n)])


def backward_hop(v):
    n = len(CYCLE)
    return lax.ppermute(v, "row", [(CYCLE[(i + 1) % n], CYCLE[i]) for i in range(n)])


def col_swap(v, mask):
    count = lax.axis_size("col")
    return lax.ppermute(v, "col", [(i, i ^ mask) for i in range(count)])


def cycle_place():
    row = lax.axis_index("row")
    return sum(jnp.where(row == CYCLE[i], i, 0) for i in range(len(CYCLE))).astype(jnp.int32)


def cycle_row(place):
    place = lax.rem(place + 2 * len(CYCLE), len(CYCLE))
    return sum(jnp.where(place == i, CYCLE[i], 0) for i in range(len(CYCLE))).astype(jnp.int32)


def cycle_rounds(block, axis):
    half = block.shape[axis] // 2
    behind, ahead = forward_hop(block), backward_hop(block)
    out = [(behind, ahead)]
    for _ in range(2):
        behind, ahead = forward_hop(behind), backward_hop(ahead)
        out.append((behind, ahead))
    first = forward_hop(lax.slice_in_dim(behind, 0, half, axis=axis))
    second = backward_hop(lax.slice_in_dim(ahead, half, 2 * half, axis=axis))
    return out + [(first, second)]


ROUND_STEPS = (-1, 1, -2, 2, -3, 3, 4, 4)


def cycle_sum(blocks):
    b0, b1, b2, b3, b4a, b4b, b5, b6, b7 = blocks
    half = b4a.shape[0]

    def add(v, block):
        return (v.astype(F32) + block.astype(F32)).astype(BF)

    ahead, back = forward_hop(b4a), backward_hop(b4b)
    ahead = jnp.concatenate([add(ahead, b3[:half]), b3[half:]], axis=0)
    back = jnp.concatenate([b5[:half], add(back, b5[half:])], axis=0)
    for up, down in ((b2, b6), (b1, b7)):
        ahead, back = add(forward_hop(ahead), up), add(backward_hop(back), down)
    ahead, back = forward_hop(ahead), backward_hop(back)
    return b0.astype(F32) + ahead.astype(F32) + back.astype(F32)


def row_sum(blocks):
    if len(blocks) == 1:
        return lax.psum_scatter(blocks[0].astype(F32), "row", scatter_dimension=0, tiled=True)
    return cycle_sum(blocks)


def col_pieces(v):
    side = col_swap(v, 2)
    return [v, side, col_swap(v, 1), col_swap(side, 1)]


def col_exchange(near, far):
    own = near.shape[0] // 2
    other = col_swap(far, 1)
    passed = (near[own:].astype(F32) + other[own:].astype(F32)).astype(BF)
    return near, other, col_swap(passed, 2)


def whole(shape):
    return pl.BlockSpec(shape, lambda *_: (0,) * len(shape))


ANY = pl.BlockSpec(memory_space=pl.ANY)


def call(kernel, name, args, outs, prefetch=(), scratch=(), specs=None, out_specs=None, aliases=None, grid=(1,), flops=0, exps=0):
    args, outs = list(args), list(outs)
    moved = sum(a.size * a.dtype.itemsize for a in args) + sum(
        math.prod(o.shape) * o.dtype.itemsize for o in outs
    )
    return pl.pallas_call(
        kernel,
        grid_spec=pltpu.PrefetchScalarGridSpec(
            num_scalar_prefetch=len(prefetch),
            grid=grid,
            in_specs=specs or [whole(a.shape) for a in args],
            out_specs=out_specs or [whole(o.shape) for o in outs],
            scratch_shapes=list(scratch),
        ),
        out_shape=outs,
        input_output_aliases=aliases or {},
        cost_estimate=pl.CostEstimate(flops=int(flops), bytes_accessed=int(moved), transcendentals=int(exps)),
        name=name,
    )(*prefetch, *args)


def struct(shape, kind):
    return jax.ShapeDtypeStruct(tuple(shape), kind)


def rows_at(start, count):
    return pl.ds(pl.multiple_of(start, 4), count)


def assemble_kernel(split, starts, *refs):
    pieces, (mix, out, held) = refs[:-3], refs[-3:]
    for i, piece in enumerate(pieces):
        held[pl.ds(pl.multiple_of(starts[i], 16), piece.shape[0]), :] = piece[...]
    mix[...] = held[:, :split].T
    out[...] = held[:, split:].T


def assemble(pieces, starts, split):
    width = pieces[0].shape[1]
    total = sum(p.shape[0] for p in pieces)
    return call(
        functools.partial(assemble_kernel, split),
        "assemble",
        pieces,
        [struct((split, total), BF), struct((width - split, total), BF)],
        prefetch=[starts],
        scratch=[pltpu.VMEM((total, width), BF)],
    )


def project_into(pieces, weight, turn, marks, q_out, k_out, v_out, heads):
    half = HEAD // 2
    width = heads * HEAD
    begin = 0
    for piece in pieces:
        count = piece.shape[0]
        lanes = slice(begin, begin + count)
        begin += count
        mixed = dot(weight[...], piece[...], NT)
        cosine, sine = turn[:half, lanes], turn[half:, lanes]
        for h in range(heads):
            for base, out, scale, tail in (
                (0, q_out, 1.0 / math.sqrt(HEAD), AUX),
                (width, k_out, None, 0),
            ):
                at = base + h * HEAD
                first, second = mixed[at : at + half], mixed[at + half : at + HEAD]
                turned = jnp.concatenate(
                    [first * cosine - second * sine, second * cosine + first * sine], axis=0
                )
                if scale is not None:
                    turned = turned * scale
                out[h, :HEAD, lanes] = turned.astype(BF)
                out[h, HEAD:, lanes] = marks[tail : tail + AUX, lanes]
            at = 2 * width + h * HEAD
            v_out[h, :HEAD, lanes] = mixed[at : at + HEAD].astype(BF)
            v_out[h, HEAD:, lanes] = marks[2 * AUX : 3 * AUX, lanes]


def attend_kernel(mode, heads, count, slot, *refs):
    pieces, refs = refs[:count], refs[count:]
    weight, turn, marks = refs[:3]
    refs = refs[3:]
    if mode != "first":
        q_own, top_in, sum_in, acc_in = refs[:4]
        refs = refs[7:]
    if mode == "last":
        w_out, refs = refs[0], refs[1:]
    k, v, q = refs[:3]
    refs = refs[3:]
    project_into(pieces, weight, turn, marks, q, k, v, heads)
    if mode == "first":
        q_own, refs = refs[0], refs[1:]
        q_own[...] = q[...]
    each = range(heads)
    scores = [dot(k[h], q_own[h], TN) for h in each]
    news = [jnp.max(s, axis=0, keepdims=True) for s in scores]
    if mode != "first":
        olds = [top_in[h : h + 1] for h in each]
        news = [jnp.maximum(o, n) for o, n in zip(olds, news)]
        keeps = [jnp.exp(o - n) for o, n in zip(olds, news)]
    weights = [jnp.exp(s - n) for s, n in zip(scores, news)]
    sums = [jnp.sum(w, axis=0, keepdims=True) for w in weights]
    values = [dot(v[h, :HEAD, :], w.astype(BF), NN) for h, w in enumerate(weights)]
    if mode != "first":
        sums = [sum_in[h : h + 1] * keeps[h] + sums[h] for h in each]
        values = [acc_in[h] * keeps[h] + values[h] for h in each]
    if mode != "last":
        top, total, acc = refs
        for h in each:
            top[h : h + 1] = news[h]
            total[h : h + 1] = sums[h]
            acc[h] = values[h]
        return
    near, far, context_bf, context, log_total = refs
    for h in each:
        value = values[h] / sums[h]
        context[h] = value
        context_bf[h * HEAD : (h + 1) * HEAD] = value.astype(BF)
        log_total[h : h + 1] = news[h] + jnp.log(sums[h])
    attn = dot(context_bf[...], w_out[...], TN)
    half = near.shape[0]
    near[...] = attn[:half].astype(BF)
    far[...] = attn[half:].astype(BF)


def attend(mode, pieces, slot, weight, turn, marks, heads, total, group, carried=(), w_out=None):
    width = sum(p.shape[0] for p in pieces)
    rows = HEAD + AUX

    def lanes(*lead):
        return pl.BlockSpec((*lead, width), lambda i, s: (*(0,) * len(lead), s[0]))

    args = [*pieces, weight, turn, marks, *carried]
    specs = [whole(p.shape) for p in pieces]
    specs += [whole(weight.shape), lanes(turn.shape[0]), lanes(marks.shape[0])]
    buffers = [struct((heads, rows, total), BF)] * 3
    outs, out_specs = list(buffers), [lanes(heads, rows)] * 3
    aliases = {}
    if mode != "first":
        specs += [whole(c.shape) for c in carried[:4]] + [ANY] * 3
        base = 1 + len(pieces) + 3 + 4
        aliases = {base: 0, base + 1: 1, base + 2: 2}
    features = weight.shape[1]
    if mode == "last":
        args.append(w_out)
        specs.append(whole(w_out.shape))
        extra = [
            struct((group // 2, features), BF),
            struct((group // 2, features), BF),
            struct((heads * HEAD, group), BF),
            struct((heads, HEAD, group), F32),
            struct((heads, group), F32),
        ]
    else:
        extra = [
            struct((heads, group), F32),
            struct((heads, group), F32),
            struct((heads, HEAD, group), F32),
        ]
        if mode == "first":
            extra = [struct((heads, rows, group), BF)] + extra
    outs += extra
    out_specs += [whole(e.shape) for e in extra]
    scores = heads * width * group
    return call(
        functools.partial(attend_kernel, mode, heads, len(pieces)),
        "attend",
        args,
        outs,
        prefetch=[slot],
        specs=specs,
        out_specs=out_specs,
        aliases=aliases,
        flops=scores * 512,
        exps=scores,
    )


def with_terms(q, g):
    return jnp.concatenate([q[:HEAD], q[HEAD:] + g[HEAD:]], axis=0)


def query_grad_kernel(heads, q, g, k, v, out):
    @pl.when(pl.program_id(0) == 0)
    def _():
        out[...] = jnp.zeros_like(out)

    rows = HEAD + AUX
    each = range(heads)
    terms = [g[h * rows : (h + 1) * rows] for h in each]
    probs = [jnp.exp(dot(k[h], with_terms(q[h], terms[h]), TN)) for h in each]
    grads = [(probs[h] * dot(v[h], terms[h], TN)).astype(BF) for h in each]
    for h in each:
        out[h] += dot(k[h, :HEAD, :], grads[h], NN)


def query_grad(q, g, keys, values, heads, width):
    rows, total = keys.shape[1:]
    group = q.shape[2]
    each = pl.BlockSpec((heads, rows, width), lambda i: (0, 0, i))
    scores = heads * group * total
    return call(
        functools.partial(query_grad_kernel, heads),
        "query_grad",
        [q, g, keys, values],
        [struct((heads, HEAD, group), F32)],
        specs=[whole(q.shape), whole(g.shape), each, each],
        grid=(total // width,),
        flops=scores * 768,
        exps=scores,
    )[0]


def key_grad_kernel(heads, count, carried, slots, *refs):
    pieces, (q, k, v), refs = refs[:count], refs[count : count + 3], refs[count + 3 :]
    rows = HEAD + AUX
    each = range(heads)
    if carried:
        dk_in, dv_in = refs[:2]
        refs = refs[2:]
    dk, dv, norms = refs

    def of(h):
        parts = [p[h * rows : (h + 1) * rows] for p in pieces]
        return parts[0] if count == 1 else jnp.concatenate(parts, axis=1)

    terms = [of(h) for h in each]
    probs = [jnp.exp(dot(with_terms(q[h], terms[h]), k[h], TN)) for h in each]
    grads = [(probs[h] * dot(terms[h], v[h], TN)).astype(BF) for h in each]
    for h in each:
        value = dot(terms[h][:HEAD], probs[h].astype(BF), NN)
        key = dot(q[h, :HEAD, :], grads[h], NN)
        dv[h] = dv_in[h] + value if carried else value
        dk[h] = dk_in[h] + key if carried else key
    for i in range(norms.shape[0]):
        norms[i] = pieces[i][heads * rows : heads * rows + NORM_ROWS, :NORM_LANES].astype(F32)


NORM_LANES = 256


def key_grad(pieces, chunks, slots, q, keys, values, heads, group, sums=()):
    width = sum(p.shape[1] for p in pieces)
    rows = HEAD + AUX
    own = pl.BlockSpec((heads, rows, group), lambda i, s: (0, 0, s[1]))
    specs = [whole(p.shape) for p in pieces]
    specs += [pl.BlockSpec((heads, rows, width), lambda i, s: (0, 0, s[0])), own, own]
    specs += [whole(s.shape) for s in sums]
    scores = heads * group * width
    return call(
        functools.partial(key_grad_kernel, heads, len(pieces), bool(sums)),
        "key_grad",
        [*pieces, q, keys, values, *sums],
        [struct((heads, HEAD, group), F32)] * 2 + [struct((chunks, NORM_ROWS, NORM_LANES), F32)],
        prefetch=[slots],
        specs=specs,
        flops=scores * 1024,
        exps=scores,
    )


def norm_parts(values):
    centered = values - jnp.mean(values, axis=-1, keepdims=True)
    inverse = lax.rsqrt(jnp.mean(centered * centered, axis=-1, keepdims=True) + NORM_EPS)
    return centered * inverse, inverse


def norm_back(grad_out, normed, inverse, gain):
    scaled = grad_out * gain
    grad_in = inverse * (
        scaled
        - jnp.mean(scaled, axis=-1, keepdims=True)
        - normed * jnp.mean(scaled * normed, axis=-1, keepdims=True)
    )
    sums = [jnp.sum(grad_out * normed, axis=0, keepdims=True), jnp.sum(grad_out, axis=0, keepdims=True)]
    return grad_in, sums


def col_total(near, other, last):
    own = last.shape[0]
    return near[:own].astype(F32) + other[:own].astype(F32) + last[...].astype(F32)


def first_norm_kernel(near, other, last, tokens, gain, bias, residual, hidden):
    value = tokens[...].astype(F32) + col_total(near, other, last)
    residual[...] = value
    normed, _ = norm_parts(value)
    hidden[...] = (normed * gain[...] + bias[...]).astype(BF)


def second_norm_kernel(near, other, last, residual, gain1, bias1, gain2, bias2, cotangent, result, grad, grad_bf, sums):
    hidden = norm_parts(residual[...])[0] * gain1[...] + bias1[...]
    normed, inverse = norm_parts(hidden + col_total(near, other, last))
    result[...] = (normed * gain2[...] + bias2[...]).astype(BF)
    value, (dgain, dbias) = norm_back(cotangent[...].astype(F32), normed, inverse, gain2[...])
    grad[...] = value
    grad_bf[...] = value.astype(BF)
    sums[0:1] = dgain
    sums[1:2] = dbias


def first_norm_back_kernel(near, other, last, residual, gain, grad2, sums2, grad, package):
    normed, inverse = norm_parts(residual[...])
    grad_out = grad2[...] + col_total(near, other, last)
    value, (dgain, dbias) = norm_back(grad_out, normed, inverse, gain[...])
    grad[...] = value
    own = value.shape[0]
    package[:own] = value.astype(BF)
    sums = jnp.concatenate([dgain, dbias, sums2[0:1], sums2[1:2]], axis=0)
    high = sums.astype(BF)
    low = (sums - high.astype(F32)).astype(BF)
    blank = jnp.zeros((8, sums.shape[1]), F32)
    package[own:] = jnp.concatenate([high.astype(F32), low.astype(F32), blank], axis=0).astype(BF)


def stacked(refs, rows):
    return jnp.concatenate([r[:rows] for r in refs], axis=0)


def forward_kernel(count, units, starts, *refs):
    pieces, hidden, (gu, dn, gate_up, inner, near, far) = refs[:count], refs[count:-6], refs[-6:]
    for i, piece in enumerate(pieces):
        rows = pl.ds(pl.multiple_of(starts[i], 16), piece.shape[0])
        gu[rows, :] = piece[:, : 2 * units]
        dn[rows, :] = piece[:, 2 * units :]
    pairs = len(hidden) // 2
    for out, part in ((near, hidden[:pairs]), (far, hidden[pairs:])):
        x = stacked(part, part[0].shape[0])
        size = x.shape[0]
        begin = 0 if out is near else size
        both = dot(x, gu[...], NN)
        gate_up[begin : begin + size] = both
        up, gate = both[:, :units], both[:, units:]
        value = (gate * jax.nn.sigmoid(gate) * up).astype(BF)
        inner[begin : begin + size] = value
        out[...] = dot(value, dn[...], NT).astype(BF)


def backward_kernel(units, *refs):
    pieces, (gu, dn, gate_up, grads, near, far) = refs[:-6], refs[-6:]
    pairs = len(pieces) // 2
    for out, part in ((near, pieces[:pairs]), (far, pieces[pairs:])):
        g = stacked(part, part[0].shape[0])
        size = g.shape[0]
        begin = 0 if out is near else size
        grad_inner = dot(g, dn[...], NN)
        up = gate_up[begin : begin + size, :units]
        gate = gate_up[begin : begin + size, units:]
        sigma = jax.nn.sigmoid(gate)
        grads[begin : begin + size, :units] = (grad_inner * gate * sigma).astype(BF)
        grads[begin : begin + size, units:] = (
            grad_inner * up * sigma * (1.0 + gate * (1.0 - sigma))
        ).astype(BF)
        out[...] = dot(grads[begin : begin + size], gu[...], NT).astype(BF)


def write_blocks(held, starts, outs):
    for i, out in enumerate(outs):
        out[...] = held[pl.ds(pl.multiple_of(starts[i], 16), out.shape[0]), :]


def block_structs(features, width, ring):
    if not ring:
        return [struct((features, width), BF)]
    share = features // len(CYCLE)
    sizes = [share] * 4 + [share // 2] * 2 + [share] * 3
    return [struct((n, width), BF) for n in sizes]


def ffn_grad_kernel(units, n_blocks, starts, *refs):
    hidden, g, (grads, inner) = refs[:4], refs[4:8], refs[8:10]
    outs, held = refs[10 : 10 + n_blocks], refs[10 + n_blocks]
    own = hidden[0].shape[0]
    turned = stacked(hidden, own).T
    for t in range(0, 2 * units, units):
        held[:, t : t + units] = dot(turned, grads[:, t : t + units], NN).astype(BF)
    held[:, 2 * units :] = dot(stacked(g, own).T, inner[...], NN).astype(BF)
    write_blocks(held, starts, outs)


def prepare_kernel(heads, own, *refs):
    pieces, (w_out, context, log_total, package) = refs[:4], refs[4:]
    g = stacked(pieces, own)
    rows = HEAD + AUX
    grad = dot(w_out[...], g, NT).astype(BF)
    index = lax.broadcasted_iota(jnp.int32, (AUX, g.shape[0]), 0)
    for h in range(heads):
        part = grad[h * HEAD : (h + 1) * HEAD]
        package[h * rows : h * rows + HEAD] = part
        delta = jnp.sum(part.astype(F32) * context[h], axis=0, keepdims=True)
        tail = jnp.zeros(index.shape, F32)
        for at, value in ((8, -log_total[h : h + 1]), (11, -delta)):
            for j in range(3):
                high = value.astype(BF).astype(F32)
                tail = jnp.where(index == at + j, high, tail)
                value = value - high
        package[h * rows + HEAD : (h + 1) * rows] = tail.astype(BF)

    def sums(piece):
        both = piece[own : own + 16].astype(F32)
        return both[:4] + both[4:8]

    total = (sums(pieces[0]) + sums(pieces[1])) + (sums(pieces[2]) + sums(pieces[3]))
    high = total.astype(BF).astype(F32)
    both = jnp.concatenate([high, total - high], axis=0)
    base = heads * rows
    package[base:, NORM_LANES:] = jnp.zeros((package.shape[0] - base, package.shape[1] - NORM_LANES), BF)
    parts = [both[:, i * NORM_LANES : (i + 1) * NORM_LANES] for i in range(both.shape[1] // NORM_LANES)]
    parts.append(jnp.zeros((package.shape[0] - base - 8 * len(parts), NORM_LANES), F32))
    package[base:, :NORM_LANES] = jnp.concatenate(parts, axis=0).astype(BF)


def turn_back(first, second, cosine, sine):
    return jnp.concatenate([first * cosine + second * sine, second * cosine - first * sine], axis=0)


def early_grad_kernel(heads, own, n_x, n_blocks, slots, starts, *refs):
    x_refs, g_refs, refs = refs[:n_x], refs[n_x : n_x + 4], refs[n_x + 4 :]
    grad_query, turn, context, mixed, *refs = refs
    outs, held = refs[:n_blocks], refs[n_blocks]
    half = HEAD // 2
    scale = 1.0 / math.sqrt(HEAD)
    for h in range(heads):
        value = grad_query[h] * scale
        mixed[h * HEAD : (h + 1) * HEAD] = turn_back(value[:half], value[half:], turn[:half], turn[half:]).astype(BF)
    x = stacked(x_refs, x_refs[0].shape[0])
    width = heads * HEAD
    held[:, :width] = dot(mixed[...], x, NN).T.astype(BF)
    held[:, width:] = dot(context[...], stacked(g_refs, own), NN).T.astype(BF)
    write_blocks(held, starts, outs)


def late_grad_kernel(heads, n_x, n_blocks, slots, starts, *refs):
    x_refs, refs = refs[:n_x], refs[n_x:]
    mixed_q, grad_key, grad_value, turn, weight, near, far, *refs = refs
    outs, held, mixed = refs[:n_blocks], refs[n_blocks], refs[n_blocks + 1]
    half = HEAD // 2
    width = heads * HEAD
    mixed[:width] = mixed_q[...]
    for h in range(heads):
        value = grad_key[h]
        mixed[width + h * HEAD : width + (h + 1) * HEAD] = turn_back(
            value[:half], value[half:], turn[:half], turn[half:]
        ).astype(BF)
        mixed[2 * width + h * HEAD : 2 * width + (h + 1) * HEAD] = grad_value[h].astype(BF)
    back = dot(mixed[...], weight[...], TN)
    size = near.shape[0]
    near[...] = back[:size].astype(BF)
    far[...] = back[size:].astype(BF)
    x = stacked(x_refs, x_refs[0].shape[0])
    held[...] = dot(mixed[width:], x, NN).T.astype(BF)
    write_blocks(held, starts, outs)


NORM_ROWS = 24


def norm_total_kernel(rows, *refs):
    pieces, (out, held) = refs[:-2], refs[-2:]
    at = 0
    for piece in pieces:
        for i in range(piece.shape[0]):
            held[rows[at]] = piece[i]
            at += 1
    total = held[0]
    for r in range(1, at):
        total = total + held[r]
    for i in range(NORM_ROWS // 8):
        part = total[8 * i : 8 * i + 8]
        out[:, i * NORM_LANES : (i + 1) * NORM_LANES] = part[:4] + part[4:]


def slot_tables(seq_lengths, packed_order, chunk_rows, col, local):
    cols = lax.axis_size("col")
    blocks = packed_order.reshape(-1, local)
    wanted = (chunk_rows[:, None] * cols + jnp.stack([col ^ o for o in OFFSETS])[None, :]).reshape(-1)
    index = jnp.arange(blocks.shape[0], dtype=jnp.int32)
    slots = jnp.sum(
        jnp.where(wanted[:, None, None] == index[None, :, None], blocks[None], 0), axis=1
    ).reshape(1, -1)
    count = seq_lengths.shape[0]
    seq = jnp.zeros_like(slots)
    start = jnp.zeros_like(slots)
    end = jnp.int32(0)
    for s in range(count):
        end = end + seq_lengths[s]
        passed = slots >= end
        seq = seq + passed.astype(jnp.int32)
        start = jnp.where(passed, end, start)
    positions = (slots - start).astype(F32)
    half = HEAD // 2
    freqs = ROPE_BASE ** (-jnp.arange(half, dtype=F32) * 2.0 / HEAD)
    angles = positions * freqs[:, None]
    turn = jnp.concatenate([jnp.cos(angles), jnp.sin(angles)], axis=0)
    line = jnp.arange(3 * AUX, dtype=jnp.int32)[:, None]
    member = lax.rem(line, AUX) == seq
    ones = ((line >= 8) & (line < 11)) | ((line >= 2 * AUX + 11) & (line < 2 * AUX + 14))
    marks = jnp.where(ones, 1.0, 0.0)
    marks = jnp.where((line < 8) & member, 1.0, marks)
    marks = jnp.where((line >= AUX) & (line < AUX + 8) & ~member, FAR, marks)
    return turn, marks.astype(BF)


def local(
    tokens,
    w_qkv,
    w_out,
    w_gate_up,
    w_down,
    gain1,
    bias1,
    gain2,
    bias2,
    cotangent,
    seq_lengths,
    packed_order,
):
    rows = lax.axis_size("row")
    row, col = lax.axis_index("row"), lax.axis_index("col")
    ring = rows == len(CYCLE)
    own, features = tokens.shape
    group = own * lax.axis_size("col")
    total = group * rows
    share = w_qkv.shape[0]
    width = w_qkv.shape[2]
    heads = width // HEAD
    units = w_gate_up.shape[2]
    gains = [v.reshape(1, features) for v in (gain1, bias1, gain2, bias2)]

    early = jnp.concatenate([w_qkv.reshape(share, 3 * width), w_out.T], axis=1)
    late = jnp.concatenate([w_gate_up.reshape(share, 2 * units), w_down.T], axis=1)

    pair = jnp.concatenate([tokens, col_swap(tokens, 2)], axis=0)
    x_pieces = [pair, col_swap(pair, 1)]
    if ring:
        place = cycle_place()
        steps = [cycle_row(place + s) for s in ROUND_STEPS]
        half = share // 2
        starts = jnp.stack(
            [row * share] + [r * share for r in steps[:7]] + [steps[7] * share + half]
        )
        ahead = [cycle_row(place + s) * share for s in range(8)]
        block_starts = jnp.stack(ahead[:5] + [ahead[4] + half] + ahead[5:])
        chunk_rows = jnp.stack(steps[:6] + [row, steps[6]])
        rounds = cycle_rounds(early, 0)
        w_mix, full_out = assemble([early] + [p for r in rounds for p in r], starts, 3 * width)
    else:
        starts = block_starts = jnp.zeros((1,), jnp.int32)
        chunk_rows = jnp.arange(rows, dtype=jnp.int32)
        early_full = lax.all_gather(early, "row", axis=0, tiled=True)
        w_mix, full_out = assemble([early_full], starts, 3 * width)

    turn, marks = slot_tables(seq_lengths, packed_order, chunk_rows, col, own)
    fixed = (w_mix, turn, marks, heads, total, group)

    def at(slot):
        return jnp.asarray(slot, jnp.int32).reshape(1)

    own_slot = at(6) if ring else at(row)
    keys, values, queries, own_q, *state = attend("first", x_pieces, own_slot, *fixed)
    if ring:
        rounds = cycle_rounds(pair, 0)
        for i, pieces in enumerate(rounds[:3]):
            pieces = [q for p in pieces for q in (p, col_swap(p, 1))]
            keys, values, queries, *state = attend(
                "middle", pieces, at(i), *fixed, (own_q, *state, keys, values, queries)
            )
        pieces = [*rounds[3], *(col_swap(p, 1) for p in rounds[3])]
        keys, values, queries, *finished = attend(
            "last", pieces, at(7), *fixed, (own_q, *state, keys, values, queries), full_out
        )
    else:
        blocks = lax.all_gather(jnp.concatenate(x_pieces, axis=0), "row", axis=0, tiled=False)

        def block(i):
            slot = lax.rem(row + i, rows)
            return [lax.dynamic_index_in_dim(blocks, slot, 0, keepdims=False)], at(slot)

        def step(i, carried):
            *state, keys, values, queries = carried
            keys, values, queries, *state = attend(
                "middle", *block(i), *fixed, (own_q, *state, keys, values, queries)
            )
            return (*state, keys, values, queries)

        *state, keys, values, queries = lax.fori_loop(1, rows - 1, step, (*state, keys, values, queries))
        keys, values, queries, *finished = attend(
            "last", *block(rows - 1), *fixed, (own_q, *state, keys, values, queries), full_out
        )
    near, far, context_bf, context, log_total = finished

    if ring:
        late, _ = lax.optimization_barrier((late, rounds[1]))
        late_pieces = [late] + [p for r in cycle_rounds(late, 0) for p in r]
    else:
        late_pieces = [lax.all_gather(late, "row", axis=0, tiled=True)]

    part = struct((group // 2, features), BF)
    flat = struct((own, features), F32)
    residual1, hidden = call(
        first_norm_kernel,
        "first_norm",
        [*col_exchange(near, far), tokens, *gains[:2]],
        [flat, struct((own, features), BF)],
    )
    hidden_pieces = col_pieces(hidden)
    w_gu, w_dn, gate_up, inner, near, far = call(
        functools.partial(forward_kernel, len(late_pieces), units),
        "ffn_forward",
        [*late_pieces, *hidden_pieces],
        [
            struct((features, 2 * units), BF),
            struct((features, units), BF),
            struct((group, 2 * units), F32),
            struct((group, units), BF),
            part,
            part,
        ],
        prefetch=[starts],
        flops=6 * group * features * units,
    )
    result, grad_res2, grad_bf, sums2 = call(
        second_norm_kernel,
        "second_norm",
        [*col_exchange(near, far), residual1, *gains, cotangent],
        [struct((own, features), BF), flat, struct((own, features), BF), struct((8, features), F32)],
    )
    grad_pieces = col_pieces(grad_bf)
    grad_gate_up, near, far = call(
        functools.partial(backward_kernel, units),
        "ffn_backward",
        [*grad_pieces, w_gu, w_dn, gate_up],
        [struct((group, 2 * units), BF), part, part],
        flops=6 * group * features * units,
    )
    exchanged = col_exchange(near, far)
    outs = block_structs(features, 3 * units, ring)
    blocks = call(
        functools.partial(ffn_grad_kernel, units, len(outs)),
        "ffn_grad",
        [*hidden_pieces, *grad_pieces, grad_gate_up, inner],
        outs,
        prefetch=[block_starts],
        scratch=[pltpu.VMEM((features, 3 * units), BF)],
        flops=6 * group * features * units,
    )
    ffn_grad = row_sum(blocks)
    grad_res1, package = call(
        first_norm_back_kernel,
        "first_norm_back",
        [*exchanged, residual1, gains[0], grad_res2, sums2],
        [flat, struct((own + 16, features), BF)],
    )
    attn_pieces = col_pieces(package)
    (package,) = call(
        functools.partial(prepare_kernel, heads, own),
        "prepare",
        [*attn_pieces, full_out, context, log_total],
        [struct((heads * (HEAD + AUX) + 32, group), BF)],
        flops=2 * width * features * group,
    )
    grad_query = query_grad(own_q, package, keys, values, heads, min(2 * group, total))
    own_turn = pl.BlockSpec((HEAD, group), lambda i, s, b: (0, s[0]))
    outs = block_structs(features, 2 * width, ring)
    args = [*x_pieces, *attn_pieces, grad_query, turn, context_bf]
    specs = [whole(a.shape) for a in args]
    specs[-2] = own_turn
    mixed_q, *blocks = call(
        functools.partial(early_grad_kernel, heads, own, len(x_pieces), len(outs)),
        "early_grad",
        args,
        [struct((width, group), BF), *outs],
        prefetch=[own_slot, block_starts],
        scratch=[pltpu.VMEM((features, 2 * width), BF)],
        specs=specs,
        flops=4 * width * features * group,
    )
    early_grad = row_sum(blocks)

    def key_step(pieces, chunks, slot, sums):
        slots = jnp.concatenate([at(slot), own_slot])
        *sums, norms = key_grad(pieces, chunks, slots, queries, keys, values, heads, group, tuple(sums))
        return sums, norms

    norm_out = struct((4, features), F32)
    if ring:
        rounds = cycle_rounds(package, 1)
        sums, norms = key_step([package], 1, 6, ())
        norm_pieces = [norms]
        for i, pieces in enumerate(rounds[:3]):
            sums, norms = key_step(pieces, 2, i, sums)
            norm_pieces.append(norms)
        sums, norms = key_step(rounds[3], 1, 7, sums)
        norm_pieces.append(norms)
        (norm_sums,) = call(
            norm_total_kernel,
            "norm_total",
            norm_pieces,
            [norm_out],
            prefetch=[jnp.stack([row] + steps[:7])],
            scratch=[pltpu.VMEM((rows, NORM_ROWS, NORM_LANES), F32)],
        )
    else:
        packages = lax.all_gather(package, "row", axis=0, tiled=False)

        def step(i, carried):
            sums, norms = carried
            piece = lax.dynamic_index_in_dim(packages, i, 0, keepdims=False)
            sums, more = key_step([piece], 1, i, sums)
            return tuple(sums), norms + more

        zeros = jnp.zeros((heads, HEAD, group), F32)
        sums, norms = lax.fori_loop(
            0, rows, step, ((zeros, zeros), jnp.zeros((1, NORM_ROWS, NORM_LANES), F32))
        )
        (norm_sums,) = call(
            norm_total_kernel,
            "norm_total",
            [norms],
            [norm_out],
            prefetch=[jnp.zeros((1,), jnp.int32)],
            scratch=[pltpu.VMEM((1, NORM_ROWS, NORM_LANES), F32)],
        )
    args = [*x_pieces, mixed_q, *sums, turn, w_mix]
    specs = [whole(a.shape) for a in args]
    specs[-2] = own_turn
    near, far, *blocks = call(
        functools.partial(late_grad_kernel, heads, len(x_pieces), len(outs)),
        "late_grad",
        args,
        [part, part, *outs],
        prefetch=[own_slot, block_starts],
        scratch=[pltpu.VMEM((features, 2 * width), BF), pltpu.VMEM((3 * width, group), BF)],
        specs=specs,
        flops=10 * width * features * group,
    )
    late_grad = row_sum(blocks)
    near, other, last = col_exchange(near, far)
    grad_tokens = grad_res1 + (
        near[:own].astype(F32) + other[:own].astype(F32) + last.astype(F32)
    )
    grad_mix = jnp.concatenate([early_grad[:, :width], late_grad], axis=1)
    return (
        result,
        grad_tokens,
        grad_mix.reshape(share, 3, width),
        early_grad[:, width:].T,
        ffn_grad[:, : 2 * units].reshape(share, 2, units),
        ffn_grad[:, 2 * units :].T,
        norm_sums[0],
        norm_sums[1],
        norm_sums[2],
        norm_sums[3],
    )


def solution(mesh):
    placed = (
        P(("row", "col"), None),
        P("row", None, "col"),
        P("col", "row"),
        P("row", None, "col"),
        P("col", "row"),
        P(),
        P(),
        P(),
        P(),
        P(("row", "col"), None),
        P(),
        P(),
    )
    return jax.shard_map(
        local,
        mesh=mesh,
        in_specs=placed,
        out_specs=(
            P(("row", "col"), None),
            P(("row", "col"), None),
            P("row", None, "col"),
            P("col", "row"),
            P("row", None, "col"),
            P("col", "row"),
            P(),
            P(),
            P(),
            P(),
        ),
        check_vma=False,
    )
```

```python
import functools
import math

import jax
import jax.numpy as jnp
from jax import lax
from jax.experimental import pallas as pl
from jax.experimental.pallas import tpu as pltpu
from jax.sharding import PartitionSpec as P

HEAD = 64
ROPE_BASE = 1000.0
NORM_EPS = 1e-12
FAR = -(2.0**100)
LOWEST = -1e30
AUX = 16
BF = jnp.bfloat16
F32 = jnp.float32

CYCLE = (0, 2, 4, 6, 7, 5, 3, 1)
OFFSETS = (0, 2, 1, 3)


def dot(a, b, contract, out=F32):
    return lax.dot_general(a, b, (contract, ((), ())), preferred_element_type=out)


COST = 0.02

NN = ((1,), (0,))
NT = ((1,), (1,))
TN = ((0,), (0,))


def forward_hop(v):
    n = len(CYCLE)
    return lax.ppermute(v, "row", [(CYCLE[i], CYCLE[(i + 1) % n]) for i in range(n)])


def backward_hop(v):
    n = len(CYCLE)
    return lax.ppermute(v, "row", [(CYCLE[(i + 1) % n], CYCLE[i]) for i in range(n)])


def col_swap(v, mask):
    count = lax.axis_size("col")
    return lax.ppermute(v, "col", [(i, i ^ mask) for i in range(count)])


def cycle_place():
    row = lax.axis_index("row")
    return sum(jnp.where(row == CYCLE[i], i, 0) for i in range(len(CYCLE))).astype(jnp.int32)


def cycle_row(place):
    place = lax.rem(place + 2 * len(CYCLE), len(CYCLE))
    return sum(jnp.where(place == i, CYCLE[i], 0) for i in range(len(CYCLE))).astype(jnp.int32)


def after(value, *first):
    return lax.optimization_barrier((value, first))[0]


class Rounds:
    def __init__(self, block, axis):
        self.held, self.axis, self.done = (block, block), axis, []

    def step(self, *first):
        behind, ahead = after(self.held, first) if first else self.held
        if len(self.done) == 3:
            half = behind.shape[self.axis] // 2
            behind = lax.slice_in_dim(behind, 0, half, axis=self.axis)
            ahead = lax.slice_in_dim(ahead, half, 2 * half, axis=self.axis)
        self.held = forward_hop(behind), backward_hop(ahead)
        self.done.append(self.held)
        return self.held

    def pieces(self):
        while len(self.done) < 4:
            self.step()
        return [p for r in self.done for p in r]


ROUND_STEPS = (-1, 1, -2, 2, -3, 3, 4, 4)


class RowSum:
    def __init__(self, blocks):
        self.blocks, self.hops, self.moving = blocks, 0, None
        if len(blocks) > 1:
            self.moving = blocks[4], blocks[5]

    def step(self):
        if len(self.blocks) == 1:
            return ()
        half = self.blocks[4].shape[0]

        def add(v, block):
            return (v.astype(F32) + block.astype(F32)).astype(BF)

        ahead, back = forward_hop(self.moving[0]), backward_hop(self.moving[1])
        up = (self.blocks[3], self.blocks[2], self.blocks[1], None)[self.hops]
        down = (self.blocks[6], self.blocks[7], self.blocks[8], None)[self.hops]
        if self.hops == 0:
            ahead = jnp.concatenate([add(ahead, up[:half]), up[half:]], axis=0)
            back = jnp.concatenate([down[:half], add(back, down[half:])], axis=0)
        elif up is not None:
            ahead, back = add(ahead, up), add(back, down)
        self.hops += 1
        self.moving = ahead, back
        return self.moving

    def result(self):
        if len(self.blocks) == 1:
            return lax.psum_scatter(self.blocks[0].astype(F32), "row", scatter_dimension=0, tiled=True)
        while self.hops < 4:
            self.step()
        ahead, back = self.moving
        return self.blocks[0].astype(F32) + ahead.astype(F32) + back.astype(F32)


def col_pieces(v):
    side = col_swap(v, 2)
    return [v, side, col_swap(v, 1), col_swap(side, 1)]


def col_exchange(near, far):
    own = near.shape[0] // 2
    other = col_swap(far, 1)
    passed = (near[own:].astype(F32) + other[own:].astype(F32)).astype(BF)
    return (near, other, col_swap(passed, 2)), passed


def whole(shape):
    return pl.BlockSpec(shape, lambda *_: (0,) * len(shape))


ANY = pl.BlockSpec(memory_space=pl.ANY)


def call(kernel, name, args, outs, prefetch=(), scratch=(), specs=None, out_specs=None, aliases=None, grid=(1,), flops=0, exps=0):
    args, outs = list(args), list(outs)
    moved = sum(a.size * a.dtype.itemsize for a in args) + sum(
        math.prod(o.shape) * o.dtype.itemsize for o in outs
    )
    return pl.pallas_call(
        kernel,
        grid_spec=pltpu.PrefetchScalarGridSpec(
            num_scalar_prefetch=len(prefetch),
            grid=grid,
            in_specs=specs or [whole(a.shape) for a in args],
            out_specs=out_specs or [whole(o.shape) for o in outs],
            scratch_shapes=list(scratch),
        ),
        out_shape=outs,
        input_output_aliases=aliases or {},
        cost_estimate=pl.CostEstimate(flops=int(flops * COST), bytes_accessed=int(moved * COST), transcendentals=int(exps * COST)),
        name=name,
    )(*prefetch, *args)


def struct(shape, kind):
    return jax.ShapeDtypeStruct(tuple(shape), kind)


def rows_at(start, count):
    return pl.ds(pl.multiple_of(start, 4), count)


def assemble_kernel(split, starts, *refs):
    pieces, (mix, out, held) = refs[:-3], refs[-3:]
    for i, piece in enumerate(pieces):
        held[pl.ds(pl.multiple_of(starts[i], 16), piece.shape[0]), :] = piece[...]
    mix[...] = held[:, :split].T
    out[...] = held[:, split:].T


def assemble(pieces, starts, split):
    width = pieces[0].shape[1]
    total = sum(p.shape[0] for p in pieces)
    return call(
        functools.partial(assemble_kernel, split),
        "assemble",
        pieces,
        [struct((split, total), BF), struct((width - split, total), BF)],
        prefetch=[starts],
        scratch=[pltpu.VMEM((total, width), BF)],
    )


def project_into(pieces, weight, turn, marks, q_out, k_out, v_out, heads):
    half = HEAD // 2
    width = heads * HEAD
    begin = 0
    for piece in pieces:
        count = piece.shape[0]
        lanes = slice(begin, begin + count)
        begin += count
        mixed = dot(weight[...], piece[...], NT)
        cosine, sine = turn[:half, lanes], turn[half:, lanes]
        for h in range(heads):
            for base, out, scale, tail in (
                (0, q_out, 1.0 / math.sqrt(HEAD), AUX),
                (width, k_out, None, 0),
            ):
                at = base + h * HEAD
                first, second = mixed[at : at + half], mixed[at + half : at + HEAD]
                turned = jnp.concatenate(
                    [first * cosine - second * sine, second * cosine + first * sine], axis=0
                )
                if scale is not None:
                    turned = turned * scale
                out[h, :HEAD, lanes] = turned.astype(BF)
                out[h, HEAD:, lanes] = marks[tail : tail + AUX, lanes]
            at = 2 * width + h * HEAD
            v_out[h, :HEAD, lanes] = mixed[at : at + HEAD].astype(BF)
            v_out[h, HEAD:, lanes] = marks[2 * AUX : 3 * AUX, lanes]


def attend_kernel(mode, heads, count, slot, *refs):
    pieces, refs = refs[:count], refs[count:]
    weight, turn, marks = refs[:3]
    refs = refs[3:]
    if mode != "first":
        q_own, top_in, sum_in, acc_in = refs[:4]
        refs = refs[7:]
    if mode == "last":
        w_out, refs = refs[0], refs[1:]
    k, v, q = refs[:3]
    refs = refs[3:]
    project_into(pieces, weight, turn, marks, q, k, v, heads)
    if mode == "first":
        q_own, refs = refs[0], refs[1:]
        q_own[...] = q[...]
    each = range(heads)
    scores = [dot(k[h], q_own[h], TN) for h in each]
    news = [jnp.max(s, axis=0, keepdims=True) for s in scores]
    if mode != "first":
        olds = [top_in[h : h + 1] for h in each]
        news = [jnp.maximum(o, n) for o, n in zip(olds, news)]
        keeps = [jnp.exp(o - n) for o, n in zip(olds, news)]
    weights = [jnp.exp(s - n) for s, n in zip(scores, news)]
    sums = [jnp.sum(w, axis=0, keepdims=True) for w in weights]
    values = [dot(v[h, :HEAD, :], w.astype(BF), NN) for h, w in enumerate(weights)]
    if mode != "first":
        sums = [sum_in[h : h + 1] * keeps[h] + sums[h] for h in each]
        values = [acc_in[h] * keeps[h] + values[h] for h in each]
    if mode != "last":
        top, total, acc = refs
        for h in each:
            top[h : h + 1] = news[h]
            total[h : h + 1] = sums[h]
            acc[h] = values[h]
        return
    near, far, context_bf, context, log_total = refs
    for h in each:
        value = values[h] / sums[h]
        context[h] = value
        context_bf[h * HEAD : (h + 1) * HEAD] = value.astype(BF)
        log_total[h : h + 1] = news[h] + jnp.log(sums[h])
    attn = dot(context_bf[...], w_out[...], TN)
    half = near.shape[0]
    near[...] = attn[:half].astype(BF)
    far[...] = attn[half:].astype(BF)


def attend(mode, pieces, slot, weight, turn, marks, heads, total, group, carried=(), w_out=None):
    width = sum(p.shape[0] for p in pieces)
    rows = HEAD + AUX

    def lanes(*lead):
        return pl.BlockSpec((*lead, width), lambda i, s: (*(0,) * len(lead), s[0]))

    args = [*pieces, weight, turn, marks, *carried]
    specs = [whole(p.shape) for p in pieces]
    specs += [whole(weight.shape), lanes(turn.shape[0]), lanes(marks.shape[0])]
    buffers = [struct((heads, rows, total), BF)] * 3
    outs, out_specs = list(buffers), [lanes(heads, rows)] * 3
    aliases = {}
    if mode != "first":
        specs += [whole(c.shape) for c in carried[:4]] + [ANY] * 3
        base = 1 + len(pieces) + 3 + 4
        aliases = {base: 0, base + 1: 1, base + 2: 2}
    features = weight.shape[1]
    if mode == "last":
        args.append(w_out)
        specs.append(whole(w_out.shape))
        extra = [
            struct((group // 2, features), BF),
            struct((group // 2, features), BF),
            struct((heads * HEAD, group), BF),
            struct((heads, HEAD, group), F32),
            struct((heads, group), F32),
        ]
    else:
        extra = [
            struct((heads, group), F32),
            struct((heads, group), F32),
            struct((heads, HEAD, group), F32),
        ]
        if mode == "first":
            extra = [struct((heads, rows, group), BF)] + extra
    outs += extra
    out_specs += [whole(e.shape) for e in extra]
    scores = heads * width * group
    return call(
        functools.partial(attend_kernel, mode, heads, len(pieces)),
        "attend",
        args,
        outs,
        prefetch=[slot],
        specs=specs,
        out_specs=out_specs,
        aliases=aliases,
        flops=scores * 512,
        exps=scores,
    )


def with_terms(q, g):
    return jnp.concatenate([q[:HEAD], q[HEAD:] + g[HEAD:]], axis=0)


def query_grad_kernel(heads, q, g, k, v, out_in, out):
    @pl.when(pl.program_id(0) == 0)
    def _():
        out[...] = out_in[...]

    rows = HEAD + AUX
    each = range(heads)
    terms = [g[h * rows : (h + 1) * rows] for h in each]
    probs = [jnp.exp(dot(k[h], with_terms(q[h], terms[h]), TN)) for h in each]
    grads = [(probs[h] * dot(v[h], terms[h], TN)).astype(BF) for h in each]
    for h in each:
        out[h] += dot(k[h, :HEAD, :], grads[h], NN)


def query_grad(q, g, keys, values, heads, width, begin, steps, carried):
    rows = keys.shape[1]
    group = q.shape[2]
    each = pl.BlockSpec((heads, rows, width), lambda i: (0, 0, i + begin))
    scores = heads * group * steps * width
    return call(
        functools.partial(query_grad_kernel, heads),
        "query_grad",
        [q, g, keys, values, carried],
        [struct((heads, HEAD, group), F32)],
        specs=[whole(q.shape), whole(g.shape), each, each, whole(carried.shape)],
        grid=(steps,),
        flops=scores * 768,
        exps=scores,
    )[0]


def key_grad_kernel(heads, count, carried, slots, *refs):
    pieces, (q, k, v), refs = refs[:count], refs[count : count + 3], refs[count + 3 :]
    rows = HEAD + AUX
    each = range(heads)
    if carried:
        dk_in, dv_in = refs[:2]
        refs = refs[2:]
    dk, dv, norms = refs

    def of(h):
        parts = [p[h * rows : (h + 1) * rows] for p in pieces]
        return parts[0] if count == 1 else jnp.concatenate(parts, axis=1)

    terms = [of(h) for h in each]
    probs = [jnp.exp(dot(with_terms(q[h], terms[h]), k[h], TN)) for h in each]
    grads = [(probs[h] * dot(terms[h], v[h], TN)).astype(BF) for h in each]
    for h in each:
        value = dot(terms[h][:HEAD], probs[h].astype(BF), NN)
        key = dot(q[h, :HEAD, :], grads[h], NN)
        dv[h] = dv_in[h] + value if carried else value
        dk[h] = dk_in[h] + key if carried else key
    for i in range(norms.shape[0]):
        norms[i] = pieces[i][heads * rows : heads * rows + NORM_ROWS, :NORM_LANES].astype(F32)


NORM_LANES = 256


def key_grad(pieces, chunks, slots, q, keys, values, heads, group, sums=()):
    width = sum(p.shape[1] for p in pieces)
    rows = HEAD + AUX
    own = pl.BlockSpec((heads, rows, group), lambda i, s: (0, 0, s[1]))
    specs = [whole(p.shape) for p in pieces]
    specs += [pl.BlockSpec((heads, rows, width), lambda i, s: (0, 0, s[0])), own, own]
    specs += [whole(s.shape) for s in sums]
    scores = heads * group * width
    return call(
        functools.partial(key_grad_kernel, heads, len(pieces), bool(sums)),
        "key_grad",
        [*pieces, q, keys, values, *sums],
        [struct((heads, HEAD, group), F32)] * 2 + [struct((chunks, NORM_ROWS, NORM_LANES), F32)],
        prefetch=[slots],
        specs=specs,
        flops=scores * 1024,
        exps=scores,
    )


def norm_parts(values):
    centered = values - jnp.mean(values, axis=-1, keepdims=True)
    inverse = lax.rsqrt(jnp.mean(centered * centered, axis=-1, keepdims=True) + NORM_EPS)
    return centered * inverse, inverse


def norm_back(grad_out, normed, inverse, gain):
    scaled = grad_out * gain
    grad_in = inverse * (
        scaled
        - jnp.mean(scaled, axis=-1, keepdims=True)
        - normed * jnp.mean(scaled * normed, axis=-1, keepdims=True)
    )
    sums = [jnp.sum(grad_out * normed, axis=0, keepdims=True), jnp.sum(grad_out, axis=0, keepdims=True)]
    return grad_in, sums


def col_total(near, other, last):
    own = last.shape[0]
    return near[:own].astype(F32) + other[:own].astype(F32) + last[...].astype(F32)


def first_norm_kernel(near, other, last, tokens, gain, bias, residual, hidden):
    value = tokens[...].astype(F32) + col_total(near, other, last)
    residual[...] = value
    normed, _ = norm_parts(value)
    hidden[...] = (normed * gain[...] + bias[...]).astype(BF)


def second_norm_kernel(near, other, last, residual, gain1, bias1, gain2, bias2, cotangent, result, grad, grad_bf, sums):
    hidden = norm_parts(residual[...])[0] * gain1[...] + bias1[...]
    normed, inverse = norm_parts(hidden + col_total(near, other, last))
    result[...] = (normed * gain2[...] + bias2[...]).astype(BF)
    value, (dgain, dbias) = norm_back(cotangent[...].astype(F32), normed, inverse, gain2[...])
    grad[...] = value
    grad_bf[...] = value.astype(BF)
    sums[0:1] = dgain
    sums[1:2] = dbias


def first_norm_back_kernel(near, other, last, residual, gain, grad2, sums2, grad, package):
    normed, inverse = norm_parts(residual[...])
    grad_out = grad2[...] + col_total(near, other, last)
    value, (dgain, dbias) = norm_back(grad_out, normed, inverse, gain[...])
    grad[...] = value
    own = value.shape[0]
    package[:own] = value.astype(BF)
    sums = jnp.concatenate([dgain, dbias, sums2[0:1], sums2[1:2]], axis=0)
    high = sums.astype(BF)
    low = (sums - high.astype(F32)).astype(BF)
    blank = jnp.zeros((8, sums.shape[1]), F32)
    package[own:] = jnp.concatenate([high.astype(F32), low.astype(F32), blank], axis=0).astype(BF)


def stacked(refs, rows):
    return jnp.concatenate([r[:rows] for r in refs], axis=0)


def forward_kernel(count, units, starts, *refs):
    pieces, hidden, (gu, dn, gate_up, inner, near, far) = refs[:count], refs[count:-6], refs[-6:]
    for i, piece in enumerate(pieces):
        rows = pl.ds(pl.multiple_of(starts[i], 16), piece.shape[0])
        gu[rows, :] = piece[:, : 2 * units]
        dn[rows, :] = piece[:, 2 * units :]
    pairs = len(hidden) // 2
    for out, part in ((near, hidden[:pairs]), (far, hidden[pairs:])):
        x = stacked(part, part[0].shape[0])
        size = x.shape[0]
        begin = 0 if out is near else size
        both = dot(x, gu[...], NN)
        gate_up[begin : begin + size] = both
        up, gate = both[:, :units], both[:, units:]
        value = (gate * jax.nn.sigmoid(gate) * up).astype(BF)
        inner[begin : begin + size] = value
        out[...] = dot(value, dn[...], NT).astype(BF)


def backward_kernel(units, *refs):
    pieces, (gu, dn, gate_up, grads, near, far) = refs[:-6], refs[-6:]
    pairs = len(pieces) // 2
    for out, part in ((near, pieces[:pairs]), (far, pieces[pairs:])):
        g = stacked(part, part[0].shape[0])
        size = g.shape[0]
        begin = 0 if out is near else size
        grad_inner = dot(g, dn[...], NN)
        up = gate_up[begin : begin + size, :units]
        gate = gate_up[begin : begin + size, units:]
        sigma = jax.nn.sigmoid(gate)
        grads[begin : begin + size, :units] = (grad_inner * gate * sigma).astype(BF)
        grads[begin : begin + size, units:] = (
            grad_inner * up * sigma * (1.0 + gate * (1.0 - sigma))
        ).astype(BF)
        out[...] = dot(grads[begin : begin + size], gu[...], NT).astype(BF)


def write_blocks(held, starts, outs):
    for i, out in enumerate(outs):
        out[...] = held[pl.ds(pl.multiple_of(starts[i], 16), out.shape[0]), :]


def block_structs(features, width, ring):
    if not ring:
        return [struct((features, width), BF)]
    share = features // len(CYCLE)
    sizes = [share] * 4 + [share // 2] * 2 + [share] * 3
    return [struct((n, width), BF) for n in sizes]


def ffn_grad_kernel(units, n_blocks, starts, *refs):
    hidden, g, (grads, inner) = refs[:4], refs[4:8], refs[8:10]
    outs, held = refs[10 : 10 + n_blocks], refs[10 + n_blocks]
    own = hidden[0].shape[0]
    turned = stacked(hidden, own).T
    for t in range(0, 2 * units, units):
        held[:, t : t + units] = dot(turned, grads[:, t : t + units], NN).astype(BF)
    held[:, 2 * units :] = dot(stacked(g, own).T, inner[...], NN).astype(BF)
    write_blocks(held, starts, outs)


def prepare_kernel(heads, own, *refs):
    pieces, (w_out, context, log_total, package) = refs[:4], refs[4:]
    g = stacked(pieces, own)
    rows = HEAD + AUX
    grad = dot(w_out[...], g, NT).astype(BF)
    index = lax.broadcasted_iota(jnp.int32, (AUX, g.shape[0]), 0)
    for h in range(heads):
        part = grad[h * HEAD : (h + 1) * HEAD]
        package[h * rows : h * rows + HEAD] = part
        delta = jnp.sum(part.astype(F32) * context[h], axis=0, keepdims=True)
        tail = jnp.zeros(index.shape, F32)
        for at, value in ((8, -log_total[h : h + 1]), (11, -delta)):
            for j in range(3):
                high = value.astype(BF).astype(F32)
                tail = jnp.where(index == at + j, high, tail)
                value = value - high
        package[h * rows + HEAD : (h + 1) * rows] = tail.astype(BF)

    def sums(piece):
        both = piece[own : own + 16].astype(F32)
        return both[:4] + both[4:8]

    total = (sums(pieces[0]) + sums(pieces[1])) + (sums(pieces[2]) + sums(pieces[3]))
    high = total.astype(BF).astype(F32)
    both = jnp.concatenate([high, total - high], axis=0)
    base = heads * rows
    package[base:, NORM_LANES:] = jnp.zeros((package.shape[0] - base, package.shape[1] - NORM_LANES), BF)
    parts = [both[:, i * NORM_LANES : (i + 1) * NORM_LANES] for i in range(both.shape[1] // NORM_LANES)]
    parts.append(jnp.zeros((package.shape[0] - base - 8 * len(parts), NORM_LANES), F32))
    package[base:, :NORM_LANES] = jnp.concatenate(parts, axis=0).astype(BF)


def turn_back(first, second, cosine, sine):
    return jnp.concatenate([first * cosine + second * sine, second * cosine - first * sine], axis=0)


def early_grad_kernel(heads, own, n_x, slots, *refs):
    x_refs, g_refs, refs = refs[:n_x], refs[n_x : n_x + 4], refs[n_x + 4 :]
    grad_query, turn, context, mixed, held = refs
    half = HEAD // 2
    scale = 1.0 / math.sqrt(HEAD)
    for h in range(heads):
        value = grad_query[h] * scale
        mixed[h * HEAD : (h + 1) * HEAD] = turn_back(value[:half], value[half:], turn[:half], turn[half:]).astype(BF)
    x = stacked(x_refs, x_refs[0].shape[0])
    width = heads * HEAD
    held[:, :width] = dot(mixed[...], x, NN).T.astype(BF)
    held[:, width:] = dot(context[...], stacked(g_refs, own), NN).T.astype(BF)


def late_grad_kernel(heads, n_x, n_blocks, slots, starts, *refs):
    x_refs, refs = refs[:n_x], refs[n_x:]
    mixed_q, grad_key, grad_value, early, turn, weight, near, far, *refs = refs
    outs, held, mixed = refs[:n_blocks], refs[n_blocks], refs[n_blocks + 1]
    half = HEAD // 2
    width = heads * HEAD
    mixed[:width] = mixed_q[...]
    for h in range(heads):
        value = grad_key[h]
        mixed[width + h * HEAD : width + (h + 1) * HEAD] = turn_back(
            value[:half], value[half:], turn[:half], turn[half:]
        ).astype(BF)
        mixed[2 * width + h * HEAD : 2 * width + (h + 1) * HEAD] = grad_value[h].astype(BF)
    back = dot(mixed[...], weight[...], TN)
    size = near.shape[0]
    near[...] = back[:size].astype(BF)
    far[...] = back[size:].astype(BF)
    x = stacked(x_refs, x_refs[0].shape[0])
    held[:, : 2 * width] = early[...]
    held[:, 2 * width :] = dot(mixed[width:], x, NN).T.astype(BF)
    write_blocks(held, starts, outs)


NORM_ROWS = 24


def norm_total_kernel(rows, *refs):
    pieces, (out, held) = refs[:-2], refs[-2:]
    at = 0
    for piece in pieces:
        for i in range(piece.shape[0]):
            held[rows[at]] = piece[i]
            at += 1
    total = held[0]
    for r in range(1, at):
        total = total + held[r]
    for i in range(NORM_ROWS // 8):
        part = total[8 * i : 8 * i + 8]
        out[:, i * NORM_LANES : (i + 1) * NORM_LANES] = part[:4] + part[4:]


def slot_tables(seq_lengths, packed_order, chunk_rows, col, local, waits):
    cols = lax.axis_size("col")
    blocks = packed_order.reshape(-1, local)
    wanted = (chunk_rows[:, None] * cols + jnp.stack([col ^ o for o in OFFSETS])[None, :]).reshape(-1)
    index = jnp.arange(blocks.shape[0], dtype=jnp.int32)
    slots = jnp.sum(
        jnp.where(wanted[:, None, None] == index[None, :, None], blocks[None], 0), axis=1
    ).reshape(1, -1)
    count = seq_lengths.shape[0]
    seq = jnp.zeros_like(slots)
    start = jnp.zeros_like(slots)
    end = jnp.int32(0)
    for s in range(count):
        end = end + seq_lengths[s]
        passed = slots >= end
        seq = seq + passed.astype(jnp.int32)
        start = jnp.where(passed, end, start)
    positions = after((slots - start).astype(F32), waits[0])
    half = HEAD // 2
    freqs = ROPE_BASE ** (-jnp.arange(half, dtype=F32) * 2.0 / HEAD)
    angles = positions * freqs[:, None]
    turn = jnp.concatenate([jnp.cos(angles), jnp.sin(angles)], axis=0)
    line = jnp.arange(3 * AUX, dtype=jnp.int32)[:, None]
    member = lax.rem(line, AUX) == after(seq, waits[1])
    ones = ((line >= 8) & (line < 11)) | ((line >= 2 * AUX + 11) & (line < 2 * AUX + 14))
    marks = jnp.where(ones, 1.0, 0.0)
    marks = jnp.where((line < 8) & member, 1.0, marks)
    marks = jnp.where((line >= AUX) & (line < AUX + 8) & ~member, FAR, marks)
    return turn, marks.astype(BF)


def local(
    tokens,
    w_qkv,
    w_out,
    w_gate_up,
    w_down,
    gain1,
    bias1,
    gain2,
    bias2,
    cotangent,
    seq_lengths,
    packed_order,
):
    rows = lax.axis_size("row")
    row, col = lax.axis_index("row"), lax.axis_index("col")
    ring = rows == len(CYCLE)
    own, features = tokens.shape
    group = own * lax.axis_size("col")
    total = group * rows
    share = w_qkv.shape[0]
    width = w_qkv.shape[2]
    heads = width // HEAD
    units = w_gate_up.shape[2]
    gains = [v.reshape(1, features) for v in (gain1, bias1, gain2, bias2)]

    early = jnp.concatenate([w_qkv.reshape(share, 3 * width), w_out.T], axis=1)
    late = jnp.concatenate([w_gate_up.reshape(share, 2 * units), w_down.T], axis=1)

    pair = jnp.concatenate([tokens, col_swap(tokens, 2)], axis=0)
    x_pieces = [pair, col_swap(pair, 1)]
    if ring:
        place = cycle_place()
        steps = [cycle_row(place + s) for s in ROUND_STEPS]
        half = share // 2
        starts = jnp.stack(
            [row * share] + [r * share for r in steps[:7]] + [steps[7] * share + half]
        )
        ahead = [cycle_row(place + s) * share for s in range(8)]
        block_starts = jnp.stack(ahead[:5] + [ahead[4] + half] + ahead[5:])
        chunk_rows = jnp.stack(steps[:6] + [row, steps[6]])
        early_ring, pair_ring = Rounds(early, 0), Rounds(pair, 0)
        waits = [early_ring.step()]
        pair_ring.step(waits[0])
        waits.append(early_ring.step())
    else:
        starts = block_starts = jnp.zeros((1,), jnp.int32)
        chunk_rows = jnp.arange(rows, dtype=jnp.int32)
        waits = (), ()
        early_full = lax.all_gather(early, "row", axis=0, tiled=True)
        w_mix, full_out = assemble([early_full], starts, 3 * width)

    turn, marks = slot_tables(seq_lengths, packed_order, chunk_rows, col, own, waits)
    if ring:
        early_ring.step(turn)
        pair_ring.step(early_ring.step(marks))
        w_mix, full_out = assemble(
            after([early, *early_ring.pieces()], pair_ring.done[0]), starts, 3 * width
        )
    fixed = (w_mix, turn, marks, heads, total, group)

    def at(slot):
        return jnp.asarray(slot, jnp.int32).reshape(1)

    own_slot = at(6) if ring else at(row)
    keys, values, queries, own_q, *state = attend("first", x_pieces, own_slot, *fixed)
    if ring:
        late_ring = Rounds(late, 0)

        def chunks(held):
            return [p for h in held for p in (h, col_swap(h, 1))]

        def middle(i, pieces):
            return attend("middle", pieces, at(i), *fixed, (own_q, *state, keys, values, queries))

        first, second = pair_ring.done
        first = chunks(after(first, w_mix))
        pair_ring.step(state[0])
        second = chunks(after(second, state[0]))
        keys, values, queries, *state = middle(0, after(first, pair_ring.done[1]))
        keys, values, queries, *state = middle(1, second)
        third = chunks(after(pair_ring.done[2], state[0]))
        pair_ring.step(state[0])
        late_ring.step(pair_ring.done[2], state[0])
        keys, values, queries, *state = middle(2, third)
        far = after(pair_ring.done[3], state[0])
        pieces = [*far, *(col_swap(p, 1) for p in far)]
        keys, values, queries, *finished = attend(
            "last", pieces, at(7), *fixed, (own_q, *state, keys, values, queries), full_out
        )
    else:
        blocks = lax.all_gather(jnp.concatenate(x_pieces, axis=0), "row", axis=0, tiled=False)

        def block(i):
            slot = lax.rem(row + i, rows)
            return [lax.dynamic_index_in_dim(blocks, slot, 0, keepdims=False)], at(slot)

        def step(i, carried):
            *state, keys, values, queries = carried
            keys, values, queries, *state = attend(
                "middle", *block(i), *fixed, (own_q, *state, keys, values, queries)
            )
            return (*state, keys, values, queries)

        *state, keys, values, queries = lax.fori_loop(1, rows - 1, step, (*state, keys, values, queries))
        keys, values, queries, *finished = attend(
            "last", *block(rows - 1), *fixed, (own_q, *state, keys, values, queries), full_out
        )
    near, far, context_bf, context, log_total = finished

    if ring:
        near = after(near, late_ring.done[0])
        late_ring.step(context_bf)
    else:
        late_pieces = [lax.all_gather(late, "row", axis=0, tiled=True)]

    part = struct((group // 2, features), BF)
    flat = struct((own, features), F32)
    residual1, hidden = call(
        first_norm_kernel,
        "first_norm",
        [*col_exchange(near, far)[0], tokens, *gains[:2]],
        [flat, struct((own, features), BF)],
    )
    if ring:
        late_ring.step(hidden)
        late_pieces = [late, *late_ring.pieces()]
    hidden_pieces = col_pieces(hidden)
    w_gu, w_dn, gate_up, inner, near, far = call(
        functools.partial(forward_kernel, len(late_pieces), units),
        "ffn_forward",
        [*late_pieces, *hidden_pieces],
        [
            struct((features, 2 * units), BF),
            struct((features, units), BF),
            struct((group, 2 * units), F32),
            struct((group, units), BF),
            part,
            part,
        ],
        prefetch=[starts],
        flops=6 * group * features * units,
    )
    result, grad_res2, grad_bf, sums2 = call(
        second_norm_kernel,
        "second_norm",
        [*col_exchange(near, far)[0], residual1, *gains, cotangent],
        [struct((own, features), BF), flat, struct((own, features), BF), struct((8, features), F32)],
    )
    grad_pieces = col_pieces(grad_bf)
    grad_gate_up, near, far = call(
        functools.partial(backward_kernel, units),
        "ffn_backward",
        [*grad_pieces, w_gu, w_dn, gate_up],
        [struct((group, 2 * units), BF), part, part],
        flops=6 * group * features * units,
    )
    exchanged, passed = col_exchange(near, far)
    grad_gate_up = after(grad_gate_up, passed)
    outs = block_structs(features, 3 * units, ring)
    blocks = call(
        functools.partial(ffn_grad_kernel, units, len(outs)),
        "ffn_grad",
        [*hidden_pieces, *grad_pieces, grad_gate_up, inner],
        outs,
        prefetch=[block_starts],
        scratch=[pltpu.VMEM((features, 3 * units), BF)],
        flops=6 * group * features * units,
    )
    residual1 = after(residual1, blocks)
    ffn_sum = RowSum(after(blocks, exchanged))
    sent = ffn_sum.step()
    grad_res1, package = call(
        first_norm_back_kernel,
        "first_norm_back",
        [*exchanged, residual1, gains[0], grad_res2, sums2],
        [flat, struct((own + 16, features), BF)],
    )
    attn_pieces = col_pieces(package)
    (package,) = call(
        functools.partial(prepare_kernel, heads, own),
        "prepare",
        [*attn_pieces, full_out, context, log_total],
        [struct((heads * (HEAD + AUX) + 32, group), BF)],
        flops=2 * width * features * group,
    )
    span = min(2 * group, total)
    steps_all = total // span
    grad_query = jnp.zeros((heads, HEAD, group), F32)
    if ring:
        package_ring = Rounds(package, 1)
        package_ring.step()
        grad_query = after(grad_query, sent)
        ffn_sum.step()
    grad_query = query_grad(own_q, package, keys, values, heads, span, 0, steps_all, grad_query)
    own_turn = pl.BlockSpec((HEAD, group), lambda i, s, *_: (0, s[0]))
    args = [*x_pieces, *attn_pieces, grad_query, turn, context_bf]
    specs = [whole(a.shape) for a in args]
    specs[-2] = own_turn
    mixed_q, early_grad = call(
        functools.partial(early_grad_kernel, heads, own, len(x_pieces)),
        "early_grad",
        args,
        [struct((width, group), BF), struct((features, 2 * width), BF)],
        prefetch=[own_slot],
        specs=specs,
        flops=4 * width * features * group,
    )

    def key_step(pieces, chunks, slot, sums):
        slots = jnp.concatenate([at(slot), own_slot])
        *sums, norms = key_grad(pieces, chunks, slots, queries, keys, values, heads, group, tuple(sums))
        return sums, norms

    norm_out = struct((4, features), F32)
    if ring:
        package_ring.step(early_grad)
        sums, norms = key_step([after(package, early_grad, package_ring.done[0])], 1, 6, ())
        norm_pieces = [norms]
        for i in range(3):
            sums, norms = key_step(package_ring.done[i], 2, i, sums)
            norm_pieces.append(norms)
            if i < 2:
                package_ring.step(norms)
        ffn_sum.moving = after(ffn_sum.moving, norms)
        sums, norms = key_step(package_ring.done[3], 1, 7, sums)
        norm_pieces.append(norms)
        (norm_sums,) = call(
            norm_total_kernel,
            "norm_total",
            norm_pieces,
            [norm_out],
            prefetch=[jnp.stack([row] + steps[:7])],
            scratch=[pltpu.VMEM((rows, NORM_ROWS, NORM_LANES), F32)],
        )
    else:
        packages = lax.all_gather(package, "row", axis=0, tiled=False)

        def step(i, carried):
            sums, norms = carried
            piece = lax.dynamic_index_in_dim(packages, i, 0, keepdims=False)
            sums, more = key_step([piece], 1, i, sums)
            return tuple(sums), norms + more

        zeros = jnp.zeros((heads, HEAD, group), F32)
        sums, norms = lax.fori_loop(
            0, rows, step, ((zeros, zeros), jnp.zeros((1, NORM_ROWS, NORM_LANES), F32))
        )
        (norm_sums,) = call(
            norm_total_kernel,
            "norm_total",
            [norms],
            [norm_out],
            prefetch=[jnp.zeros((1,), jnp.int32)],
            scratch=[pltpu.VMEM((1, NORM_ROWS, NORM_LANES), F32)],
        )
    args = [*x_pieces, mixed_q, *sums, early_grad, turn, w_mix]
    specs = [whole(a.shape) for a in args]
    specs[-2] = own_turn
    outs = block_structs(features, 4 * width, ring)
    near, far, *blocks = call(
        functools.partial(late_grad_kernel, heads, len(x_pieces), len(outs)),
        "late_grad",
        args,
        [part, part, *outs],
        prefetch=[own_slot, block_starts],
        scratch=[pltpu.VMEM((features, 4 * width), BF), pltpu.VMEM((3 * width, group), BF)],
        specs=specs,
        flops=10 * width * features * group,
    )
    late_grad = RowSum(blocks).result()
    near, other, last = col_exchange(near, far)[0]
    ffn_grad = ffn_sum.result()
    grad_tokens = grad_res1 + (
        near[:own].astype(F32) + other[:own].astype(F32) + last.astype(F32)
    )
    grad_mix = jnp.concatenate([late_grad[:, :width], late_grad[:, 2 * width :]], axis=1)
    return (
        result,
        grad_tokens,
        grad_mix.reshape(share, 3, width),
        late_grad[:, width : 2 * width].T,
        ffn_grad[:, : 2 * units].reshape(share, 2, units),
        ffn_grad[:, 2 * units :].T,
        norm_sums[0],
        norm_sums[1],
        norm_sums[2],
        norm_sums[3],
    )


def solution(mesh):
    placed = (
        P(("row", "col"), None),
        P("row", None, "col"),
        P("col", "row"),
        P("row", None, "col"),
        P("col", "row"),
        P(),
        P(),
        P(),
        P(),
        P(("row", "col"), None),
        P(),
        P(),
    )
    return jax.shard_map(
        local,
        mesh=mesh,
        in_specs=placed,
        out_specs=(
            P(("row", "col"), None),
            P(("row", "col"), None),
            P("row", None, "col"),
            P("col", "row"),
            P("row", None, "col"),
            P("col", "row"),
            P(),
            P(),
            P(),
            P(),
        ),
        check_vma=False,
    )
```

```python
import functools
import math

import jax
import jax.numpy as jnp
from jax import lax
from jax.experimental import pallas as pl
from jax.experimental.pallas import tpu as pltpu
from jax.sharding import PartitionSpec as P

HEAD = 64
ROPE_BASE = 1000.0
NORM_EPS = 1e-12
FAR = -(2.0**100)
LOWEST = -1e30
AUX = 16
BF = jnp.bfloat16
F32 = jnp.float32

CYCLE = (0, 2, 4, 6, 7, 5, 3, 1)
OFFSETS = (0, 2, 1, 3)


def dot(a, b, contract, out=F32):
    return lax.dot_general(a, b, (contract, ((), ())), preferred_element_type=out)


COST = 0.02

NN = ((1,), (0,))
NT = ((1,), (1,))
TN = ((0,), (0,))


def forward_hop(v):
    n = len(CYCLE)
    return lax.ppermute(v, "row", [(CYCLE[i], CYCLE[(i + 1) % n]) for i in range(n)])


def backward_hop(v):
    n = len(CYCLE)
    return lax.ppermute(v, "row", [(CYCLE[(i + 1) % n], CYCLE[i]) for i in range(n)])


def col_swap(v, mask):
    count = lax.axis_size("col")
    return lax.ppermute(v, "col", [(i, i ^ mask) for i in range(count)])


def cycle_place():
    row = lax.axis_index("row")
    return sum(jnp.where(row == CYCLE[i], i, 0) for i in range(len(CYCLE))).astype(jnp.int32)


def cycle_rows(place, steps):
    places = lax.rem(place + jnp.array([s + len(CYCLE) for s in steps], jnp.int32), len(CYCLE))
    return sum(jnp.where(places == i, CYCLE[i], 0) for i in range(len(CYCLE))).astype(jnp.int32)


def after(value, *first):
    return lax.optimization_barrier((value, first))[0]


class Rounds:
    def __init__(self, block, axis):
        self.held, self.axis, self.done = (block, block), axis, []

    def step(self, *first):
        behind, ahead = after(self.held, first) if first else self.held
        if len(self.done) == 3:
            half = behind.shape[self.axis] // 2
            behind = lax.slice_in_dim(behind, 0, half, axis=self.axis)
            ahead = lax.slice_in_dim(ahead, half, 2 * half, axis=self.axis)
        self.held = forward_hop(behind), backward_hop(ahead)
        self.done.append(self.held)
        return self.held

    def pieces(self):
        while len(self.done) < 4:
            self.step()
        return [p for r in self.done for p in r]


ROUND_STEPS = (-1, 1, -2, 2, -3, 3, 4, 4)
BLOCK_STEPS = (0, 1, 2, 3, 4, 4, 5, 6, 7)


class RowSum:
    def __init__(self, blocks):
        self.blocks, self.hops, self.moving = blocks, 0, None
        if len(blocks) > 1:
            self.moving = blocks[4], blocks[5]

    def step(self):
        if len(self.blocks) == 1:
            return ()
        half = self.blocks[4].shape[0]

        def add(v, block):
            return (v.astype(F32) + block.astype(F32)).astype(BF)

        ahead, back = forward_hop(self.moving[0]), backward_hop(self.moving[1])
        up = (self.blocks[3], self.blocks[2], self.blocks[1], None)[self.hops]
        down = (self.blocks[6], self.blocks[7], self.blocks[8], None)[self.hops]
        if self.hops == 0:
            ahead = jnp.concatenate([add(ahead, up[:half]), up[half:]], axis=0)
            back = jnp.concatenate([down[:half], add(back, down[half:])], axis=0)
        elif up is not None:
            ahead, back = add(ahead, up), add(back, down)
        self.hops += 1
        self.moving = ahead, back
        return self.moving

    def result(self):
        if len(self.blocks) == 1:
            return lax.psum_scatter(self.blocks[0].astype(F32), "row", scatter_dimension=0, tiled=True)
        while self.hops < 4:
            self.step()
        ahead, back = self.moving
        return self.blocks[0].astype(F32) + ahead.astype(F32) + back.astype(F32)


def col_pieces(v):
    side = col_swap(v, 2)
    return [v, side, col_swap(v, 1), col_swap(side, 1)]


def col_exchange(near, far):
    own = near.shape[0] // 2
    other = col_swap(far, 1)
    passed = (near[own:].astype(F32) + other[own:].astype(F32)).astype(BF)
    return (near, other, col_swap(passed, 2)), passed


def whole(shape):
    return pl.BlockSpec(shape, lambda *_: (0,) * len(shape))


ANY = pl.BlockSpec(memory_space=pl.ANY)


def call(kernel, name, args, outs, prefetch=(), scratch=(), specs=None, out_specs=None, aliases=None, grid=(1,), flops=0, exps=0, limit=20):
    args, outs = list(args), list(outs)
    moved = sum(a.size * a.dtype.itemsize for a in args) + sum(
        math.prod(o.shape) * o.dtype.itemsize for o in outs
    )
    return pl.pallas_call(
        kernel,
        grid_spec=pltpu.PrefetchScalarGridSpec(
            num_scalar_prefetch=len(prefetch),
            grid=grid,
            in_specs=specs or [whole(a.shape) for a in args],
            out_specs=out_specs or [whole(o.shape) for o in outs],
            scratch_shapes=list(scratch),
        ),
        out_shape=outs,
        input_output_aliases=aliases or {},
        cost_estimate=pl.CostEstimate(flops=int(flops * COST), bytes_accessed=int(moved * COST), transcendentals=int(exps * COST)),
        compiler_params=pltpu.CompilerParams(vmem_limit_bytes=limit << 20),
        name=name,
    )(*prefetch, *args)


def struct(shape, kind):
    return jax.ShapeDtypeStruct(tuple(shape), kind)


def rows_at(start, count):
    return pl.ds(pl.multiple_of(start, 4), count)


def assemble_kernel(split, starts, *refs):
    pieces, (mix, out, held) = refs[:-3], refs[-3:]
    for i, piece in enumerate(pieces):
        held[pl.ds(pl.multiple_of(starts[i], 16), piece.shape[0]), :] = piece[...]
    mix[...] = held[:, :split].T
    out[...] = held[:, split:].T


def assemble(pieces, starts, split):
    width = pieces[0].shape[1]
    total = sum(p.shape[0] for p in pieces)
    return call(
        functools.partial(assemble_kernel, split),
        "assemble",
        pieces,
        [struct((split, total), BF), struct((width - split, total), BF)],
        prefetch=[starts],
        scratch=[pltpu.VMEM((total, width), BF)],
    )


def project_into(pieces, weight, turn, marks, q_out, k_out, v_out, heads):
    half = HEAD // 2
    width = heads * HEAD
    begin = 0
    for piece in pieces:
        count = piece.shape[0]
        lanes = slice(begin, begin + count)
        begin += count
        mixed = dot(weight[...], piece[...], NT)
        cosine, sine = turn[:half, lanes], turn[half:, lanes]
        for h in range(heads):
            for base, out, scale, tail in (
                (0, q_out, 1.0 / math.sqrt(HEAD), AUX),
                (width, k_out, None, 0),
            ):
                at = base + h * HEAD
                first, second = mixed[at : at + half], mixed[at + half : at + HEAD]
                turned = jnp.concatenate(
                    [first * cosine - second * sine, second * cosine + first * sine], axis=0
                )
                if scale is not None:
                    turned = turned * scale
                out[h, :HEAD, lanes] = turned.astype(BF)
                out[h, HEAD:, lanes] = marks[tail : tail + AUX, lanes]
            at = 2 * width + h * HEAD
            v_out[h, :HEAD, lanes] = mixed[at : at + HEAD].astype(BF)
            v_out[h, HEAD:, lanes] = marks[2 * AUX : 3 * AUX, lanes]


def attend_kernel(mode, heads, count, slot, *refs):
    pieces, refs = refs[:count], refs[count:]
    weight, turn, marks = refs[:3]
    refs = refs[3:]
    if mode != "first":
        q_own, top_in, sum_in, acc_in = refs[:4]
        refs = refs[7:]
    if mode == "last":
        w_out, refs = refs[0], refs[1:]
    k, v, q = refs[:3]
    refs = refs[3:]
    project_into(pieces, weight, turn, marks, q, k, v, heads)
    if mode == "first":
        q_own, refs = refs[0], refs[1:]
        q_own[...] = q[...]
    each = range(heads)
    scores = [dot(k[h], q_own[h], TN) for h in each]
    news = [jnp.max(s, axis=0, keepdims=True) for s in scores]
    if mode != "first":
        olds = [top_in[h : h + 1] for h in each]
        news = [jnp.maximum(o, n) for o, n in zip(olds, news)]
        keeps = [jnp.exp(o - n) for o, n in zip(olds, news)]
    weights = [jnp.exp(s - n) for s, n in zip(scores, news)]
    sums = [jnp.sum(w, axis=0, keepdims=True) for w in weights]
    values = [dot(v[h, :HEAD, :], w.astype(BF), NN) for h, w in enumerate(weights)]
    if mode != "first":
        sums = [sum_in[h : h + 1] * keeps[h] + sums[h] for h in each]
        values = [acc_in[h] * keeps[h] + values[h] for h in each]
    if mode != "last":
        top, total, acc = refs
        for h in each:
            top[h : h + 1] = news[h]
            total[h : h + 1] = sums[h]
            acc[h] = values[h]
        return
    near, far, context_bf, context, log_total = refs
    for h in each:
        value = values[h] / sums[h]
        context[h] = value
        context_bf[h * HEAD : (h + 1) * HEAD] = value.astype(BF)
        log_total[h : h + 1] = news[h] + jnp.log(sums[h])
    attn = dot(context_bf[...], w_out[...], TN)
    half = near.shape[0]
    near[...] = attn[:half].astype(BF)
    far[...] = attn[half:].astype(BF)


def attend(mode, pieces, slot, weight, turn, marks, heads, total, group, carried=(), w_out=None):
    width = sum(p.shape[0] for p in pieces)
    rows = HEAD + AUX

    def lanes(*lead):
        return pl.BlockSpec((*lead, width), lambda i, s: (*(0,) * len(lead), s[0]))

    args = [*pieces, weight, turn, marks, *carried]
    specs = [whole(p.shape) for p in pieces]
    specs += [whole(weight.shape), lanes(turn.shape[0]), lanes(marks.shape[0])]
    buffers = [struct((heads, rows, total), BF)] * 3
    outs, out_specs = list(buffers), [lanes(heads, rows)] * 3
    aliases = {}
    if mode != "first":
        specs += [whole(c.shape) for c in carried[:4]] + [ANY] * 3
        base = 1 + len(pieces) + 3 + 4
        aliases = {base: 0, base + 1: 1, base + 2: 2}
    features = weight.shape[1]
    if mode == "last":
        args.append(w_out)
        specs.append(whole(w_out.shape))
        extra = [
            struct((group // 2, features), BF),
            struct((group // 2, features), BF),
            struct((heads * HEAD, group), BF),
            struct((heads, HEAD, group), F32),
            struct((heads, group), F32),
        ]
    else:
        extra = [
            struct((heads, group), F32),
            struct((heads, group), F32),
            struct((heads, HEAD, group), F32),
        ]
        if mode == "first":
            extra = [struct((heads, rows, group), BF)] + extra
    outs += extra
    out_specs += [whole(e.shape) for e in extra]
    scores = heads * width * group
    return call(
        functools.partial(attend_kernel, mode, heads, len(pieces)),
        "attend",
        args,
        outs,
        prefetch=[slot],
        specs=specs,
        out_specs=out_specs,
        aliases=aliases,
        flops=scores * 512,
        exps=scores,
    )


def with_terms(q, g):
    return jnp.concatenate([q[:HEAD], q[HEAD:] + g[HEAD:]], axis=0)


def query_grad_kernel(heads, q, g, k, v, out_in, out):
    @pl.when(pl.program_id(0) == 0)
    def _():
        out[...] = out_in[...]

    rows = HEAD + AUX
    each = range(heads)
    terms = [g[h * rows : (h + 1) * rows] for h in each]
    probs = [jnp.exp(dot(k[h], with_terms(q[h], terms[h]), TN)) for h in each]
    grads = [(probs[h] * dot(v[h], terms[h], TN)).astype(BF) for h in each]
    for h in each:
        out[h] += dot(k[h, :HEAD, :], grads[h], NN)


def query_grad(q, g, keys, values, heads, width, begin, steps, carried):
    rows = keys.shape[1]
    group = q.shape[2]
    each = pl.BlockSpec((heads, rows, width), lambda i: (0, 0, i + begin))
    scores = heads * group * steps * width
    return call(
        functools.partial(query_grad_kernel, heads),
        "query_grad",
        [q, g, keys, values, carried],
        [struct((heads, HEAD, group), F32)],
        specs=[whole(q.shape), whole(g.shape), each, each, whole(carried.shape)],
        grid=(steps,),
        flops=scores * 768,
        exps=scores,
    )[0]


def key_grad_kernel(heads, count, carried, slots, *refs):
    pieces, (q, k, v), refs = refs[:count], refs[count : count + 3], refs[count + 3 :]
    rows = HEAD + AUX
    each = range(heads)
    if carried:
        dk_in, dv_in = refs[:2]
        refs = refs[2:]
    dk, dv, norms = refs

    def of(h):
        parts = [p[h * rows : (h + 1) * rows] for p in pieces]
        return parts[0] if count == 1 else jnp.concatenate(parts, axis=1)

    terms = [of(h) for h in each]
    probs = [jnp.exp(dot(with_terms(q[h], terms[h]), k[h], TN)) for h in each]
    grads = [(probs[h] * dot(terms[h], v[h], TN)).astype(BF) for h in each]
    for h in each:
        value = dot(terms[h][:HEAD], probs[h].astype(BF), NN)
        key = dot(q[h, :HEAD, :], grads[h], NN)
        dv[h] = dv_in[h] + value if carried else value
        dk[h] = dk_in[h] + key if carried else key
    for i in range(norms.shape[0]):
        norms[i] = pieces[i][heads * rows : heads * rows + NORM_ROWS, :NORM_LANES].astype(F32)


NORM_LANES = 256


def key_grad(pieces, chunks, slots, q, keys, values, heads, group, sums=()):
    width = sum(p.shape[1] for p in pieces)
    rows = HEAD + AUX
    own = pl.BlockSpec((heads, rows, group), lambda i, s: (0, 0, s[1]))
    specs = [whole(p.shape) for p in pieces]
    specs += [pl.BlockSpec((heads, rows, width), lambda i, s: (0, 0, s[0])), own, own]
    specs += [whole(s.shape) for s in sums]
    scores = heads * group * width
    return call(
        functools.partial(key_grad_kernel, heads, len(pieces), bool(sums)),
        "key_grad",
        [*pieces, q, keys, values, *sums],
        [struct((heads, HEAD, group), F32)] * 2 + [struct((chunks, NORM_ROWS, NORM_LANES), F32)],
        prefetch=[slots],
        specs=specs,
        flops=scores * 1024,
        exps=scores,
    )


def norm_parts(values):
    centered = values - jnp.mean(values, axis=-1, keepdims=True)
    inverse = lax.rsqrt(jnp.mean(centered * centered, axis=-1, keepdims=True) + NORM_EPS)
    return centered * inverse, inverse


def norm_back(grad_out, normed, inverse, gain):
    scaled = grad_out * gain
    grad_in = inverse * (
        scaled
        - jnp.mean(scaled, axis=-1, keepdims=True)
        - normed * jnp.mean(scaled * normed, axis=-1, keepdims=True)
    )
    sums = [jnp.sum(grad_out * normed, axis=0, keepdims=True), jnp.sum(grad_out, axis=0, keepdims=True)]
    return grad_in, sums


def col_total(near, other, last):
    own = last.shape[0]
    return near[:own].astype(F32) + other[:own].astype(F32) + last[...].astype(F32)


def first_norm_kernel(near, other, last, tokens, gain, bias, residual, hidden):
    value = tokens[...].astype(F32) + col_total(near, other, last)
    residual[...] = value
    normed, _ = norm_parts(value)
    hidden[...] = (normed * gain[...] + bias[...]).astype(BF)


def second_norm_kernel(near, other, last, residual, gain1, bias1, gain2, bias2, cotangent, result, grad, grad_bf, sums):
    hidden = norm_parts(residual[...])[0] * gain1[...] + bias1[...]
    normed, inverse = norm_parts(hidden + col_total(near, other, last))
    result[...] = (normed * gain2[...] + bias2[...]).astype(BF)
    value, (dgain, dbias) = norm_back(cotangent[...].astype(F32), normed, inverse, gain2[...])
    grad[...] = value
    grad_bf[...] = value.astype(BF)
    sums[0:1] = dgain
    sums[1:2] = dbias


def first_norm_back_kernel(near, other, last, residual, gain, grad2, sums2, grad, package):
    normed, inverse = norm_parts(residual[...])
    grad_out = grad2[...] + col_total(near, other, last)
    value, (dgain, dbias) = norm_back(grad_out, normed, inverse, gain[...])
    grad[...] = value
    own = value.shape[0]
    package[:own] = value.astype(BF)
    sums = jnp.concatenate([dgain, dbias, sums2[0:1], sums2[1:2]], axis=0)
    high = sums.astype(BF)
    low = (sums - high.astype(F32)).astype(BF)
    blank = jnp.zeros((8, sums.shape[1]), F32)
    package[own:] = jnp.concatenate([high.astype(F32), low.astype(F32), blank], axis=0).astype(BF)


def stacked(refs, rows):
    return jnp.concatenate([r[:rows] for r in refs], axis=0)


def forward_kernel(count, units, starts, *refs):
    pieces, hidden, (gu, dn, gate_up, inner, near, far) = refs[:count], refs[count:-6], refs[-6:]
    for i, piece in enumerate(pieces):
        rows = pl.ds(pl.multiple_of(starts[i], 16), piece.shape[0])
        gu[rows, :] = piece[:, : 2 * units]
        dn[rows, :] = piece[:, 2 * units :]
    pairs = len(hidden) // 2
    for out, part in ((near, hidden[:pairs]), (far, hidden[pairs:])):
        x = stacked(part, part[0].shape[0])
        size = x.shape[0]
        begin = 0 if out is near else size
        both = dot(x, gu[...], NN)
        gate_up[begin : begin + size] = both
        up, gate = both[:, :units], both[:, units:]
        value = (gate * jax.nn.sigmoid(gate) * up).astype(BF)
        inner[begin : begin + size] = value
        out[...] = dot(value, dn[...], NT).astype(BF)


def backward_kernel(units, *refs):
    pieces, (gu, dn, gate_up, grads, near, far) = refs[:-6], refs[-6:]
    pairs = len(pieces) // 2
    for out, part in ((near, pieces[:pairs]), (far, pieces[pairs:])):
        g = stacked(part, part[0].shape[0])
        size = g.shape[0]
        begin = 0 if out is near else size
        grad_inner = dot(g, dn[...], NN)
        up = gate_up[begin : begin + size, :units]
        gate = gate_up[begin : begin + size, units:]
        sigma = jax.nn.sigmoid(gate)
        grads[begin : begin + size, :units] = (grad_inner * gate * sigma).astype(BF)
        grads[begin : begin + size, units:] = (
            grad_inner * up * sigma * (1.0 + gate * (1.0 - sigma))
        ).astype(BF)
        out[...] = dot(grads[begin : begin + size], gu[...], NT).astype(BF)


def write_blocks(held, starts, outs):
    for i, out in enumerate(outs):
        out[...] = held[pl.ds(pl.multiple_of(starts[i], 16), out.shape[0]), :]


def block_structs(features, width, ring):
    if not ring:
        return [struct((features, width), BF)]
    share = features // len(CYCLE)
    sizes = [share] * 4 + [share // 2] * 2 + [share] * 3
    return [struct((n, width), BF) for n in sizes]


def ffn_grad_kernel(units, n_blocks, starts, *refs):
    hidden, g, (grads, inner) = refs[:4], refs[4:8], refs[8:10]
    outs, held = refs[10 : 10 + n_blocks], refs[10 + n_blocks]
    own = hidden[0].shape[0]
    turned = stacked(hidden, own).T
    for t in range(0, 2 * units, units):
        held[:, t : t + units] = dot(turned, grads[:, t : t + units], NN).astype(BF)
    held[:, 2 * units :] = dot(stacked(g, own).T, inner[...], NN).astype(BF)
    write_blocks(held, starts, outs)


def prepare_kernel(heads, own, *refs):
    pieces, (w_out, context, log_total, package) = refs[:4], refs[4:]
    g = stacked(pieces, own)
    rows = HEAD + AUX
    grad = dot(w_out[...], g, NT).astype(BF)
    index = lax.broadcasted_iota(jnp.int32, (AUX, g.shape[0]), 0)
    for h in range(heads):
        part = grad[h * HEAD : (h + 1) * HEAD]
        package[h * rows : h * rows + HEAD] = part
        delta = jnp.sum(part.astype(F32) * context[h], axis=0, keepdims=True)
        tail = jnp.zeros(index.shape, F32)
        for at, value in ((8, -log_total[h : h + 1]), (11, -delta)):
            for j in range(3):
                high = value.astype(BF).astype(F32)
                tail = jnp.where(index == at + j, high, tail)
                value = value - high
        package[h * rows + HEAD : (h + 1) * rows] = tail.astype(BF)

    def sums(piece):
        both = piece[own : own + 16].astype(F32)
        return both[:4] + both[4:8]

    total = (sums(pieces[0]) + sums(pieces[1])) + (sums(pieces[2]) + sums(pieces[3]))
    high = total.astype(BF).astype(F32)
    both = jnp.concatenate([high, total - high], axis=0)
    base = heads * rows
    package[base:, NORM_LANES:] = jnp.zeros((package.shape[0] - base, package.shape[1] - NORM_LANES), BF)
    parts = [both[:, i * NORM_LANES : (i + 1) * NORM_LANES] for i in range(both.shape[1] // NORM_LANES)]
    parts.append(jnp.zeros((package.shape[0] - base - 8 * len(parts), NORM_LANES), F32))
    package[base:, :NORM_LANES] = jnp.concatenate(parts, axis=0).astype(BF)


def turn_back(first, second, cosine, sine):
    return jnp.concatenate([first * cosine + second * sine, second * cosine - first * sine], axis=0)


def early_grad_kernel(heads, own, n_x, slots, *refs):
    x_refs, g_refs, refs = refs[:n_x], refs[n_x : n_x + 4], refs[n_x + 4 :]
    grad_query, turn, context, mixed, held = refs
    half = HEAD // 2
    scale = 1.0 / math.sqrt(HEAD)
    for h in range(heads):
        value = grad_query[h] * scale
        mixed[h * HEAD : (h + 1) * HEAD] = turn_back(value[:half], value[half:], turn[:half], turn[half:]).astype(BF)
    x = stacked(x_refs, x_refs[0].shape[0])
    width = heads * HEAD
    held[:, :width] = dot(mixed[...], x, NN).T.astype(BF)
    held[:, width:] = dot(context[...], stacked(g_refs, own), NN).T.astype(BF)


def late_grad_kernel(heads, n_x, n_blocks, slots, starts, *refs):
    x_refs, refs = refs[:n_x], refs[n_x:]
    mixed_q, grad_key, grad_value, early, turn, weight, near, far, *refs = refs
    outs, held, mixed = refs[:n_blocks], refs[n_blocks], refs[n_blocks + 1]
    half = HEAD // 2
    width = heads * HEAD
    mixed[:width] = mixed_q[...]
    for h in range(heads):
        value = grad_key[h]
        mixed[width + h * HEAD : width + (h + 1) * HEAD] = turn_back(
            value[:half], value[half:], turn[:half], turn[half:]
        ).astype(BF)
        mixed[2 * width + h * HEAD : 2 * width + (h + 1) * HEAD] = grad_value[h].astype(BF)
    back = dot(mixed[...], weight[...], TN)
    size = near.shape[0]
    near[...] = back[:size].astype(BF)
    far[...] = back[size:].astype(BF)
    x = stacked(x_refs, x_refs[0].shape[0])
    held[:, : 2 * width] = early[...]
    held[:, 2 * width :] = dot(mixed[width:], x, NN).T.astype(BF)
    write_blocks(held, starts, outs)


NORM_ROWS = 24


def norm_total_kernel(rows, *refs):
    pieces, (out, held) = refs[:-2], refs[-2:]
    at = 0
    for piece in pieces:
        for i in range(piece.shape[0]):
            held[rows[at]] = piece[i]
            at += 1
    total = held[0]
    for r in range(1, at):
        total = total + held[r]
    for i in range(NORM_ROWS // 8):
        part = total[8 * i : 8 * i + 8]
        out[:, i * NORM_LANES : (i + 1) * NORM_LANES] = part[:4] + part[4:]


def slot_tables(seq_lengths, packed_order, chunk_rows, col, local, waits):
    cols = lax.axis_size("col")
    blocks = packed_order.reshape(-1, local)
    wanted = (chunk_rows[:, None] * cols + (col ^ jnp.array(OFFSETS, jnp.int32))[None, :]).reshape(-1)
    index = jnp.arange(blocks.shape[0], dtype=jnp.int32)
    slots = jnp.sum(
        jnp.where(wanted[:, None, None] == index[None, :, None], blocks[None], 0), axis=1
    ).reshape(1, -1)
    count = seq_lengths.shape[0]
    seq = jnp.zeros_like(slots)
    start = jnp.zeros_like(slots)
    end = jnp.int32(0)
    for s in range(count):
        end = end + seq_lengths[s]
        passed = slots >= end
        seq = seq + passed.astype(jnp.int32)
        start = jnp.where(passed, end, start)
    positions = after((slots - start).astype(F32), waits[0])
    half = HEAD // 2
    freqs = ROPE_BASE ** (-jnp.arange(half, dtype=F32) * 2.0 / HEAD)
    angles = positions * freqs[:, None]
    turn = jnp.concatenate([jnp.cos(angles), jnp.sin(angles)], axis=0)
    line = jnp.arange(3 * AUX, dtype=jnp.int32)[:, None]
    member = lax.rem(line, AUX) == after(seq, waits[1])
    ones = ((line >= 8) & (line < 11)) | ((line >= 2 * AUX + 11) & (line < 2 * AUX + 14))
    marks = jnp.where(ones, 1.0, 0.0)
    marks = jnp.where((line < 8) & member, 1.0, marks)
    marks = jnp.where((line >= AUX) & (line < AUX + 8) & ~member, FAR, marks)
    return turn, marks.astype(BF)


def local(
    tokens,
    w_qkv,
    w_out,
    w_gate_up,
    w_down,
    gain1,
    bias1,
    gain2,
    bias2,
    cotangent,
    seq_lengths,
    packed_order,
):
    rows = lax.axis_size("row")
    row, col = lax.axis_index("row"), lax.axis_index("col")
    ring = rows == len(CYCLE)
    own, features = tokens.shape
    group = own * lax.axis_size("col")
    total = group * rows
    share = w_qkv.shape[0]
    width = w_qkv.shape[2]
    heads = width // HEAD
    units = w_gate_up.shape[2]
    gains = [v.reshape(1, features) for v in (gain1, bias1, gain2, bias2)]

    early = jnp.concatenate([w_qkv.reshape(share, 3 * width), w_out.T], axis=1)
    late = jnp.concatenate([w_gate_up.reshape(share, 2 * units), w_down.T], axis=1)

    pair = jnp.concatenate([tokens, col_swap(tokens, 2)], axis=0)
    x_pieces = [pair, col_swap(pair, 1)]
    if ring:
        place = cycle_place()
        half = share // 2
        starts = cycle_rows(place, (0, *ROUND_STEPS)) * share + jnp.array([0] * 8 + [half], jnp.int32)
        block_starts = cycle_rows(place, BLOCK_STEPS) * share + jnp.array([0] * 5 + [half] + [0] * 3, jnp.int32)
        chunk_rows = cycle_rows(place, (*ROUND_STEPS[:6], 0, 4))
        early_ring, pair_ring = Rounds(early, 0), Rounds(pair, 0)
        waits = [early_ring.step()]
        pair_ring.step(waits[0])
        waits.append(early_ring.step())
    else:
        starts = block_starts = jnp.zeros((1,), jnp.int32)
        chunk_rows = jnp.arange(rows, dtype=jnp.int32)
        waits = (), ()
        early_full = lax.all_gather(early, "row", axis=0, tiled=True)
        w_mix, full_out = assemble([early_full], starts, 3 * width)

    turn, marks = slot_tables(seq_lengths, packed_order, chunk_rows, col, own, waits)
    if ring:
        early_ring.step(turn)
        pair_ring.step(early_ring.step(marks))
        w_mix, full_out = assemble(
            after([early, *early_ring.pieces()], pair_ring.done[0]), starts, 3 * width
        )
    fixed = (w_mix, turn, marks, heads, total, group)

    def at(slot):
        return jnp.asarray(slot, jnp.int32).reshape(1)

    own_slot = at(6) if ring else at(row)
    keys, values, queries, own_q, *state = attend("first", x_pieces, own_slot, *fixed)
    if ring:
        late_ring = Rounds(late, 0)

        def chunks(held):
            return [p for h in held for p in (h, col_swap(h, 1))]

        def middle(i, pieces):
            return attend("middle", pieces, at(i), *fixed, (own_q, *state, keys, values, queries))

        first, second = pair_ring.done
        first = chunks(after(first, w_mix))
        pair_ring.step(state[0])
        second = chunks(after(second, state[0]))
        keys, values, queries, *state = middle(0, after(first, pair_ring.done[1]))
        keys, values, queries, *state = middle(1, second)
        third = chunks(after(pair_ring.done[2], state[0]))
        pair_ring.step(state[0])
        late_ring.step(pair_ring.done[2], state[0])
        keys, values, queries, *state = middle(2, third)
        far = after(pair_ring.done[3], state[0])
        pieces = [*far, *(col_swap(p, 1) for p in far)]
        keys, values, queries, *finished = attend(
            "last", pieces, at(7), *fixed, (own_q, *state, keys, values, queries), full_out
        )
    else:
        blocks = lax.all_gather(jnp.concatenate(x_pieces, axis=0), "row", axis=0, tiled=False)

        def block(i):
            slot = lax.rem(row + i, rows)
            return [lax.dynamic_index_in_dim(blocks, slot, 0, keepdims=False)], at(slot)

        def step(i, carried):
            *state, keys, values, queries = carried
            keys, values, queries, *state = attend(
                "middle", *block(i), *fixed, (own_q, *state, keys, values, queries)
            )
            return (*state, keys, values, queries)

        *state, keys, values, queries = lax.fori_loop(1, rows - 1, step, (*state, keys, values, queries))
        keys, values, queries, *finished = attend(
            "last", *block(rows - 1), *fixed, (own_q, *state, keys, values, queries), full_out
        )
    near, far, context_bf, context, log_total = finished

    if ring:
        near = after(near, late_ring.done[0])
        late_ring.step(context_bf)
    else:
        late_pieces = [lax.all_gather(late, "row", axis=0, tiled=True)]

    part = struct((group // 2, features), BF)
    flat = struct((own, features), F32)
    residual1, hidden = call(
        first_norm_kernel,
        "first_norm",
        [*col_exchange(near, far)[0], tokens, *gains[:2]],
        [flat, struct((own, features), BF)],
    )
    if ring:
        late_ring.step(hidden)
        late_pieces = [late, *late_ring.pieces()]
    hidden_pieces = col_pieces(hidden)
    w_gu, w_dn, gate_up, inner, near, far = call(
        functools.partial(forward_kernel, len(late_pieces), units),
        "ffn_forward",
        [*late_pieces, *hidden_pieces],
        [
            struct((features, 2 * units), BF),
            struct((features, units), BF),
            struct((group, 2 * units), F32),
            struct((group, units), BF),
            part,
            part,
        ],
        prefetch=[starts],
        flops=6 * group * features * units,
    )
    result, grad_res2, grad_bf, sums2 = call(
        second_norm_kernel,
        "second_norm",
        [*col_exchange(near, far)[0], residual1, *gains, cotangent],
        [struct((own, features), BF), flat, struct((own, features), BF), struct((8, features), F32)],
    )
    grad_pieces = col_pieces(grad_bf)
    grad_gate_up, near, far = call(
        functools.partial(backward_kernel, units),
        "ffn_backward",
        [*grad_pieces, w_gu, w_dn, gate_up],
        [struct((group, 2 * units), BF), part, part],
        flops=6 * group * features * units,
    )
    exchanged, passed = col_exchange(near, far)
    grad_gate_up = after(grad_gate_up, passed)
    outs = block_structs(features, 3 * units, ring)
    blocks = call(
        functools.partial(ffn_grad_kernel, units, len(outs)),
        "ffn_grad",
        [*hidden_pieces, *grad_pieces, grad_gate_up, inner],
        outs,
        prefetch=[block_starts],
        scratch=[pltpu.VMEM((features, 3 * units), BF)],
        flops=6 * group * features * units,
    )
    residual1 = after(residual1, blocks)
    ffn_sum = RowSum(after(blocks, exchanged))
    sent = ffn_sum.step()
    grad_res1, package = call(
        first_norm_back_kernel,
        "first_norm_back",
        [*exchanged, residual1, gains[0], grad_res2, sums2],
        [flat, struct((own + 16, features), BF)],
    )
    attn_pieces = col_pieces(package)
    (package,) = call(
        functools.partial(prepare_kernel, heads, own),
        "prepare",
        [*attn_pieces, full_out, context, log_total],
        [struct((heads * (HEAD + AUX) + 32, group), BF)],
        flops=2 * width * features * group,
    )
    span = min(2 * group, total)
    steps_all = total // span
    grad_query = jnp.zeros((heads, HEAD, group), F32)
    if ring:
        package_ring = Rounds(package, 1)
        package_ring.step()
        grad_query = after(grad_query, sent)
        ffn_sum.step()
    grad_query = query_grad(own_q, package, keys, values, heads, span, 0, steps_all, grad_query)
    own_turn = pl.BlockSpec((HEAD, group), lambda i, s, *_: (0, s[0]))
    args = [*x_pieces, *attn_pieces, grad_query, turn, context_bf]
    specs = [whole(a.shape) for a in args]
    specs[-2] = own_turn
    mixed_q, early_grad = call(
        functools.partial(early_grad_kernel, heads, own, len(x_pieces)),
        "early_grad",
        args,
        [struct((width, group), BF), struct((features, 2 * width), BF)],
        prefetch=[own_slot],
        specs=specs,
        flops=4 * width * features * group,
    )

    def key_step(pieces, chunks, slot, sums):
        slots = jnp.where(jnp.arange(2) == 0, at(slot), own_slot)
        *sums, norms = key_grad(pieces, chunks, slots, queries, keys, values, heads, group, tuple(sums))
        return sums, norms

    norm_out = struct((4, features), F32)
    if ring:
        package_ring.step(early_grad)
        sums, norms = key_step([after(package, early_grad, package_ring.done[0])], 1, 6, ())
        norm_pieces = [norms]
        for i in range(3):
            sums, norms = key_step(package_ring.done[i], 2, i, sums)
            norm_pieces.append(norms)
            if i < 2:
                package_ring.step(norms)
        ffn_sum.moving = after(ffn_sum.moving, norms)
        sums, norms = key_step(package_ring.done[3], 1, 7, sums)
        norm_pieces.append(norms)
        (norm_sums,) = call(
            norm_total_kernel,
            "norm_total",
            norm_pieces,
            [norm_out],
            prefetch=[cycle_rows(place, (0, *ROUND_STEPS[:7]))],
            scratch=[pltpu.VMEM((rows, NORM_ROWS, NORM_LANES), F32)],
        )
    else:
        packages = lax.all_gather(package, "row", axis=0, tiled=False)

        def step(i, carried):
            sums, norms = carried
            piece = lax.dynamic_index_in_dim(packages, i, 0, keepdims=False)
            sums, more = key_step([piece], 1, i, sums)
            return tuple(sums), norms + more

        zeros = jnp.zeros((heads, HEAD, group), F32)
        sums, norms = lax.fori_loop(
            0, rows, step, ((zeros, zeros), jnp.zeros((1, NORM_ROWS, NORM_LANES), F32))
        )
        (norm_sums,) = call(
            norm_total_kernel,
            "norm_total",
            [norms],
            [norm_out],
            prefetch=[jnp.zeros((1,), jnp.int32)],
            scratch=[pltpu.VMEM((1, NORM_ROWS, NORM_LANES), F32)],
        )
    args = [*x_pieces, mixed_q, *sums, early_grad, turn, w_mix]
    specs = [whole(a.shape) for a in args]
    specs[-2] = own_turn
    outs = block_structs(features, 4 * width, ring)
    near, far, *blocks = call(
        functools.partial(late_grad_kernel, heads, len(x_pieces), len(outs)),
        "late_grad",
        args,
        [part, part, *outs],
        prefetch=[own_slot, block_starts],
        scratch=[pltpu.VMEM((features, 4 * width), BF), pltpu.VMEM((3 * width, group), BF)],
        specs=specs,
        flops=10 * width * features * group,
    )
    late_grad = RowSum(blocks).result()
    near, other, last = col_exchange(near, far)[0]
    ffn_grad = ffn_sum.result()
    grad_tokens = grad_res1 + (
        near[:own].astype(F32) + other[:own].astype(F32) + last.astype(F32)
    )
    grad_mix = jnp.concatenate([late_grad[:, :width], late_grad[:, 2 * width :]], axis=1)
    return (
        result,
        grad_tokens,
        grad_mix.reshape(share, 3, width),
        late_grad[:, width : 2 * width].T,
        ffn_grad[:, : 2 * units].reshape(share, 2, units),
        ffn_grad[:, 2 * units :].T,
        norm_sums[0],
        norm_sums[1],
        norm_sums[2],
        norm_sums[3],
    )


def solution(mesh):
    placed = (
        P(("row", "col"), None),
        P("row", None, "col"),
        P("col", "row"),
        P("row", None, "col"),
        P("col", "row"),
        P(),
        P(),
        P(),
        P(),
        P(("row", "col"), None),
        P(),
        P(),
    )
    return jax.shard_map(
        local,
        mesh=mesh,
        in_specs=placed,
        out_specs=(
            P(("row", "col"), None),
            P(("row", "col"), None),
            P("row", None, "col"),
            P("col", "row"),
            P("row", None, "col"),
            P("col", "row"),
            P(),
            P(),
            P(),
            P(),
        ),
        check_vma=False,
    )
```

```python
import functools
import math

import jax
import jax.numpy as jnp
from jax import lax
from jax.experimental import pallas as pl
from jax.experimental.pallas import tpu as pltpu
from jax.sharding import PartitionSpec as P

HEAD = 64
ROPE_BASE = 1000.0
NORM_EPS = 1e-12
FAR = -(2.0**100)
LOWEST = -1e30
AUX = 16
BF = jnp.bfloat16
F32 = jnp.float32

CYCLE = (0, 2, 4, 6, 7, 5, 3, 1)
OFFSETS = (0, 2, 1, 3)


def dot(a, b, contract, out=F32):
    return lax.dot_general(a, b, (contract, ((), ())), preferred_element_type=out)


COST = 0.02

NN = ((1,), (0,))
NT = ((1,), (1,))
TN = ((0,), (0,))


def forward_hop(v):
    n = len(CYCLE)
    return lax.ppermute(v, "row", [(CYCLE[i], CYCLE[(i + 1) % n]) for i in range(n)])


def backward_hop(v):
    n = len(CYCLE)
    return lax.ppermute(v, "row", [(CYCLE[(i + 1) % n], CYCLE[i]) for i in range(n)])


def col_swap(v, mask):
    count = lax.axis_size("col")
    return lax.ppermute(v, "col", [(i, i ^ mask) for i in range(count)])


def cycle_place():
    row = lax.axis_index("row")
    return sum(jnp.where(row == CYCLE[i], i, 0) for i in range(len(CYCLE))).astype(jnp.int32)


def cycle_rows(place, steps):
    places = lax.rem(place + jnp.array([s + len(CYCLE) for s in steps], jnp.int32), len(CYCLE))
    return sum(jnp.where(places == i, CYCLE[i], 0) for i in range(len(CYCLE))).astype(jnp.int32)


def after(value, *first):
    return lax.optimization_barrier((value, first))[0]


class Rounds:
    def __init__(self, block, axis):
        self.block, self.held, self.axis, self.done = block, (block, block), axis, []

    def step(self, *first):
        behind, ahead = after(self.held, first) if first else self.held
        if len(self.done) == 3:
            half = behind.shape[self.axis] // 2
            behind = lax.slice_in_dim(behind, 0, half, axis=self.axis)
            ahead = lax.slice_in_dim(ahead, half, 2 * half, axis=self.axis)
        self.held = forward_hop(behind), backward_hop(ahead)
        self.done.append(self.held)
        return self.held

    def pieces(self):
        while len(self.done) < 4:
            self.step()
        return [p for r in self.done for p in r]


ROUND_STEPS = (-1, 1, -2, 2, -3, 3, 4, 4)
BLOCK_STEPS = (0, 1, 2, 3, 4, 4, 5, 6, 7)


class RowSum:
    def __init__(self, blocks):
        self.blocks, self.hops, self.moving = blocks, 0, None
        if len(blocks) > 1:
            self.moving = blocks[4], blocks[5]

    def step(self):
        if len(self.blocks) == 1:
            return ()
        half = self.blocks[4].shape[0]

        def add(v, block):
            return (v.astype(F32) + block.astype(F32)).astype(BF)

        ahead, back = forward_hop(self.moving[0]), backward_hop(self.moving[1])
        up = (self.blocks[3], self.blocks[2], self.blocks[1], None)[self.hops]
        down = (self.blocks[6], self.blocks[7], self.blocks[8], None)[self.hops]
        if self.hops == 0:
            ahead = jnp.concatenate([add(ahead, up[:half]), up[half:]], axis=0)
            back = jnp.concatenate([down[:half], add(back, down[half:])], axis=0)
        elif up is not None:
            ahead, back = add(ahead, up), add(back, down)
        self.hops += 1
        self.moving = ahead, back
        return self.moving

    def result(self):
        if len(self.blocks) == 1:
            return lax.psum_scatter(self.blocks[0].astype(F32), "row", scatter_dimension=0, tiled=True)
        while self.hops < 4:
            self.step()
        ahead, back = self.moving
        return self.blocks[0].astype(F32) + ahead.astype(F32) + back.astype(F32)


def col_pieces(v, *first):
    side = col_swap(v, 2)
    return [v, side, col_swap(v, 1), col_swap(after(side, first), 1)]


def col_exchange(near, far):
    own = near.shape[0] // 2
    other = col_swap(far, 1)
    passed = (near[own:].astype(F32) + other[own:].astype(F32)).astype(BF)
    return (near, other, col_swap(passed, 2)), passed


def whole(shape):
    return pl.BlockSpec(shape, lambda *_: (0,) * len(shape))


ANY = pl.BlockSpec(memory_space=pl.ANY)


def call(kernel, name, args, outs, prefetch=(), scratch=(), specs=None, out_specs=None, aliases=None, grid=(1,), flops=0, exps=0, limit=20):
    args, outs = list(args), list(outs)
    moved = sum(a.size * a.dtype.itemsize for a in args) + sum(
        math.prod(o.shape) * o.dtype.itemsize for o in outs
    )
    return pl.pallas_call(
        kernel,
        grid_spec=pltpu.PrefetchScalarGridSpec(
            num_scalar_prefetch=len(prefetch),
            grid=grid,
            in_specs=specs or [whole(a.shape) for a in args],
            out_specs=out_specs or [whole(o.shape) for o in outs],
            scratch_shapes=list(scratch),
        ),
        out_shape=outs,
        input_output_aliases=aliases or {},
        cost_estimate=pl.CostEstimate(flops=int(flops * COST), bytes_accessed=int(moved * COST), transcendentals=int(exps * COST)),
        compiler_params=pltpu.CompilerParams(vmem_limit_bytes=limit << 20),
        name=name,
    )(*prefetch, *args)


def struct(shape, kind):
    return jax.ShapeDtypeStruct(tuple(shape), kind)


def rows_at(start, count):
    return pl.ds(pl.multiple_of(start, 4), count)


def assemble_kernel(split, cuts, starts, *refs):
    pieces, (mix, out, held) = refs[:-3], refs[-3:]
    for i, piece in enumerate(pieces):
        for begin, count, shift in cuts[i]:
            held[pl.ds(pl.multiple_of(starts[i] + shift, 16), count), :] = piece[begin : begin + count]
    mix[...] = held[:, :split].T
    out[...] = held[:, split:].T


def assemble(pieces, cuts, starts, split):
    width = pieces[0].shape[1]
    total = sum(c[1] for cut in cuts for c in cut)
    return call(
        functools.partial(assemble_kernel, split, cuts),
        "assemble",
        pieces,
        [struct((split, total), BF), struct((width - split, total), BF)],
        prefetch=[starts],
        scratch=[pltpu.VMEM((total, width), BF)],
    )


def project_into(pieces, weight, turn, marks, q_out, k_out, v_out, heads):
    half = HEAD // 2
    width = heads * HEAD
    begin = 0
    for piece in pieces:
        count = piece.shape[0]
        lanes = slice(begin, begin + count)
        begin += count
        mixed = dot(weight[...], piece[...], NT)
        cosine, sine = turn[:half, lanes], turn[half:, lanes]
        for h in range(heads):
            for base, out, scale, tail in (
                (0, q_out, 1.0 / math.sqrt(HEAD), AUX),
                (width, k_out, None, 0),
            ):
                at = base + h * HEAD
                first, second = mixed[at : at + half], mixed[at + half : at + HEAD]
                turned = jnp.concatenate(
                    [first * cosine - second * sine, second * cosine + first * sine], axis=0
                )
                if scale is not None:
                    turned = turned * scale
                out[h, :HEAD, lanes] = turned.astype(BF)
                out[h, HEAD:, lanes] = marks[tail : tail + AUX, lanes]
            at = 2 * width + h * HEAD
            v_out[h, :HEAD, lanes] = mixed[at : at + HEAD].astype(BF)
            v_out[h, HEAD:, lanes] = marks[2 * AUX : 3 * AUX, lanes]


def attend_kernel(mode, heads, count, slot, *refs):
    pieces, refs = refs[:count], refs[count:]
    weight, turn, marks = refs[:3]
    refs = refs[3:]
    if mode != "first":
        q_own, top_in, sum_in, acc_in = refs[:4]
        refs = refs[7:]
    if mode == "last":
        w_out, refs = refs[0], refs[1:]
    k, v, q = refs[:3]
    refs = refs[3:]
    project_into(pieces, weight, turn, marks, q, k, v, heads)
    if mode == "first":
        q_own, refs = refs[0], refs[1:]
        q_own[...] = q[...]
    each = range(heads)
    scores = [dot(k[h], q_own[h], TN) for h in each]
    news = [jnp.max(s, axis=0, keepdims=True) for s in scores]
    if mode != "first":
        olds = [top_in[h : h + 1] for h in each]
        news = [jnp.maximum(o, n) for o, n in zip(olds, news)]
        keeps = [jnp.exp(o - n) for o, n in zip(olds, news)]
    weights = [jnp.exp(s - n) for s, n in zip(scores, news)]
    sums = [jnp.sum(w, axis=0, keepdims=True) for w in weights]
    values = [dot(v[h, :HEAD, :], w.astype(BF), NN) for h, w in enumerate(weights)]
    if mode != "first":
        sums = [sum_in[h : h + 1] * keeps[h] + sums[h] for h in each]
        values = [acc_in[h] * keeps[h] + values[h] for h in each]
    if mode != "last":
        top, total, acc = refs
        for h in each:
            top[h : h + 1] = news[h]
            total[h : h + 1] = sums[h]
            acc[h] = values[h]
        return
    near, far, context_bf, context, log_total = refs
    for h in each:
        value = values[h] / sums[h]
        context[h] = value
        context_bf[h * HEAD : (h + 1) * HEAD] = value.astype(BF)
        log_total[h : h + 1] = news[h] + jnp.log(sums[h])
    attn = dot(context_bf[...], w_out[...], TN)
    half = near.shape[0]
    near[...] = attn[:half].astype(BF)
    far[...] = attn[half:].astype(BF)


def attend(mode, pieces, slot, weight, turn, marks, heads, total, group, carried=(), w_out=None):
    width = sum(p.shape[0] for p in pieces)
    rows = HEAD + AUX

    def lanes(*lead):
        return pl.BlockSpec((*lead, width), lambda i, s: (*(0,) * len(lead), s[0]))

    args = [*pieces, weight, turn, marks, *carried]
    specs = [whole(p.shape) for p in pieces]
    specs += [whole(weight.shape), lanes(turn.shape[0]), lanes(marks.shape[0])]
    buffers = [struct((heads, rows, total), BF)] * 3
    outs, out_specs = list(buffers), [lanes(heads, rows)] * 3
    aliases = {}
    if mode != "first":
        specs += [whole(c.shape) for c in carried[:4]] + [ANY] * 3
        base = 1 + len(pieces) + 3 + 4
        aliases = {base: 0, base + 1: 1, base + 2: 2}
    features = weight.shape[1]
    if mode == "last":
        args.append(w_out)
        specs.append(whole(w_out.shape))
        extra = [
            struct((group // 2, features), BF),
            struct((group // 2, features), BF),
            struct((heads * HEAD, group), BF),
            struct((heads, HEAD, group), F32),
            struct((heads, group), F32),
        ]
    else:
        extra = [
            struct((heads, group), F32),
            struct((heads, group), F32),
            struct((heads, HEAD, group), F32),
        ]
        if mode == "first":
            extra = [struct((heads, rows, group), BF)] + extra
    outs += extra
    out_specs += [whole(e.shape) for e in extra]
    scores = heads * width * group
    return call(
        functools.partial(attend_kernel, mode, heads, len(pieces)),
        "attend",
        args,
        outs,
        prefetch=[slot],
        specs=specs,
        out_specs=out_specs,
        aliases=aliases,
        flops=scores * 512,
        exps=scores,
    )


def with_terms(q, g):
    return jnp.concatenate([q[:HEAD], q[HEAD:] + g[HEAD:]], axis=0)


def query_grad_kernel(heads, q, g, k, v, out_in, out):
    @pl.when(pl.program_id(0) == 0)
    def _():
        out[...] = out_in[...]

    rows = HEAD + AUX
    each = range(heads)
    terms = [g[h * rows : (h + 1) * rows] for h in each]
    probs = [jnp.exp(dot(k[h], with_terms(q[h], terms[h]), TN)) for h in each]
    grads = [(probs[h] * dot(v[h], terms[h], TN)).astype(BF) for h in each]
    for h in each:
        out[h] += dot(k[h, :HEAD, :], grads[h], NN)


def query_grad(q, g, keys, values, heads, width, begin, steps, carried):
    rows = keys.shape[1]
    group = q.shape[2]
    each = pl.BlockSpec((heads, rows, width), lambda i: (0, 0, i + begin))
    scores = heads * group * steps * width
    return call(
        functools.partial(query_grad_kernel, heads),
        "query_grad",
        [q, g, keys, values, carried],
        [struct((heads, HEAD, group), F32)],
        specs=[whole(q.shape), whole(g.shape), each, each, whole(carried.shape)],
        grid=(steps,),
        flops=scores * 768,
        exps=scores,
    )[0]


def key_grad_kernel(heads, count, step, carried, slots, *refs):
    pieces, (q, k, v), refs = refs[:count], refs[count : count + 3], refs[count + 3 :]
    rows = HEAD + AUX
    each = range(heads)
    if carried:
        dk_in, dv_in = refs[:2]
        refs = refs[2:]
    dk, dv, norms = refs

    def of(h):
        if count == 1:
            return pieces[0][h * rows : (h + 1) * rows]
        lanes = [slice(i, i + step) for i in range(0, pieces[0].shape[1], step)]
        return jnp.concatenate([p[h * rows : (h + 1) * rows, n] for n in lanes for p in pieces], axis=1)

    terms = [of(h) for h in each]
    probs = [jnp.exp(dot(with_terms(q[h], terms[h]), k[h], TN)) for h in each]
    grads = [(probs[h] * dot(terms[h], v[h], TN)).astype(BF) for h in each]
    for h in each:
        value = dot(terms[h][:HEAD], probs[h].astype(BF), NN)
        key = dot(q[h, :HEAD, :], grads[h], NN)
        dv[h] = dv_in[h] + value if carried else value
        dk[h] = dk_in[h] + key if carried else key
    for i in range(norms.shape[0]):
        norms[i] = pieces[i][heads * rows : heads * rows + NORM_ROWS, :NORM_LANES].astype(F32)


NORM_LANES = 256


def key_grad(pieces, chunks, step, slots, q, keys, values, heads, group, sums=()):
    width = sum(p.shape[1] for p in pieces)
    rows = HEAD + AUX
    own = pl.BlockSpec((heads, rows, group), lambda i, s: (0, 0, s[1]))
    specs = [whole(p.shape) for p in pieces]
    specs += [pl.BlockSpec((heads, rows, width), lambda i, s: (0, 0, s[0])), own, own]
    specs += [whole(s.shape) for s in sums]
    scores = heads * group * width
    return call(
        functools.partial(key_grad_kernel, heads, len(pieces), step, bool(sums)),
        "key_grad",
        [*pieces, q, keys, values, *sums],
        [struct((heads, HEAD, group), F32)] * 2 + [struct((chunks, NORM_ROWS, NORM_LANES), F32)],
        prefetch=[slots],
        specs=specs,
        flops=scores * 1024,
        exps=scores,
    )


def norm_parts(values):
    centered = values - jnp.mean(values, axis=-1, keepdims=True)
    inverse = lax.rsqrt(jnp.mean(centered * centered, axis=-1, keepdims=True) + NORM_EPS)
    return centered * inverse, inverse


def norm_back(grad_out, normed, inverse, gain):
    scaled = grad_out * gain
    grad_in = inverse * (
        scaled
        - jnp.mean(scaled, axis=-1, keepdims=True)
        - normed * jnp.mean(scaled * normed, axis=-1, keepdims=True)
    )
    sums = [jnp.sum(grad_out * normed, axis=0, keepdims=True), jnp.sum(grad_out, axis=0, keepdims=True)]
    return grad_in, sums


def col_total(near, other, last):
    own = last.shape[0]
    return near[:own].astype(F32) + other[:own].astype(F32) + last[...].astype(F32)


def first_norm_kernel(near, other, last, tokens, gain, bias, residual, hidden):
    value = tokens[...].astype(F32) + col_total(near, other, last)
    residual[...] = value
    normed, _ = norm_parts(value)
    hidden[...] = (normed * gain[...] + bias[...]).astype(BF)


def second_norm_kernel(near, other, last, residual, gain1, bias1, gain2, bias2, cotangent, result, grad, grad_bf, sums):
    hidden = norm_parts(residual[...])[0] * gain1[...] + bias1[...]
    normed, inverse = norm_parts(hidden + col_total(near, other, last))
    result[...] = (normed * gain2[...] + bias2[...]).astype(BF)
    value, (dgain, dbias) = norm_back(cotangent[...].astype(F32), normed, inverse, gain2[...])
    grad[...] = value
    grad_bf[...] = value.astype(BF)
    sums[0:1] = dgain
    sums[1:2] = dbias


def first_norm_back_kernel(near, other, last, residual, gain, grad2, sums2, grad, package):
    normed, inverse = norm_parts(residual[...])
    grad_out = grad2[...] + col_total(near, other, last)
    value, (dgain, dbias) = norm_back(grad_out, normed, inverse, gain[...])
    grad[...] = value
    own = value.shape[0]
    package[:own] = value.astype(BF)
    sums = jnp.concatenate([dgain, dbias, sums2[0:1], sums2[1:2]], axis=0)
    high = sums.astype(BF)
    low = (sums - high.astype(F32)).astype(BF)
    blank = jnp.zeros((8, sums.shape[1]), F32)
    package[own:] = jnp.concatenate([high.astype(F32), low.astype(F32), blank], axis=0).astype(BF)


def stacked(refs, rows):
    return jnp.concatenate([r[:rows] for r in refs], axis=0)


def forward_kernel(count, units, starts, *refs):
    pieces, hidden, (gu, dn, gate_up, inner, near, far) = refs[:count], refs[count:-6], refs[-6:]
    for i, piece in enumerate(pieces):
        rows = pl.ds(pl.multiple_of(starts[i], 16), piece.shape[0])
        gu[rows, :] = piece[:, : 2 * units]
        dn[rows, :] = piece[:, 2 * units :]
    pairs = len(hidden) // 2
    for out, part in ((near, hidden[:pairs]), (far, hidden[pairs:])):
        x = stacked(part, part[0].shape[0])
        size = x.shape[0]
        begin = 0 if out is near else size
        both = dot(x, gu[...], NN)
        gate_up[begin : begin + size] = both
        up, gate = both[:, :units], both[:, units:]
        value = (gate * jax.nn.sigmoid(gate) * up).astype(BF)
        inner[begin : begin + size] = value
        out[...] = dot(value, dn[...], NT).astype(BF)


def backward_kernel(units, *refs):
    pieces, (gu, dn, gate_up, grads, near, far) = refs[:-6], refs[-6:]
    pairs = len(pieces) // 2
    for out, part in ((near, pieces[:pairs]), (far, pieces[pairs:])):
        g = stacked(part, part[0].shape[0])
        size = g.shape[0]
        begin = 0 if out is near else size
        grad_inner = dot(g, dn[...], NN)
        up = gate_up[begin : begin + size, :units]
        gate = gate_up[begin : begin + size, units:]
        sigma = jax.nn.sigmoid(gate)
        grads[begin : begin + size, :units] = (grad_inner * gate * sigma).astype(BF)
        grads[begin : begin + size, units:] = (
            grad_inner * up * sigma * (1.0 + gate * (1.0 - sigma))
        ).astype(BF)
        out[...] = dot(grads[begin : begin + size], gu[...], NT).astype(BF)


def write_blocks(held, starts, outs):
    for i, out in enumerate(outs):
        out[...] = held[pl.ds(pl.multiple_of(starts[i], 16), out.shape[0]), :]


def block_structs(features, width, ring):
    if not ring:
        return [struct((features, width), BF)]
    share = features // len(CYCLE)
    sizes = [share] * 4 + [share // 2] * 2 + [share] * 3
    return [struct((n, width), BF) for n in sizes]


def ffn_grad_kernel(units, n_blocks, starts, *refs):
    hidden, g, (grads, inner) = refs[:4], refs[4:8], refs[8:10]
    outs, held = refs[10 : 10 + n_blocks], refs[10 + n_blocks]
    own = hidden[0].shape[0]
    turned = stacked(hidden, own).T
    for t in range(0, 2 * units, units):
        held[:, t : t + units] = dot(turned, grads[:, t : t + units], NN).astype(BF)
    held[:, 2 * units :] = dot(stacked(g, own).T, inner[...], NN).astype(BF)
    write_blocks(held, starts, outs)


def prepare_kernel(heads, own, *refs):
    pieces, (w_out, context, log_total, package) = refs[:4], refs[4:]
    g = stacked(pieces, own)
    rows = HEAD + AUX
    grad = dot(w_out[...], g, NT).astype(BF)
    index = lax.broadcasted_iota(jnp.int32, (AUX, g.shape[0]), 0)
    for h in range(heads):
        part = grad[h * HEAD : (h + 1) * HEAD]
        package[h * rows : h * rows + HEAD] = part
        delta = jnp.sum(part.astype(F32) * context[h], axis=0, keepdims=True)
        tail = jnp.zeros(index.shape, F32)
        for at, value in ((8, -log_total[h : h + 1]), (11, -delta)):
            for j in range(3):
                high = value.astype(BF).astype(F32)
                tail = jnp.where(index == at + j, high, tail)
                value = value - high
        package[h * rows + HEAD : (h + 1) * rows] = tail.astype(BF)

    def sums(piece):
        both = piece[own : own + 16].astype(F32)
        return both[:4] + both[4:8]

    total = (sums(pieces[0]) + sums(pieces[1])) + (sums(pieces[2]) + sums(pieces[3]))
    high = total.astype(BF).astype(F32)
    both = jnp.concatenate([high, total - high], axis=0)
    base = heads * rows
    package[base:, NORM_LANES:] = jnp.zeros((package.shape[0] - base, package.shape[1] - NORM_LANES), BF)
    parts = [both[:, i * NORM_LANES : (i + 1) * NORM_LANES] for i in range(both.shape[1] // NORM_LANES)]
    parts.append(jnp.zeros((package.shape[0] - base - 8 * len(parts), NORM_LANES), F32))
    package[base:, :NORM_LANES] = jnp.concatenate(parts, axis=0).astype(BF)


def turn_back(first, second, cosine, sine):
    return jnp.concatenate([first * cosine + second * sine, second * cosine - first * sine], axis=0)


def early_grad_kernel(heads, own, n_x, slots, *refs):
    x_refs, g_refs, refs = refs[:n_x], refs[n_x : n_x + 4], refs[n_x + 4 :]
    grad_query, turn, context, mixed, held = refs
    half = HEAD // 2
    scale = 1.0 / math.sqrt(HEAD)
    for h in range(heads):
        value = grad_query[h] * scale
        mixed[h * HEAD : (h + 1) * HEAD] = turn_back(value[:half], value[half:], turn[:half], turn[half:]).astype(BF)
    x = stacked(x_refs, x_refs[0].shape[0])
    width = heads * HEAD
    held[:, :width] = dot(mixed[...], x, NN).T.astype(BF)
    held[:, width:] = dot(context[...], stacked(g_refs, own), NN).T.astype(BF)


def late_grad_kernel(heads, n_x, n_blocks, slots, starts, *refs):
    x_refs, refs = refs[:n_x], refs[n_x:]
    mixed_q, grad_key, grad_value, early, turn, weight, near, far, *refs = refs
    outs, held, mixed = refs[:n_blocks], refs[n_blocks], refs[n_blocks + 1]
    half = HEAD // 2
    width = heads * HEAD
    mixed[:width] = mixed_q[...]
    for h in range(heads):
        value = grad_key[h]
        mixed[width + h * HEAD : width + (h + 1) * HEAD] = turn_back(
            value[:half], value[half:], turn[:half], turn[half:]
        ).astype(BF)
        mixed[2 * width + h * HEAD : 2 * width + (h + 1) * HEAD] = grad_value[h].astype(BF)
    back = dot(mixed[...], weight[...], TN)
    size = near.shape[0]
    near[...] = back[:size].astype(BF)
    far[...] = back[size:].astype(BF)
    x = stacked(x_refs, x_refs[0].shape[0])
    held[:, : 2 * width] = early[...]
    held[:, 2 * width :] = dot(mixed[width:], x, NN).T.astype(BF)
    write_blocks(held, starts, outs)


NORM_ROWS = 24


def norm_total_kernel(rows, *refs):
    pieces, (out, held) = refs[:-2], refs[-2:]
    at = 0
    for piece in pieces:
        for i in range(piece.shape[0]):
            held[rows[at]] = piece[i]
            at += 1
    total = held[0]
    for r in range(1, at):
        total = total + held[r]
    for i in range(NORM_ROWS // 8):
        part = total[8 * i : 8 * i + 8]
        out[:, i * NORM_LANES : (i + 1) * NORM_LANES] = part[:4] + part[4:]


def slot_tables(seq_lengths, packed_order, wanted, local, waits):
    blocks = packed_order.reshape(-1, local)
    index = jnp.arange(blocks.shape[0], dtype=jnp.int32)
    slots = jnp.sum(
        jnp.where(wanted[:, None, None] == index[None, :, None], blocks[None], 0), axis=1
    ).reshape(1, -1)
    count = seq_lengths.shape[0]
    seq = jnp.zeros_like(slots)
    start = jnp.zeros_like(slots)
    end = jnp.int32(0)
    for s in range(count):
        end = end + seq_lengths[s]
        passed = slots >= end
        seq = seq + passed.astype(jnp.int32)
        start = jnp.where(passed, end, start)
    positions = after((slots - start).astype(F32), waits[0])
    half = HEAD // 2
    freqs = ROPE_BASE ** (-jnp.arange(half, dtype=F32) * 2.0 / HEAD)
    angles = positions * freqs[:, None]
    turn = jnp.concatenate([jnp.cos(angles), jnp.sin(angles)], axis=0)
    line = jnp.arange(3 * AUX, dtype=jnp.int32)[:, None]
    member = lax.rem(line, AUX) == after(seq, waits[1])
    ones = ((line >= 8) & (line < 11)) | ((line >= 2 * AUX + 11) & (line < 2 * AUX + 14))
    marks = jnp.where(ones, 1.0, 0.0)
    marks = jnp.where((line < 8) & member, 1.0, marks)
    marks = jnp.where((line >= AUX) & (line < AUX + 8) & ~member, FAR, marks)
    return turn, marks.astype(BF)


def local(
    tokens,
    w_qkv,
    w_out,
    w_gate_up,
    w_down,
    gain1,
    bias1,
    gain2,
    bias2,
    cotangent,
    seq_lengths,
    packed_order,
):
    rows = lax.axis_size("row")
    row, col = lax.axis_index("row"), lax.axis_index("col")
    ring = rows == len(CYCLE)
    own, features = tokens.shape
    group = own * lax.axis_size("col")
    total = group * rows
    share = w_qkv.shape[0]
    width = w_qkv.shape[2]
    heads = width // HEAD
    units = w_gate_up.shape[2]
    gains = [v.reshape(1, features) for v in (gain1, bias1, gain2, bias2)]

    early = jnp.concatenate([w_qkv.reshape(share, 3 * width), w_out.T], axis=1)
    late = jnp.concatenate([w_gate_up.reshape(share, 2 * units), w_down.T], axis=1)

    pair = jnp.concatenate([tokens, col_swap(tokens, 2)], axis=0)
    if ring:
        place = cycle_place()
        half = share // 2
        starts = cycle_rows(place, (0, *ROUND_STEPS)) * share + jnp.array([0] * 8 + [half], jnp.int32)
        block_starts = cycle_rows(place, BLOCK_STEPS) * share + jnp.array([0] * 5 + [half] + [0] * 3, jnp.int32)
        layout = [(ROUND_STEPS[2 * i + j], o) for i in range(3) for o in OFFSETS for j in range(2)]
        layout += [(step, o) for step in (0, 4) for o in OFFSETS]
        wanted = cycle_rows(place, [step for step, _ in layout]) * len(OFFSETS)
        wanted = wanted + (col ^ jnp.array([o for _, o in layout], jnp.int32))
        token_half = own // 2
        ring_early = Rounds(
            jnp.concatenate(
                [early[:half], tokens[:token_half], early[half:], tokens[token_half:]], axis=0
            ),
            0,
        )
        waits = [ring_early.step(), ring_early.step()]
        ring_early.step()
        ring_early.step()
        packed_order = after(packed_order, waits[0])

        def token_rows(v):
            step = half + token_half
            return [v[i + half : i + step] for i in range(0, v.shape[0], step)]

    else:
        starts = block_starts = jnp.zeros((1,), jnp.int32)
        wanted = jnp.arange(rows, dtype=jnp.int32)[:, None] * len(OFFSETS)
        wanted = (wanted + (col ^ jnp.array(OFFSETS, jnp.int32))[None, :]).reshape(-1)
        waits = (), ()
        early_full = lax.all_gather(early, "row", axis=0, tiled=True)
        w_mix, full_out = assemble([early_full], [[(0, features, 0)]], starts, 3 * width)

    turn, marks = slot_tables(seq_lengths, packed_order, wanted, own, waits)
    if ring:
        cuts = [[(0, half, 0), (half + token_half, half, half)]] * 7 + [[(0, half, 0)]] * 2
        w_mix, full_out = assemble([ring_early.block, *ring_early.pieces()], cuts, starts, 3 * width)
    fixed = (w_mix, turn, marks, heads, total, group)
    if ring:
        pair = after(pair, ring_early.done[3])
    x_pieces = [pair, col_swap(pair, 1)]

    def at(slot):
        return jnp.asarray(slot, jnp.int32).reshape(1)

    own_slot = at(6) if ring else at(row)
    keys, values, queries, own_q, *state = attend("first", x_pieces, own_slot, *fixed)
    if ring:
        late_ring = Rounds(late, 0)
        rounds = ring_early.done

        def side(held):
            both = jnp.concatenate([rows for v in held for rows in token_rows(v)], axis=0)
            return jnp.concatenate([both, col_swap(both, 2)], axis=0)

        def middle(i, chunk):
            return attend(
                "middle",
                [chunk, col_swap(chunk, 1)],
                at(i),
                *fixed,
                (own_q, *state, keys, values, queries),
            )

        one = side(rounds[0])
        two = side(after(rounds[1], one))
        three = side(after(rounds[2], two))
        late_ring.step(rounds[2])
        two = after(two, state[0])
        keys, values, queries, *state = middle(0, after(one, rounds[3]))
        far = side(after(rounds[3], three))
        three = after(three, state[0])
        keys, values, queries, *state = middle(1, after(two, late_ring.done[0]))
        late_ring.step()
        far = after(far, state[0])
        keys, values, queries, *state = middle(2, three)
        keys, values, queries, *finished = attend(
            "last",
            [far, col_swap(far, 1)],
            at(7),
            *fixed,
            (own_q, *state, keys, values, queries),
            full_out,
        )
    else:
        blocks = lax.all_gather(jnp.concatenate(x_pieces, axis=0), "row", axis=0, tiled=False)

        def block(i):
            slot = lax.rem(row + i, rows)
            return [lax.dynamic_index_in_dim(blocks, slot, 0, keepdims=False)], at(slot)

        def step(i, carried):
            *state, keys, values, queries = carried
            keys, values, queries, *state = attend(
                "middle", *block(i), *fixed, (own_q, *state, keys, values, queries)
            )
            return (*state, keys, values, queries)

        *state, keys, values, queries = lax.fori_loop(1, rows - 1, step, (*state, keys, values, queries))
        keys, values, queries, *finished = attend(
            "last", *block(rows - 1), *fixed, (own_q, *state, keys, values, queries), full_out
        )
    near, far, context_bf, context, log_total = finished

    if ring:
        near = after(near, late_ring.done[1])
        late_ring.step(near)
    else:
        late_pieces = [lax.all_gather(late, "row", axis=0, tiled=True)]

    part = struct((group // 2, features), BF)
    flat = struct((own, features), F32)
    residual1, hidden = call(
        first_norm_kernel,
        "first_norm",
        [*col_exchange(near, far)[0], tokens, *gains[:2]],
        [flat, struct((own, features), BF)],
    )
    if ring:
        hidden_pieces = col_pieces(hidden, late_ring.done[2])
        late_pieces = [late, *late_ring.pieces()]
    else:
        hidden_pieces = col_pieces(hidden)
    w_gu, w_dn, gate_up, inner, near, far = call(
        functools.partial(forward_kernel, len(late_pieces), units),
        "ffn_forward",
        [*late_pieces, *hidden_pieces],
        [
            struct((features, 2 * units), BF),
            struct((features, units), BF),
            struct((group, 2 * units), F32),
            struct((group, units), BF),
            part,
            part,
        ],
        prefetch=[starts],
        flops=6 * group * features * units,
    )
    result, grad_res2, grad_bf, sums2 = call(
        second_norm_kernel,
        "second_norm",
        [*col_exchange(near, far)[0], residual1, *gains, cotangent],
        [struct((own, features), BF), flat, struct((own, features), BF), struct((8, features), F32)],
    )
    grad_pieces = col_pieces(grad_bf)
    grad_gate_up, near, far = call(
        functools.partial(backward_kernel, units),
        "ffn_backward",
        [*grad_pieces, w_gu, w_dn, gate_up],
        [struct((group, 2 * units), BF), part, part],
        flops=6 * group * features * units,
    )
    exchanged, passed = col_exchange(near, far)
    grad_gate_up = after(grad_gate_up, passed)
    outs = block_structs(features, 3 * units, ring)
    blocks = call(
        functools.partial(ffn_grad_kernel, units, len(outs)),
        "ffn_grad",
        [*hidden_pieces, *grad_pieces, grad_gate_up, inner],
        outs,
        prefetch=[block_starts],
        scratch=[pltpu.VMEM((features, 3 * units), BF)],
        flops=6 * group * features * units,
    )
    residual1 = after(residual1, blocks)
    ffn_sum = RowSum(blocks)
    sent = ffn_sum.step()
    grad_res1, package = call(
        first_norm_back_kernel,
        "first_norm_back",
        [*exchanged, residual1, gains[0], grad_res2, sums2],
        [flat, struct((own + 16, features), BF)],
    )
    attn_pieces = col_pieces(package)
    (package,) = call(
        functools.partial(prepare_kernel, heads, own),
        "prepare",
        [*attn_pieces, full_out, context, log_total],
        [struct((heads * (HEAD + AUX) + 32, group), BF)],
        flops=2 * width * features * group,
    )
    span = min(2 * group, total)
    steps_all = total // span
    grad_query = jnp.zeros((heads, HEAD, group), F32)
    if ring:
        package_ring = Rounds(package, 1)
        package_ring.step()
        grad_query = after(grad_query, sent)
        ffn_sum.step()
    grad_query = query_grad(own_q, package, keys, values, heads, span, 0, steps_all, grad_query)
    own_turn = pl.BlockSpec((HEAD, group), lambda i, s, *_: (0, s[0]))
    args = [*x_pieces, *attn_pieces, grad_query, turn, context_bf]
    specs = [whole(a.shape) for a in args]
    specs[-2] = own_turn
    mixed_q, early_grad = call(
        functools.partial(early_grad_kernel, heads, own, len(x_pieces)),
        "early_grad",
        args,
        [struct((width, group), BF), struct((features, 2 * width), BF)],
        prefetch=[own_slot],
        specs=specs,
        flops=4 * width * features * group,
    )

    def key_step(pieces, chunks, slot, sums):
        slots = jnp.where(jnp.arange(2) == 0, at(slot), own_slot)
        step = own if chunks == 2 else pieces[0].shape[1]
        *sums, norms = key_grad(
            pieces, chunks, step, slots, queries, keys, values, heads, group, tuple(sums)
        )
        return sums, norms

    norm_out = struct((4, features), F32)
    if ring:
        package_ring.step(early_grad)
        sums, norms = key_step([after(package, early_grad, package_ring.done[0])], 1, 6, ())
        norm_pieces = [norms]
        for i in range(3):
            sums, norms = key_step(package_ring.done[i], 2, i, sums)
            norm_pieces.append(norms)
            if i < 2:
                package_ring.step(norms)
        ffn_sum.moving = after(ffn_sum.moving, norms)
        sums, norms = key_step(package_ring.done[3], 1, 7, sums)
        norm_pieces.append(norms)
        (norm_sums,) = call(
            norm_total_kernel,
            "norm_total",
            norm_pieces,
            [norm_out],
            prefetch=[cycle_rows(place, (0, *ROUND_STEPS[:7]))],
            scratch=[pltpu.VMEM((rows, NORM_ROWS, NORM_LANES), F32)],
        )
    else:
        packages = lax.all_gather(package, "row", axis=0, tiled=False)

        def step(i, carried):
            sums, norms = carried
            piece = lax.dynamic_index_in_dim(packages, i, 0, keepdims=False)
            sums, more = key_step([piece], 1, i, sums)
            return tuple(sums), norms + more

        zeros = jnp.zeros((heads, HEAD, group), F32)
        sums, norms = lax.fori_loop(
            0, rows, step, ((zeros, zeros), jnp.zeros((1, NORM_ROWS, NORM_LANES), F32))
        )
        (norm_sums,) = call(
            norm_total_kernel,
            "norm_total",
            [norms],
            [norm_out],
            prefetch=[jnp.zeros((1,), jnp.int32)],
            scratch=[pltpu.VMEM((1, NORM_ROWS, NORM_LANES), F32)],
        )
    args = [*x_pieces, mixed_q, *sums, early_grad, turn, w_mix]
    specs = [whole(a.shape) for a in args]
    specs[-2] = own_turn
    outs = block_structs(features, 4 * width, ring)
    near, far, *blocks = call(
        functools.partial(late_grad_kernel, heads, len(x_pieces), len(outs)),
        "late_grad",
        args,
        [part, part, *outs],
        prefetch=[own_slot, block_starts],
        scratch=[pltpu.VMEM((features, 4 * width), BF), pltpu.VMEM((3 * width, group), BF)],
        specs=specs,
        flops=10 * width * features * group,
    )
    late_grad = RowSum(blocks).result()
    near, other, last = col_exchange(near, far)[0]
    ffn_grad = ffn_sum.result()
    grad_tokens = grad_res1 + (
        near[:own].astype(F32) + other[:own].astype(F32) + last.astype(F32)
    )
    grad_mix = jnp.concatenate([late_grad[:, :width], late_grad[:, 2 * width :]], axis=1)
    return (
        result,
        grad_tokens,
        grad_mix.reshape(share, 3, width),
        late_grad[:, width : 2 * width].T,
        ffn_grad[:, : 2 * units].reshape(share, 2, units),
        ffn_grad[:, 2 * units :].T,
        norm_sums[0],
        norm_sums[1],
        norm_sums[2],
        norm_sums[3],
    )


def solution(mesh):
    placed = (
        P(("row", "col"), None),
        P("row", None, "col"),
        P("col", "row"),
        P("row", None, "col"),
        P("col", "row"),
        P(),
        P(),
        P(),
        P(),
        P(("row", "col"), None),
        P(),
        P(),
    )
    return jax.shard_map(
        local,
        mesh=mesh,
        in_specs=placed,
        out_specs=(
            P(("row", "col"), None),
            P(("row", "col"), None),
            P("row", None, "col"),
            P("col", "row"),
            P("row", None, "col"),
            P("col", "row"),
            P(),
            P(),
            P(),
            P(),
        ),
        check_vma=False,
    )
```

```python
import functools
import math

import jax
import jax.numpy as jnp
from jax import lax
from jax.experimental import pallas as pl
from jax.experimental.pallas import tpu as pltpu
from jax.sharding import PartitionSpec as P

HEAD = 64
ROPE_BASE = 1000.0
NORM_EPS = 1e-12
FAR = -(2.0**100)
LOWEST = -1e30
AUX = 16
BF = jnp.bfloat16
F32 = jnp.float32

CYCLE = (0, 2, 4, 6, 7, 5, 3, 1)
OFFSETS = (0, 2, 1, 3)


def dot(a, b, contract, out=F32):
    return lax.dot_general(a, b, (contract, ((), ())), preferred_element_type=out)


COST = 0.02

NN = ((1,), (0,))
NT = ((1,), (1,))
TN = ((0,), (0,))


def forward_hop(v):
    n = len(CYCLE)
    return lax.ppermute(v, "row", [(CYCLE[i], CYCLE[(i + 1) % n]) for i in range(n)])


def backward_hop(v):
    n = len(CYCLE)
    return lax.ppermute(v, "row", [(CYCLE[(i + 1) % n], CYCLE[i]) for i in range(n)])


def col_swap(v, mask):
    count = lax.axis_size("col")
    return lax.ppermute(v, "col", [(i, i ^ mask) for i in range(count)])


def cycle_place():
    row = lax.axis_index("row")
    return sum(jnp.where(row == CYCLE[i], i, 0) for i in range(len(CYCLE))).astype(jnp.int32)


def cycle_rows(place, steps):
    places = lax.rem(place + jnp.array([s + len(CYCLE) for s in steps], jnp.int32), len(CYCLE))
    return sum(jnp.where(places == i, CYCLE[i], 0) for i in range(len(CYCLE))).astype(jnp.int32)


def after(value, *first):
    return lax.optimization_barrier((value, first))[0]


class Rounds:
    def __init__(self, block, axis):
        self.block, self.held, self.axis, self.done = block, (block, block), axis, []

    def step(self, *first):
        behind, ahead = after(self.held, first) if first else self.held
        if len(self.done) == 3:
            half = behind.shape[self.axis] // 2
            behind = lax.slice_in_dim(behind, 0, half, axis=self.axis)
            ahead = lax.slice_in_dim(ahead, half, 2 * half, axis=self.axis)
        self.held = forward_hop(behind), backward_hop(ahead)
        self.done.append(self.held)
        return self.held

    def pieces(self):
        while len(self.done) < 4:
            self.step()
        return [p for r in self.done for p in r]


ROUND_STEPS = (-1, 1, -2, 2, -3, 3, 4, 4)
BLOCK_STEPS = (0, 1, 2, 3, 4, 4, 5, 6, 7)


class RowSum:
    def __init__(self, blocks):
        self.blocks, self.hops, self.moving = blocks, 0, None
        if len(blocks) > 1:
            self.moving = blocks[4], blocks[5]

    def step(self):
        if len(self.blocks) == 1:
            return ()
        half = self.blocks[4].shape[0]

        def add(v, block):
            return (v.astype(F32) + block.astype(F32)).astype(BF)

        ahead, back = forward_hop(self.moving[0]), backward_hop(self.moving[1])
        up = (self.blocks[3], self.blocks[2], self.blocks[1], None)[self.hops]
        down = (self.blocks[6], self.blocks[7], self.blocks[8], None)[self.hops]
        if self.hops == 0:
            ahead = jnp.concatenate([add(ahead, up[:half]), up[half:]], axis=0)
            back = jnp.concatenate([down[:half], add(back, down[half:])], axis=0)
        elif up is not None:
            ahead, back = add(ahead, up), add(back, down)
        self.hops += 1
        self.moving = ahead, back
        return self.moving

    def terms(self):
        if len(self.blocks) == 1:
            full = lax.psum_scatter(self.blocks[0].astype(F32), "row", scatter_dimension=0, tiled=True)
            return [full, jnp.zeros_like(full), jnp.zeros_like(full)]
        while self.hops < 4:
            self.step()
        return [self.blocks[0], *self.moving]


def col_pieces(v, *first):
    side = col_swap(v, 2)
    return [v, side, col_swap(v, 1), col_swap(after(side, first), 1)]


def col_exchange(near, far):
    own = near.shape[0] // 2
    other = col_swap(far, 1)
    passed = (near[own:].astype(F32) + other[own:].astype(F32)).astype(BF)
    return (near, other, col_swap(passed, 2)), passed


def whole(shape):
    return pl.BlockSpec(shape, lambda *_: (0,) * len(shape))


ANY = pl.BlockSpec(memory_space=pl.ANY)


def call(kernel, name, args, outs, prefetch=(), scratch=(), specs=None, out_specs=None, aliases=None, grid=(1,), flops=0, exps=0, limit=20, cost=COST):
    args, outs = list(args), list(outs)
    moved = sum(a.size * a.dtype.itemsize for a in args) + sum(
        math.prod(o.shape) * o.dtype.itemsize for o in outs
    )
    return pl.pallas_call(
        kernel,
        grid_spec=pltpu.PrefetchScalarGridSpec(
            num_scalar_prefetch=len(prefetch),
            grid=grid,
            in_specs=specs or [whole(a.shape) for a in args],
            out_specs=out_specs or [whole(o.shape) for o in outs],
            scratch_shapes=list(scratch),
        ),
        out_shape=outs,
        input_output_aliases=aliases or {},
        cost_estimate=pl.CostEstimate(flops=int(flops * cost), bytes_accessed=int(moved * cost), transcendentals=int(exps * cost)),
        compiler_params=pltpu.CompilerParams(vmem_limit_bytes=limit << 20),
        name=name,
    )(*prefetch, *args)


def struct(shape, kind):
    return jax.ShapeDtypeStruct(tuple(shape), kind)


def rows_at(start, count):
    return pl.ds(pl.multiple_of(start, 4), count)


def pack_kernel(parts, weights, w_out, tokens, out):
    early = jnp.concatenate([*(weights[c] for c in range(3)), w_out[...].T], axis=1)
    half, token_half = early.shape[0] // parts, tokens.shape[0] // parts
    for i in range(parts):
        at = i * (half + token_half)
        out[at : at + half] = early[i * half : (i + 1) * half]
        out[at + half : at + half + token_half] = tokens[i * token_half : (i + 1) * token_half]


def assemble_kernel(split, cuts, starts, *refs):
    pieces, (mix, out, held) = refs[:-3], refs[-3:]
    for i, piece in enumerate(pieces):
        for begin, count, shift in cuts[i]:
            held[pl.ds(pl.multiple_of(starts[i] + shift, 16), count), :] = piece[begin : begin + count]
    mix[...] = held[:, :split].T
    out[...] = held[:, split:].T


def assemble(pieces, cuts, starts, split):
    width = pieces[0].shape[1]
    total = sum(c[1] for cut in cuts for c in cut)
    return call(
        functools.partial(assemble_kernel, split, cuts),
        "assemble",
        pieces,
        [struct((split, total), BF), struct((width - split, total), BF)],
        prefetch=[starts],
        scratch=[pltpu.VMEM((total, width), BF)],
    )


def project_into(pieces, weight, turn, marks, q_out, k_out, v_out, heads):
    half = HEAD // 2
    width = heads * HEAD
    begin = 0
    for piece in pieces:
        count = piece.shape[0]
        lanes = slice(begin, begin + count)
        begin += count
        mixed = dot(weight[...], piece[...], NT)
        cosine, sine = turn[:half, lanes], turn[half:, lanes]
        for h in range(heads):
            for base, out, scale, tail in (
                (0, q_out, 1.0 / math.sqrt(HEAD), AUX),
                (width, k_out, None, 0),
            ):
                at = base + h * HEAD
                first, second = mixed[at : at + half], mixed[at + half : at + HEAD]
                turned = jnp.concatenate(
                    [first * cosine - second * sine, second * cosine + first * sine], axis=0
                )
                if scale is not None:
                    turned = turned * scale
                out[h, :HEAD, lanes] = turned.astype(BF)
                out[h, HEAD:, lanes] = marks[tail : tail + AUX, lanes]
            at = 2 * width + h * HEAD
            v_out[h, :HEAD, lanes] = mixed[at : at + HEAD].astype(BF)
            v_out[h, HEAD:, lanes] = marks[2 * AUX : 3 * AUX, lanes]


def attend_kernel(mode, heads, count, slot, *refs):
    pieces, refs = refs[:count], refs[count:]
    weight, turn, marks = refs[:3]
    refs = refs[3:]
    if mode != "first":
        q_own, top_in, sum_in, acc_in = refs[:4]
        refs = refs[7:]
    if mode == "last":
        w_out, refs = refs[0], refs[1:]
    k, v, q = refs[:3]
    refs = refs[3:]
    project_into(pieces, weight, turn, marks, q, k, v, heads)
    if mode == "first":
        q_own, refs = refs[0], refs[1:]
        q_own[...] = q[...]
    if mode == "last":
        near, far, context_bf, context, log_total = refs
    else:
        top, total, acc = refs

    @pl.loop(0, heads)
    def _(h):
        one = pl.ds(h, 1)
        scores = dot(k[h], q_own[h], TN)
        new = jnp.max(scores, axis=0, keepdims=True)
        if mode != "first":
            old = top_in[one, :]
            new = jnp.maximum(old, new)
            keep = jnp.exp(old - new)
        weights = jnp.exp(scores - new)
        count = jnp.sum(weights, axis=0, keepdims=True)
        value = dot(v[h, :HEAD, :], weights.astype(BF), NN)
        if mode != "first":
            count = sum_in[one, :] * keep + count
            value = acc_in[h] * keep + value
        if mode == "last":
            value = value / count
            context[h] = value
            context_bf[pl.ds(pl.multiple_of(h * HEAD, HEAD), HEAD), :] = value.astype(BF)
            log_total[one, :] = new + jnp.log(count)
        else:
            top[one, :] = new
            total[one, :] = count
            acc[h] = value

    if mode == "last":
        attn = dot(context_bf[...], w_out[...], TN)
        half = near.shape[0]
        near[...] = attn[:half].astype(BF)
        far[...] = attn[half:].astype(BF)


def attend(mode, pieces, slot, weight, turn, marks, heads, total, group, carried=(), w_out=None):
    width = sum(p.shape[0] for p in pieces)
    rows = HEAD + AUX

    def lanes(*lead):
        return pl.BlockSpec((*lead, width), lambda i, s: (*(0,) * len(lead), s[0]))

    args = [*pieces, weight, turn, marks, *carried]
    specs = [whole(p.shape) for p in pieces]
    specs += [whole(weight.shape), lanes(turn.shape[0]), lanes(marks.shape[0])]
    buffers = [struct((heads, rows, total), BF)] * 3
    outs, out_specs = list(buffers), [lanes(heads, rows)] * 3
    aliases = {}
    if mode != "first":
        specs += [whole(c.shape) for c in carried[:4]] + [ANY] * 3
        base = 1 + len(pieces) + 3 + 4
        aliases = {base: 0, base + 1: 1, base + 2: 2}
    features = weight.shape[1]
    if mode == "last":
        args.append(w_out)
        specs.append(whole(w_out.shape))
        extra = [
            struct((group // 2, features), BF),
            struct((group // 2, features), BF),
            struct((heads * HEAD, group), BF),
            struct((heads, HEAD, group), F32),
            struct((heads, group), F32),
        ]
    else:
        extra = [
            struct((heads, group), F32),
            struct((heads, group), F32),
            struct((heads, HEAD, group), F32),
        ]
        if mode == "first":
            extra = [struct((heads, rows, group), BF)] + extra
    outs += extra
    out_specs += [whole(e.shape) for e in extra]
    scores = heads * width * group
    return call(
        functools.partial(attend_kernel, mode, heads, len(pieces)),
        "attend",
        args,
        outs,
        prefetch=[slot],
        specs=specs,
        out_specs=out_specs,
        aliases=aliases,
        flops=scores * 512,
        exps=scores,
    )


def with_terms(q, g):
    return jnp.concatenate([q[:HEAD], q[HEAD:] + g[HEAD:]], axis=0)


def query_grad_kernel(heads, q, g, k, v, out_in, out):
    @pl.when(pl.program_id(0) == 0)
    def _():
        out[...] = out_in[...]

    rows = HEAD + AUX

    @pl.loop(0, heads)
    def _(h):
        terms = g[pl.ds(pl.multiple_of(h * rows, 16), rows), :]
        probs = jnp.exp(dot(k[h], with_terms(q[h], terms), TN))
        grads = (probs * dot(v[h], terms, TN)).astype(BF)
        out[h] += dot(k[h, :HEAD, :], grads, NN)


def query_grad(q, g, keys, values, heads, width, begin, steps, carried):
    rows = keys.shape[1]
    group = q.shape[2]
    each = pl.BlockSpec((heads, rows, width), lambda i: (0, 0, i + begin))
    scores = heads * group * steps * width
    return call(
        functools.partial(query_grad_kernel, heads),
        "query_grad",
        [q, g, keys, values, carried],
        [struct((heads, HEAD, group), F32)],
        specs=[whole(q.shape), whole(g.shape), each, each, whole(carried.shape)],
        grid=(steps,),
        flops=scores * 768,
        exps=scores,
    )[0]


def key_grad_kernel(heads, count, step, carried, slots, *refs):
    pieces, (q, k, v), refs = refs[:count], refs[count : count + 3], refs[count + 3 :]
    rows = HEAD + AUX
    if carried:
        dk_in, dv_in = refs[:2]
        refs = refs[2:]
    dk, dv, norms = refs

    @pl.loop(0, heads)
    def _(h):
        mine = pl.ds(pl.multiple_of(h * rows, 16), rows)
        lanes = [slice(i, i + step) for i in range(0, pieces[0].shape[1], step)]
        parts = [p[mine, n] for n in lanes for p in pieces]
        terms = parts[0] if len(parts) == 1 else jnp.concatenate(parts, axis=1)
        probs = jnp.exp(dot(with_terms(q[h], terms), k[h], TN))
        grads = (probs * dot(terms, v[h], TN)).astype(BF)
        value = dot(terms[:HEAD], probs.astype(BF), NN)
        key = dot(q[h, :HEAD, :], grads, NN)
        dv[h] = dv_in[h] + value if carried else value
        dk[h] = dk_in[h] + key if carried else key

    for i in range(norms.shape[0]):
        norms[i] = pieces[i][heads * rows : heads * rows + NORM_ROWS, :NORM_LANES].astype(F32)


NORM_LANES = 256


def key_grad(pieces, chunks, step, slots, q, keys, values, heads, group, sums=()):
    width = sum(p.shape[1] for p in pieces)
    rows = HEAD + AUX
    own = pl.BlockSpec((heads, rows, group), lambda i, s: (0, 0, s[1]))
    specs = [whole(p.shape) for p in pieces]
    specs += [pl.BlockSpec((heads, rows, width), lambda i, s: (0, 0, s[0])), own, own]
    specs += [whole(s.shape) for s in sums]
    scores = heads * group * width
    return call(
        functools.partial(key_grad_kernel, heads, len(pieces), step, bool(sums)),
        "key_grad",
        [*pieces, q, keys, values, *sums],
        [struct((heads, HEAD, group), F32)] * 2 + [struct((chunks, NORM_ROWS, NORM_LANES), F32)],
        prefetch=[slots],
        specs=specs,
        flops=scores * 1024,
        exps=scores,
    )


def norm_parts(values):
    centered = values - jnp.mean(values, axis=-1, keepdims=True)
    inverse = lax.rsqrt(jnp.mean(centered * centered, axis=-1, keepdims=True) + NORM_EPS)
    return centered * inverse, inverse


def norm_back(grad_out, normed, inverse, gain):
    scaled = grad_out * gain
    grad_in = inverse * (
        scaled
        - jnp.mean(scaled, axis=-1, keepdims=True)
        - normed * jnp.mean(scaled * normed, axis=-1, keepdims=True)
    )
    sums = [jnp.sum(grad_out * normed, axis=0, keepdims=True), jnp.sum(grad_out, axis=0, keepdims=True)]
    return grad_in, sums


def col_total(near, other, last):
    own = last.shape[0]
    return near[:own].astype(F32) + other[:own].astype(F32) + last[...].astype(F32)


def first_norm_kernel(near, other, last, tokens, gain, bias, residual, hidden):
    value = tokens[...].astype(F32) + col_total(near, other, last)
    residual[...] = value
    normed, _ = norm_parts(value)
    hidden[...] = (normed * gain[...] + bias[...]).astype(BF)


def second_norm_kernel(near, other, last, residual, gain1, bias1, gain2, bias2, cotangent, result, grad, grad_bf, sums):
    hidden = norm_parts(residual[...])[0] * gain1[...] + bias1[...]
    normed, inverse = norm_parts(hidden + col_total(near, other, last))
    result[...] = (normed * gain2[...] + bias2[...]).astype(BF)
    value, (dgain, dbias) = norm_back(cotangent[...].astype(F32), normed, inverse, gain2[...])
    grad[...] = value
    grad_bf[...] = value.astype(BF)
    sums[0:1] = dgain
    sums[1:2] = dbias


def first_norm_back_kernel(near, other, last, residual, gain, grad2, sums2, grad, package):
    normed, inverse = norm_parts(residual[...])
    grad_out = grad2[...] + col_total(near, other, last)
    value, (dgain, dbias) = norm_back(grad_out, normed, inverse, gain[...])
    grad[...] = value
    own = value.shape[0]
    package[:own] = value.astype(BF)
    sums = jnp.concatenate([dgain, dbias, sums2[0:1], sums2[1:2]], axis=0)
    high = sums.astype(BF)
    low = (sums - high.astype(F32)).astype(BF)
    blank = jnp.zeros((8, sums.shape[1]), F32)
    package[own:] = jnp.concatenate([high.astype(F32), low.astype(F32), blank], axis=0).astype(BF)


def stacked(refs, rows):
    return jnp.concatenate([r[:rows] for r in refs], axis=0)


def forward_kernel(count, units, starts, *refs):
    pieces, hidden, (gu, dn, gate_up, inner, near, far, held) = refs[:count], refs[count:-7], refs[-7:]
    for i, piece in enumerate(pieces):
        rows = pl.ds(pl.multiple_of(starts[i], 16), piece.shape[0])
        gu[rows, :] = piece[:, : 2 * units]
        dn[rows, :] = piece[:, 2 * units :]
    held[...] = stacked(hidden, hidden[0].shape[0])
    size = held.shape[0] // 2

    @pl.loop(0, 2)
    def _(i):
        rows = pl.ds(pl.multiple_of(i * size, 128), size)
        both = dot(held[rows, :], gu[...], NN)
        gate_up[rows, :] = both
        up, gate = both[:, :units], both[:, units:]
        value = (gate * jax.nn.sigmoid(gate) * up).astype(BF)
        inner[rows, :] = value
        part = dot(value, dn[...], NT).astype(BF)
        for j, out in enumerate((near, far)):

            @pl.when(i == j)
            def _():
                out[...] = part


def backward_kernel(units, *refs):
    pieces, (gu, dn, gate_up, grads, near, far, held) = refs[:-7], refs[-7:]
    held[...] = stacked(pieces, pieces[0].shape[0])
    size = held.shape[0] // 2

    @pl.loop(0, 2)
    def _(i):
        rows = pl.ds(pl.multiple_of(i * size, 128), size)
        grad_inner = dot(held[rows, :], dn[...], NN)
        up, gate = gate_up[rows, :units], gate_up[rows, units:]
        sigma = jax.nn.sigmoid(gate)
        grads[rows, :units] = (grad_inner * gate * sigma).astype(BF)
        grads[rows, units:] = (grad_inner * up * sigma * (1.0 + gate * (1.0 - sigma))).astype(BF)
        part = dot(grads[rows, :], gu[...], NT).astype(BF)
        for j, out in enumerate((near, far)):

            @pl.when(i == j)
            def _():
                out[...] = part


def write_blocks(held, starts, outs):
    for i, out in enumerate(outs):
        out[...] = held[pl.ds(pl.multiple_of(starts[i], 16), out.shape[0]), :]


def block_structs(features, width, ring):
    if not ring:
        return [struct((features, width), BF)]
    share = features // len(CYCLE)
    sizes = [share] * 4 + [share // 2] * 2 + [share] * 3
    return [struct((n, width), BF) for n in sizes]


def ffn_grad_kernel(units, n_blocks, starts, *refs):
    hidden, g, (grads, inner) = refs[:4], refs[4:8], refs[8:10]
    outs, held = refs[10 : 10 + n_blocks], refs[10 + n_blocks]
    own = hidden[0].shape[0]
    turned = stacked(hidden, own).T
    for t in range(0, 2 * units, units):
        held[:, t : t + units] = dot(turned, grads[:, t : t + units], NN).astype(BF)
    held[:, 2 * units :] = dot(stacked(g, own).T, inner[...], NN).astype(BF)
    write_blocks(held, starts, outs)


def prepare_kernel(heads, own, *refs):
    pieces, (w_out, context, log_total, package) = refs[:4], refs[4:]
    g = stacked(pieces, own)
    rows = HEAD + AUX
    grad = dot(w_out[...], g, NT).astype(BF)
    index = lax.broadcasted_iota(jnp.int32, (AUX, g.shape[0]), 0)
    for h in range(heads):
        part = grad[h * HEAD : (h + 1) * HEAD]
        package[h * rows : h * rows + HEAD] = part
        delta = jnp.sum(part.astype(F32) * context[h], axis=0, keepdims=True)
        tail = jnp.zeros(index.shape, F32)
        for at, value in ((8, -log_total[h : h + 1]), (11, -delta)):
            for j in range(3):
                high = value.astype(BF).astype(F32)
                tail = jnp.where(index == at + j, high, tail)
                value = value - high
        package[h * rows + HEAD : (h + 1) * rows] = tail.astype(BF)

    def sums(piece):
        both = piece[own : own + 16].astype(F32)
        return both[:4] + both[4:8]

    total = (sums(pieces[0]) + sums(pieces[1])) + (sums(pieces[2]) + sums(pieces[3]))
    high = total.astype(BF).astype(F32)
    both = jnp.concatenate([high, total - high], axis=0)
    base = heads * rows
    package[base:, NORM_LANES:] = jnp.zeros((package.shape[0] - base, package.shape[1] - NORM_LANES), BF)
    parts = [both[:, i * NORM_LANES : (i + 1) * NORM_LANES] for i in range(both.shape[1] // NORM_LANES)]
    parts.append(jnp.zeros((package.shape[0] - base - 8 * len(parts), NORM_LANES), F32))
    package[base:, :NORM_LANES] = jnp.concatenate(parts, axis=0).astype(BF)


def turn_back(first, second, cosine, sine):
    return jnp.concatenate([first * cosine + second * sine, second * cosine - first * sine], axis=0)


def early_grad_kernel(heads, own, n_x, slots, *refs):
    x_refs, g_refs, refs = refs[:n_x], refs[n_x : n_x + 4], refs[n_x + 4 :]
    grad_query, turn, context, mixed, held = refs
    half = HEAD // 2
    scale = 1.0 / math.sqrt(HEAD)
    for h in range(heads):
        value = grad_query[h] * scale
        mixed[h * HEAD : (h + 1) * HEAD] = turn_back(value[:half], value[half:], turn[:half], turn[half:]).astype(BF)
    x = stacked(x_refs, x_refs[0].shape[0])
    width = heads * HEAD
    held[:, :width] = dot(mixed[...], x, NN).T.astype(BF)
    held[:, width:] = dot(context[...], stacked(g_refs, own), NN).T.astype(BF)


def late_grad_kernel(heads, n_x, n_blocks, slots, starts, *refs):
    x_refs, refs = refs[:n_x], refs[n_x:]
    mixed_q, grad_key, grad_value, early, turn, weight, near, far, *refs = refs
    outs, held, mixed = refs[:n_blocks], refs[n_blocks], refs[n_blocks + 1]
    half = HEAD // 2
    width = heads * HEAD
    mixed[:width] = mixed_q[...]
    for h in range(heads):
        value = grad_key[h]
        mixed[width + h * HEAD : width + (h + 1) * HEAD] = turn_back(
            value[:half], value[half:], turn[:half], turn[half:]
        ).astype(BF)
        mixed[2 * width + h * HEAD : 2 * width + (h + 1) * HEAD] = grad_value[h].astype(BF)
    back = dot(mixed[...], weight[...], TN)
    size = near.shape[0]
    near[...] = back[:size].astype(BF)
    far[...] = back[size:].astype(BF)
    x = stacked(x_refs, x_refs[0].shape[0])
    held[:, : 2 * width] = early[...]
    held[:, 2 * width :] = dot(mixed[width:], x, NN).T.astype(BF)
    write_blocks(held, starts, outs)


def finish_ffn_kernel(units, block, ahead, back, gu, dn):
    total = block[...].astype(F32) + ahead[...].astype(F32) + back[...].astype(F32)
    gu[:, 0, :] = total[:, :units]
    gu[:, 1, :] = total[:, units : 2 * units]
    dn[...] = total[:, 2 * units :].T


def finish_mix_kernel(width, block, ahead, back, mix, out):
    total = block[...].astype(F32) + ahead[...].astype(F32) + back[...].astype(F32)
    mix[0] = total[:, :width]
    mix[1] = total[:, 2 * width : 3 * width]
    mix[2] = total[:, 3 * width :]
    out[...] = total[:, width : 2 * width].T


NORM_ROWS = 24


def norm_total_kernel(rows, *refs):
    pieces, (out, held) = refs[:-2], refs[-2:]
    at = 0
    for piece in pieces:
        for i in range(piece.shape[0]):
            held[rows[at]] = piece[i]
            at += 1
    total = held[0]
    for r in range(1, at):
        total = total + held[r]
    for i in range(NORM_ROWS // 8):
        part = total[8 * i : 8 * i + 8]
        out[:, i * NORM_LANES : (i + 1) * NORM_LANES] = part[:4] + part[4:]


def slot_tables(seq_lengths, packed_order, wanted, local, waits):
    blocks = packed_order.reshape(-1, local)
    index = jnp.arange(blocks.shape[0], dtype=jnp.int32)
    slots = jnp.sum(
        jnp.where(wanted[:, None, None] == index[None, :, None], blocks[None], 0), axis=1
    ).reshape(1, -1)
    count = seq_lengths.shape[0]
    seq = jnp.zeros_like(slots)
    start = jnp.zeros_like(slots)
    end = jnp.int32(0)
    for s in range(count):
        end = end + seq_lengths[s]
        passed = slots >= end
        seq = seq + passed.astype(jnp.int32)
        start = jnp.where(passed, end, start)
    positions = after((slots - start).astype(F32), waits[0])
    half = HEAD // 2
    freqs = ROPE_BASE ** (-jnp.arange(half, dtype=F32) * 2.0 / HEAD)
    angles = positions * freqs[:, None]
    turn = jnp.concatenate([jnp.cos(angles), jnp.sin(angles)], axis=0)
    line = jnp.arange(3 * AUX, dtype=jnp.int32)[:, None]
    member = lax.rem(line, AUX) == after(seq, waits[1])
    ones = ((line >= 8) & (line < 11)) | ((line >= 2 * AUX + 11) & (line < 2 * AUX + 14))
    marks = jnp.where(ones, 1.0, 0.0)
    marks = jnp.where((line < 8) & member, 1.0, marks)
    marks = jnp.where((line >= AUX) & (line < AUX + 8) & ~member, FAR, marks)
    return turn, marks.astype(BF)


def local(
    tokens,
    w_qkv,
    w_out,
    w_gate_up,
    w_down,
    gain1,
    bias1,
    gain2,
    bias2,
    cotangent,
    seq_lengths,
    packed_order,
):
    rows = lax.axis_size("row")
    row, col = lax.axis_index("row"), lax.axis_index("col")
    ring = rows == len(CYCLE)
    own, features = tokens.shape
    group = own * lax.axis_size("col")
    total = group * rows
    share = w_qkv.shape[0]
    width = w_qkv.shape[2]
    heads = width // HEAD
    units = w_gate_up.shape[2]
    gains = [v.reshape(1, features) for v in (gain1, bias1, gain2, bias2)]

    early = jnp.concatenate([w_qkv.reshape(share, 3 * width), w_out.T], axis=1)
    late = jnp.concatenate([w_gate_up.reshape(share, 2 * units), w_down.T], axis=1)

    pair = jnp.concatenate([tokens, col_swap(tokens, 2)], axis=0)
    if ring:
        place = cycle_place()
        half = share // 2
        starts = cycle_rows(place, (0, *ROUND_STEPS)) * share + jnp.array([0] * 8 + [half], jnp.int32)
        block_starts = cycle_rows(place, BLOCK_STEPS) * share + jnp.array([0] * 5 + [half] + [0] * 3, jnp.int32)
        layout = [(ROUND_STEPS[2 * i + j], o) for i in range(3) for o in OFFSETS for j in range(2)]
        layout += [(step, o) for step in (0, 4) for o in OFFSETS]
        wanted = cycle_rows(place, [step for step, _ in layout]) * len(OFFSETS)
        wanted = wanted + (col ^ jnp.array([o for _, o in layout], jnp.int32))
        token_half = own // 2
        (packed,) = call(
            functools.partial(pack_kernel, 2),
            "pack",
            [w_qkv.transpose(1, 0, 2), w_out, tokens],
            [struct((share + own, features), BF)],
        )
        ring_early = Rounds(packed, 0)
        waits = [ring_early.step(), ring_early.step()]
        ring_early.step()
        ring_early.step()
        packed_order = after(packed_order, waits[0])

        def token_rows(v):
            step = half + token_half
            return [v[i + half : i + step] for i in range(0, v.shape[0], step)]

    else:
        starts = block_starts = jnp.zeros((1,), jnp.int32)
        wanted = jnp.arange(rows, dtype=jnp.int32)[:, None] * len(OFFSETS)
        wanted = (wanted + (col ^ jnp.array(OFFSETS, jnp.int32))[None, :]).reshape(-1)
        waits = (), ()
        early_full = lax.all_gather(early, "row", axis=0, tiled=True)
        w_mix, full_out = assemble([early_full], [[(0, features, 0)]], starts, 3 * width)

    turn, marks = slot_tables(seq_lengths, packed_order, wanted, own, waits)
    if ring:
        cuts = [[(0, half, 0), (half + token_half, half, half)]] * 7 + [[(0, half, 0)]] * 2
        w_mix, full_out = assemble([ring_early.block, *ring_early.pieces()], cuts, starts, 3 * width)
    fixed = (w_mix, turn, marks, heads, total, group)
    if ring:
        pair = after(pair, ring_early.done[3])
    x_pieces = [pair, col_swap(pair, 1)]

    def at(slot):
        return jnp.asarray(slot, jnp.int32).reshape(1)

    own_slot = at(6) if ring else at(row)
    keys, values, queries, own_q, *state = attend("first", x_pieces, own_slot, *fixed)
    if ring:
        late_ring = Rounds(late, 0)
        rounds = ring_early.done

        def side(held):
            both = jnp.concatenate([rows for v in held for rows in token_rows(v)], axis=0)
            return jnp.concatenate([both, col_swap(both, 2)], axis=0)

        def middle(i, chunk):
            return attend(
                "middle",
                [chunk, col_swap(chunk, 1)],
                at(i),
                *fixed,
                (own_q, *state, keys, values, queries),
            )

        one = side(rounds[0])
        two = side(after(rounds[1], one))
        three = side(after(rounds[2], two))
        late_ring.step(rounds[2])
        two = after(two, state[0])
        keys, values, queries, *state = middle(0, after(one, rounds[3]))
        far = side(after(rounds[3], three))
        three = after(three, state[0])
        keys, values, queries, *state = middle(1, after(two, late_ring.done[0]))
        late_ring.step()
        far = after(far, state[0])
        keys, values, queries, *state = middle(2, three)
        far = after(far, late_ring.done[1])
        keys, values, queries, *finished = attend(
            "last",
            [far, col_swap(far, 1)],
            at(7),
            *fixed,
            (own_q, *state, keys, values, queries),
            full_out,
        )
    else:
        blocks = lax.all_gather(jnp.concatenate(x_pieces, axis=0), "row", axis=0, tiled=False)

        def block(i):
            slot = lax.rem(row + i, rows)
            return [lax.dynamic_index_in_dim(blocks, slot, 0, keepdims=False)], at(slot)

        def step(i, carried):
            *state, keys, values, queries = carried
            keys, values, queries, *state = attend(
                "middle", *block(i), *fixed, (own_q, *state, keys, values, queries)
            )
            return (*state, keys, values, queries)

        *state, keys, values, queries = lax.fori_loop(1, rows - 1, step, (*state, keys, values, queries))
        keys, values, queries, *finished = attend(
            "last", *block(rows - 1), *fixed, (own_q, *state, keys, values, queries), full_out
        )
    near, far, context_bf, context, log_total = finished

    if ring:
        late_ring.step(near)
    else:
        late_pieces = [lax.all_gather(late, "row", axis=0, tiled=True)]

    part = struct((group // 2, features), BF)
    flat = struct((own, features), F32)
    residual1, hidden = call(
        first_norm_kernel,
        "first_norm",
        [*col_exchange(near, far)[0], tokens, *gains[:2]],
        [flat, struct((own, features), BF)],
    )
    if ring:
        hidden_pieces = col_pieces(hidden, late_ring.done[2])
        late_pieces = [late, *late_ring.pieces()]
    else:
        hidden_pieces = col_pieces(hidden)
    w_gu, w_dn, gate_up, inner, near, far = call(
        functools.partial(forward_kernel, len(late_pieces), units),
        "ffn_forward",
        [*late_pieces, *hidden_pieces],
        [
            struct((features, 2 * units), BF),
            struct((features, units), BF),
            struct((group, 2 * units), F32),
            struct((group, units), BF),
            part,
            part,
        ],
        prefetch=[starts],
        scratch=[pltpu.VMEM((group, features), BF)],
        flops=6 * group * features * units,
    )
    result, grad_res2, grad_bf, sums2 = call(
        second_norm_kernel,
        "second_norm",
        [*col_exchange(near, far)[0], residual1, *gains, cotangent],
        [struct((own, features), BF), flat, struct((own, features), BF), struct((8, features), F32)],
    )
    grad_pieces = col_pieces(grad_bf)
    grad_gate_up, near, far = call(
        functools.partial(backward_kernel, units),
        "ffn_backward",
        [*grad_pieces, w_gu, w_dn, gate_up],
        [struct((group, 2 * units), BF), part, part],
        scratch=[pltpu.VMEM((group, features), BF)],
        flops=6 * group * features * units,
    )
    exchanged, passed = col_exchange(near, far)
    grad_gate_up = after(grad_gate_up, passed)
    outs = block_structs(features, 3 * units, ring)
    blocks = call(
        functools.partial(ffn_grad_kernel, units, len(outs)),
        "ffn_grad",
        [*hidden_pieces, *grad_pieces, grad_gate_up, inner],
        outs,
        prefetch=[block_starts],
        scratch=[pltpu.VMEM((features, 3 * units), BF)],
        flops=6 * group * features * units,
    )
    residual1 = after(residual1, blocks)
    ffn_sum = RowSum(blocks)
    sent = ffn_sum.step()
    grad_res1, package = call(
        first_norm_back_kernel,
        "first_norm_back",
        [*exchanged, residual1, gains[0], grad_res2, sums2],
        [flat, struct((own + 16, features), BF)],
    )
    attn_pieces = after(col_pieces(package), sent)
    (package,) = call(
        functools.partial(prepare_kernel, heads, own),
        "prepare",
        [*attn_pieces, full_out, context, log_total],
        [struct((heads * (HEAD + AUX) + 32, group), BF)],
        flops=2 * width * features * group,
    )
    span = min(2 * group, total)
    steps_all = total // span
    grad_query = jnp.zeros((heads, HEAD, group), F32)
    if ring:
        package_ring = Rounds(package, 1)
        package_ring.step()
        sent = ffn_sum.step()
    grad_query = query_grad(own_q, package, keys, values, heads, span, 0, steps_all, grad_query)
    own_turn = pl.BlockSpec((HEAD, group), lambda i, s, *_: (0, s[0]))
    args = [*x_pieces, *attn_pieces, grad_query, turn, context_bf]
    specs = [whole(a.shape) for a in args]
    specs[-2] = own_turn
    mixed_q, early_grad = call(
        functools.partial(early_grad_kernel, heads, own, len(x_pieces)),
        "early_grad",
        args,
        [struct((width, group), BF), struct((features, 2 * width), BF)],
        prefetch=[own_slot],
        specs=specs,
        flops=4 * width * features * group,
    )

    def key_step(pieces, chunks, slot, sums):
        slots = jnp.where(jnp.arange(2) == 0, at(slot), own_slot)
        step = own if chunks == 2 else pieces[0].shape[1]
        *sums, norms = key_grad(
            pieces, chunks, step, slots, queries, keys, values, heads, group, tuple(sums)
        )
        return sums, norms

    norm_out = struct((4, features), F32)
    if ring:
        package_ring.step(early_grad)
        sums, norms = key_step([after(package, early_grad, package_ring.done[0], sent)], 1, 6, ())
        norm_pieces = [norms]
        for i in range(3):
            sums, norms = key_step(package_ring.done[i], 2, i, sums)
            norm_pieces.append(norms)
            if i < 2:
                package_ring.step(norms)
        ffn_sum.moving = after(ffn_sum.moving, norms)
        sums, norms = key_step(package_ring.done[3], 1, 7, sums)
        norm_pieces.append(norms)
        (norm_sums,) = call(
            norm_total_kernel,
            "norm_total",
            norm_pieces,
            [norm_out],
            prefetch=[cycle_rows(place, (0, *ROUND_STEPS[:7]))],
            scratch=[pltpu.VMEM((rows, NORM_ROWS, NORM_LANES), F32)],
        )
    else:
        packages = lax.all_gather(package, "row", axis=0, tiled=False)

        def step(i, carried):
            sums, norms = carried
            piece = lax.dynamic_index_in_dim(packages, i, 0, keepdims=False)
            sums, more = key_step([piece], 1, i, sums)
            return tuple(sums), norms + more

        zeros = jnp.zeros((heads, HEAD, group), F32)
        sums, norms = lax.fori_loop(
            0, rows, step, ((zeros, zeros), jnp.zeros((1, NORM_ROWS, NORM_LANES), F32))
        )
        (norm_sums,) = call(
            norm_total_kernel,
            "norm_total",
            [norms],
            [norm_out],
            prefetch=[jnp.zeros((1,), jnp.int32)],
            scratch=[pltpu.VMEM((1, NORM_ROWS, NORM_LANES), F32)],
        )
    args = [*x_pieces, mixed_q, *sums, early_grad, turn, w_mix]
    specs = [whole(a.shape) for a in args]
    specs[-2] = own_turn
    outs = block_structs(features, 4 * width, ring)
    near, far, *blocks = call(
        functools.partial(late_grad_kernel, heads, len(x_pieces), len(outs)),
        "late_grad",
        args,
        [part, part, *outs],
        prefetch=[own_slot, block_starts],
        scratch=[pltpu.VMEM((features, 4 * width), BF), pltpu.VMEM((3 * width, group), BF)],
        specs=specs,
        flops=10 * width * features * group,
    )
    late_sum = RowSum(blocks)
    late_sum = late_sum.terms()
    near, other, last = col_exchange(near, far)[0]
    grad_gu, grad_dn = call(
        functools.partial(finish_ffn_kernel, units),
        "finish_ffn",
        ffn_sum.terms(),
        [struct((share, 2, units), F32), struct((units, share), F32)],
        cost=20.0,
    )
    grad_tokens = grad_res1 + (
        near[:own].astype(F32) + other[:own].astype(F32) + last.astype(F32)
    )
    grad_mix, grad_out = call(
        functools.partial(finish_mix_kernel, width),
        "finish_mix",
        late_sum,
        [struct((3, share, width), F32), struct((width, share), F32)],
        cost=20.0,
    )
    return (
        result,
        grad_tokens,
        grad_mix.transpose(1, 0, 2),
        grad_out,
        grad_gu,
        grad_dn,
        norm_sums[0],
        norm_sums[1],
        norm_sums[2],
        norm_sums[3],
    )


def solution(mesh):
    placed = (
        P(("row", "col"), None),
        P("row", None, "col"),
        P("col", "row"),
        P("row", None, "col"),
        P("col", "row"),
        P(),
        P(),
        P(),
        P(),
        P(("row", "col"), None),
        P(),
        P(),
    )
    return jax.shard_map(
        local,
        mesh=mesh,
        in_specs=placed,
        out_specs=(
            P(("row", "col"), None),
            P(("row", "col"), None),
            P("row", None, "col"),
            P("col", "row"),
            P("row", None, "col"),
            P("col", "row"),
            P(),
            P(),
            P(),
            P(),
        ),
        check_vma=False,
    )
```

```python
import functools
import math

import jax
import jax.numpy as jnp
from jax import lax
from jax.experimental import pallas as pl
from jax.experimental.pallas import tpu as pltpu
from jax.sharding import PartitionSpec as P

HEAD = 64
ROPE_BASE = 1000.0
NORM_EPS = 1e-12
FAR = -(2.0**100)
LOWEST = -1e30
AUX = 16
BF = jnp.bfloat16
F32 = jnp.float32

CYCLE = (0, 2, 4, 6, 7, 5, 3, 1)
OFFSETS = (0, 2, 1, 3)


def dot(a, b, contract, out=F32):
    return lax.dot_general(a, b, (contract, ((), ())), preferred_element_type=out)


COST = 0.02

NN = ((1,), (0,))
NT = ((1,), (1,))
TN = ((0,), (0,))


def forward_hop(v):
    n = len(CYCLE)
    return lax.ppermute(v, "row", [(CYCLE[i], CYCLE[(i + 1) % n]) for i in range(n)])


def backward_hop(v):
    n = len(CYCLE)
    return lax.ppermute(v, "row", [(CYCLE[(i + 1) % n], CYCLE[i]) for i in range(n)])


def col_swap(v, mask):
    count = lax.axis_size("col")
    return lax.ppermute(v, "col", [(i, i ^ mask) for i in range(count)])


def cycle_place():
    row = lax.axis_index("row")
    return sum(jnp.where(row == CYCLE[i], i, 0) for i in range(len(CYCLE))).astype(jnp.int32)


def cycle_rows(place, steps):
    places = lax.rem(place + jnp.array([s + len(CYCLE) for s in steps], jnp.int32), len(CYCLE))
    return sum(jnp.where(places == i, CYCLE[i], 0) for i in range(len(CYCLE))).astype(jnp.int32)


def after(value, *first):
    return lax.optimization_barrier((value, first))[0]


class Rounds:
    def __init__(self, block, axis):
        self.block, self.held, self.axis, self.done = block, (block, block), axis, []

    def step(self, *first):
        behind, ahead = after(self.held, first) if first else self.held
        if len(self.done) == 3:
            half = behind.shape[self.axis] // 2
            behind = lax.slice_in_dim(behind, 0, half, axis=self.axis)
            ahead = lax.slice_in_dim(ahead, half, 2 * half, axis=self.axis)
        self.held = forward_hop(behind), backward_hop(ahead)
        self.done.append(self.held)
        return self.held

    def pieces(self):
        while len(self.done) < 4:
            self.step()
        return [p for r in self.done for p in r]


ROUND_STEPS = (-1, 1, -2, 2, -3, 3, 4, 4)
BLOCK_STEPS = (0, 1, 2, 3, 4, 4, 5, 6, 7)


class RowSum:
    def __init__(self, blocks):
        self.blocks, self.hops, self.moving = blocks, 0, None
        if len(blocks) > 1:
            self.moving = blocks[4], blocks[5]

    def step(self):
        if len(self.blocks) == 1:
            return ()
        half = self.blocks[4].shape[0]

        def add(v, block):
            return (v.astype(F32) + block.astype(F32)).astype(BF)

        ahead, back = forward_hop(self.moving[0]), backward_hop(self.moving[1])
        up = (self.blocks[3], self.blocks[2], self.blocks[1], None)[self.hops]
        down = (self.blocks[6], self.blocks[7], self.blocks[8], None)[self.hops]
        if self.hops == 0:
            ahead = jnp.concatenate([add(ahead, up[:half]), up[half:]], axis=0)
            back = jnp.concatenate([down[:half], add(back, down[half:])], axis=0)
        elif up is not None:
            ahead, back = add(ahead, up), add(back, down)
        self.hops += 1
        self.moving = ahead, back
        return self.moving

    def terms(self):
        if len(self.blocks) == 1:
            full = lax.psum_scatter(self.blocks[0].astype(F32), "row", scatter_dimension=0, tiled=True)
            return [full, jnp.zeros_like(full), jnp.zeros_like(full)]
        while self.hops < 4:
            self.step()
        return [self.blocks[0], *self.moving]


def core_sum(near, far):
    return (near.astype(F32) + col_swap(far, 1).astype(F32)).astype(BF)


def col_exchange(near, far):
    mine = core_sum(near, far)
    return [mine, col_swap(mine, 2)]


def col_sum(near, far):
    mine = core_sum(near, far)
    own = mine.shape[0] // 2
    return mine[:own].astype(F32) + col_swap(mine[own:], 2).astype(F32)


def whole(shape):
    return pl.BlockSpec(shape, lambda *_: (0,) * len(shape))


ANY = pl.BlockSpec(memory_space=pl.ANY)


def call(kernel, name, args, outs, prefetch=(), scratch=(), specs=None, out_specs=None, aliases=None, grid=(1,), flops=0, exps=0, limit=20, cost=COST):
    args, outs = list(args), list(outs)
    moved = sum(a.size * a.dtype.itemsize for a in args) + sum(
        math.prod(o.shape) * o.dtype.itemsize for o in outs
    )
    return pl.pallas_call(
        kernel,
        grid_spec=pltpu.PrefetchScalarGridSpec(
            num_scalar_prefetch=len(prefetch),
            grid=grid,
            in_specs=specs or [whole(a.shape) for a in args],
            out_specs=out_specs or [whole(o.shape) for o in outs],
            scratch_shapes=list(scratch),
        ),
        out_shape=outs,
        input_output_aliases=aliases or {},
        cost_estimate=pl.CostEstimate(flops=int(flops * cost), bytes_accessed=int(moved * cost), transcendentals=int(exps * cost)),
        compiler_params=pltpu.CompilerParams(vmem_limit_bytes=limit << 20),
        name=name,
    )(*prefetch, *args)


def struct(shape, kind):
    return jax.ShapeDtypeStruct(tuple(shape), kind)


def rows_at(start, count):
    return pl.ds(pl.multiple_of(start, 4), count)


def pack_kernel(parts, weights, w_out, tokens, out):
    early = jnp.concatenate([*(weights[c] for c in range(3)), w_out[...].T], axis=1)
    half, token_half = early.shape[0] // parts, tokens.shape[0] // parts
    for i in range(parts):
        at = i * (half + token_half)
        out[at : at + half] = early[i * half : (i + 1) * half]
        out[at + half : at + half + token_half] = tokens[i * token_half : (i + 1) * token_half]


def assemble_kernel(split, cuts, starts, *refs):
    pieces, (mix, out, held) = refs[:-3], refs[-3:]
    for i, piece in enumerate(pieces):
        for begin, count, shift in cuts[i]:
            held[pl.ds(pl.multiple_of(starts[i] + shift, 16), count), :] = piece[begin : begin + count]
    mix[...] = held[:, :split].T
    out[...] = held[:, split:].T


def assemble(pieces, cuts, starts, split):
    width = pieces[0].shape[1]
    total = sum(c[1] for cut in cuts for c in cut)
    return call(
        functools.partial(assemble_kernel, split, cuts),
        "assemble",
        pieces,
        [struct((split, total), BF), struct((width - split, total), BF)],
        prefetch=[starts],
        scratch=[pltpu.VMEM((total, width), BF)],
    )


def project_into(pieces, weight, turn, marks, q_out, k_out, v_out, heads):
    half = HEAD // 2
    width = heads * HEAD
    begin = 0
    for piece in pieces:
        count = piece.shape[0]
        lanes = slice(begin, begin + count)
        begin += count
        mixed = dot(weight[...], piece[...], NT)
        cosine, sine = turn[:half, lanes], turn[half:, lanes]
        for h in range(heads):
            for base, out, scale, tail in (
                (0, q_out, 1.0 / math.sqrt(HEAD), AUX),
                (width, k_out, None, 0),
            ):
                at = base + h * HEAD
                first, second = mixed[at : at + half], mixed[at + half : at + HEAD]
                turned = jnp.concatenate(
                    [first * cosine - second * sine, second * cosine + first * sine], axis=0
                )
                if scale is not None:
                    turned = turned * scale
                out[h, :HEAD, lanes] = turned.astype(BF)
                out[h, HEAD:, lanes] = marks[tail : tail + AUX, lanes]
            at = 2 * width + h * HEAD
            v_out[h, :HEAD, lanes] = mixed[at : at + HEAD].astype(BF)
            v_out[h, HEAD:, lanes] = marks[2 * AUX : 3 * AUX, lanes]


def attend_kernel(mode, heads, count, slot, *refs):
    pieces, refs = refs[:count], refs[count:]
    weight, turn, marks = refs[:3]
    refs = refs[3:]
    if mode != "first":
        q_own, top_in, sum_in, acc_in = refs[:4]
        refs = refs[7:]
    if mode == "last":
        w_out, refs = refs[0], refs[1:]
    k, v, q = refs[:3]
    refs = refs[3:]
    project_into(pieces, weight, turn, marks, q, k, v, heads)
    if mode == "first":
        q_own, refs = refs[0], refs[1:]
        q_own[...] = q[...]
    if mode == "last":
        near, far, context_bf, context, log_total = refs
    else:
        top, total, acc = refs

    @pl.loop(0, heads)
    def _(h):
        one = pl.ds(h, 1)
        scores = dot(k[h], q_own[h], TN)
        new = jnp.max(scores, axis=0, keepdims=True)
        if mode != "first":
            old = top_in[one, :]
            new = jnp.maximum(old, new)
            keep = jnp.exp(old - new)
        weights = jnp.exp(scores - new)
        count = jnp.sum(weights, axis=0, keepdims=True)
        value = dot(v[h, :HEAD, :], weights.astype(BF), NN)
        if mode != "first":
            count = sum_in[one, :] * keep + count
            value = acc_in[h] * keep + value
        if mode == "last":
            value = value / count
            context[h] = value
            context_bf[pl.ds(pl.multiple_of(h * HEAD, HEAD), HEAD), :] = value.astype(BF)
            log_total[one, :] = new + jnp.log(count)
        else:
            top[one, :] = new
            total[one, :] = count
            acc[h] = value

    if mode == "last":
        attn = dot(context_bf[...], w_out[...], TN)
        half = near.shape[0]
        near[...] = attn[:half].astype(BF)
        far[...] = attn[half:].astype(BF)


def attend(mode, pieces, slot, weight, turn, marks, heads, total, group, carried=(), w_out=None):
    width = sum(p.shape[0] for p in pieces)
    rows = HEAD + AUX

    def lanes(*lead):
        return pl.BlockSpec((*lead, width), lambda i, s: (*(0,) * len(lead), s[0]))

    args = [*pieces, weight, turn, marks, *carried]
    specs = [whole(p.shape) for p in pieces]
    specs += [whole(weight.shape), lanes(turn.shape[0]), lanes(marks.shape[0])]
    buffers = [struct((heads, rows, total), BF)] * 3
    outs, out_specs = list(buffers), [lanes(heads, rows)] * 3
    aliases = {}
    if mode != "first":
        specs += [whole(c.shape) for c in carried[:4]] + [ANY] * 3
        base = 1 + len(pieces) + 3 + 4
        aliases = {base: 0, base + 1: 1, base + 2: 2}
    features = weight.shape[1]
    if mode == "last":
        args.append(w_out)
        specs.append(whole(w_out.shape))
        extra = [
            struct((group // 2, features), BF),
            struct((group // 2, features), BF),
            struct((heads * HEAD, group), BF),
            struct((heads, HEAD, group), F32),
            struct((heads, group), F32),
        ]
    else:
        extra = [
            struct((heads, group), F32),
            struct((heads, group), F32),
            struct((heads, HEAD, group), F32),
        ]
        if mode == "first":
            extra = [struct((heads, rows, group), BF)] + extra
    outs += extra
    out_specs += [whole(e.shape) for e in extra]
    scores = heads * width * group
    return call(
        functools.partial(attend_kernel, mode, heads, len(pieces)),
        "attend",
        args,
        outs,
        prefetch=[slot],
        specs=specs,
        out_specs=out_specs,
        aliases=aliases,
        flops=scores * 512,
        exps=scores,
    )


def with_terms(q, g):
    return jnp.concatenate([q[:HEAD], q[HEAD:] + g[HEAD:]], axis=0)


def query_grad_kernel(heads, q, g, k, v, out_in, out):
    @pl.when(pl.program_id(0) == 0)
    def _():
        out[...] = out_in[...]

    rows = HEAD + AUX

    @pl.loop(0, heads)
    def _(h):
        terms = g[pl.ds(pl.multiple_of(h * rows, 16), rows), :]
        probs = jnp.exp(dot(k[h], with_terms(q[h], terms), TN))
        grads = (probs * dot(v[h], terms, TN)).astype(BF)
        out[h] += dot(k[h, :HEAD, :], grads, NN)


def query_grad(q, g, keys, values, heads, width, begin, steps, carried):
    rows = keys.shape[1]
    group = q.shape[2]
    each = pl.BlockSpec((heads, rows, width), lambda i: (0, 0, i + begin))
    scores = heads * group * steps * width
    return call(
        functools.partial(query_grad_kernel, heads),
        "query_grad",
        [q, g, keys, values, carried],
        [struct((heads, HEAD, group), F32)],
        specs=[whole(q.shape), whole(g.shape), each, each, whole(carried.shape)],
        grid=(steps,),
        flops=scores * 768,
        exps=scores,
    )[0]


def key_grad_kernel(heads, count, step, carried, slots, *refs):
    pieces, (q, k, v), refs = refs[:count], refs[count : count + 3], refs[count + 3 :]
    rows = HEAD + AUX
    if carried:
        dk_in, dv_in = refs[:2]
        refs = refs[2:]
    dk, dv, norms = refs

    @pl.loop(0, heads)
    def _(h):
        mine = pl.ds(pl.multiple_of(h * rows, 16), rows)
        lanes = [slice(i, i + step) for i in range(0, pieces[0].shape[1], step)]
        parts = [p[mine, n] for n in lanes for p in pieces]
        terms = parts[0] if len(parts) == 1 else jnp.concatenate(parts, axis=1)
        probs = jnp.exp(dot(with_terms(q[h], terms), k[h], TN))
        grads = (probs * dot(terms, v[h], TN)).astype(BF)
        value = dot(terms[:HEAD], probs.astype(BF), NN)
        key = dot(q[h, :HEAD, :], grads, NN)
        dv[h] = dv_in[h] + value if carried else value
        dk[h] = dk_in[h] + key if carried else key

    for i in range(norms.shape[0]):
        norms[i] = pieces[i][heads * rows : heads * rows + NORM_ROWS, :NORM_LANES].astype(F32)


NORM_LANES = 256


def key_grad(pieces, chunks, step, slots, q, keys, values, heads, group, sums=()):
    width = sum(p.shape[1] for p in pieces)
    rows = HEAD + AUX
    own = pl.BlockSpec((heads, rows, group), lambda i, s: (0, 0, s[1]))
    specs = [whole(p.shape) for p in pieces]
    specs += [pl.BlockSpec((heads, rows, width), lambda i, s: (0, 0, s[0])), own, own]
    specs += [whole(s.shape) for s in sums]
    scores = heads * group * width
    return call(
        functools.partial(key_grad_kernel, heads, len(pieces), step, bool(sums)),
        "key_grad",
        [*pieces, q, keys, values, *sums],
        [struct((heads, HEAD, group), F32)] * 2 + [struct((chunks, NORM_ROWS, NORM_LANES), F32)],
        prefetch=[slots],
        specs=specs,
        flops=scores * 1024,
        exps=scores,
    )


def norm_parts(values):
    centered = values - jnp.mean(values, axis=-1, keepdims=True)
    inverse = lax.rsqrt(jnp.mean(centered * centered, axis=-1, keepdims=True) + NORM_EPS)
    return centered * inverse, inverse


def norm_back(grad_out, normed, inverse, gain):
    scaled = grad_out * gain
    grad_in = inverse * (
        scaled
        - jnp.mean(scaled, axis=-1, keepdims=True)
        - normed * jnp.mean(scaled * normed, axis=-1, keepdims=True)
    )
    own = grad_out.shape[0] // 2

    def total(v):
        return jnp.sum(v[:own], axis=0, keepdims=True) + jnp.sum(v[own:], axis=0, keepdims=True)

    return grad_in, (total(grad_out * normed), total(grad_out))


def col_total(mine, other):
    own = mine.shape[0] // 2
    return mine[...].astype(F32) + jnp.concatenate([other[own:], other[:own]], axis=0).astype(F32)


def first_norm_kernel(mine, other, tokens, gain, bias, residual, hidden):
    value = tokens[...].astype(F32) + col_total(mine, other)
    residual[...] = value
    normed, _ = norm_parts(value)
    hidden[...] = (normed * gain[...] + bias[...]).astype(BF)


def second_norm_kernel(mine, other, residual, gain1, bias1, gain2, bias2, cotangent, result, grad, grad_bf, sums):
    hidden = norm_parts(residual[...])[0] * gain1[...] + bias1[...]
    normed, inverse = norm_parts(hidden + col_total(mine, other))
    own = result.shape[0]
    result[...] = (normed[:own] * gain2[...] + bias2[...]).astype(BF)
    value, (dgain, dbias) = norm_back(cotangent[...].astype(F32), normed, inverse, gain2[...])
    grad[...] = value
    grad_bf[...] = value.astype(BF)
    sums[0:1] = dgain
    sums[1:2] = dbias


def first_norm_back_kernel(mine, other, residual, gain, grad2, sums2, grad, package):
    normed, inverse = norm_parts(residual[...])
    grad_out = grad2[...] + col_total(mine, other)
    value, (dgain, dbias) = norm_back(grad_out, normed, inverse, gain[...])
    grad[...] = value[: grad.shape[0]]
    rows = value.shape[0]
    package[:rows] = value.astype(BF)
    sums = jnp.concatenate([dgain, dbias, sums2[0:1], sums2[1:2]], axis=0)
    high = sums.astype(BF)
    low = (sums - high.astype(F32)).astype(BF)
    blank = jnp.zeros((8, sums.shape[1]), F32)
    package[rows:] = jnp.concatenate([high.astype(F32), low.astype(F32), blank], axis=0).astype(BF)


def stacked(refs, rows):
    return jnp.concatenate([r[:rows] for r in refs], axis=0)


def forward_kernel(count, units, starts, *refs):
    pieces, hidden, (gu, dn, gate_up, inner, near, far, held) = refs[:count], refs[count:-7], refs[-7:]
    for i, piece in enumerate(pieces):
        rows = pl.ds(pl.multiple_of(starts[i], 16), piece.shape[0])
        gu[rows, :] = piece[:, : 2 * units]
        dn[rows, :] = piece[:, 2 * units :]
    held[...] = stacked(hidden, hidden[0].shape[0])
    size = held.shape[0] // 2

    @pl.loop(0, 2)
    def _(i):
        rows = pl.ds(pl.multiple_of(i * size, 128), size)
        both = dot(held[rows, :], gu[...], NN)
        gate_up[rows, :] = both
        up, gate = both[:, :units], both[:, units:]
        value = (gate * jax.nn.sigmoid(gate) * up).astype(BF)
        inner[rows, :] = value
        part = dot(value, dn[...], NT).astype(BF)
        for j, out in enumerate((near, far)):

            @pl.when(i == j)
            def _():
                out[...] = part


def backward_kernel(units, *refs):
    pieces, (gu, dn, gate_up, grads, near, far, held) = refs[:-7], refs[-7:]
    held[...] = stacked(pieces, pieces[0].shape[0])
    size = held.shape[0] // 2

    @pl.loop(0, 2)
    def _(i):
        rows = pl.ds(pl.multiple_of(i * size, 128), size)
        grad_inner = dot(held[rows, :], dn[...], NN)
        up, gate = gate_up[rows, :units], gate_up[rows, units:]
        sigma = jax.nn.sigmoid(gate)
        grads[rows, :units] = (grad_inner * gate * sigma).astype(BF)
        grads[rows, units:] = (grad_inner * up * sigma * (1.0 + gate * (1.0 - sigma))).astype(BF)
        part = dot(grads[rows, :], gu[...], NT).astype(BF)
        for j, out in enumerate((near, far)):

            @pl.when(i == j)
            def _():
                out[...] = part


def write_blocks(held, starts, outs):
    for i, out in enumerate(outs):
        out[...] = held[pl.ds(pl.multiple_of(starts[i], 16), out.shape[0]), :]


def block_structs(features, width, ring):
    if not ring:
        return [struct((features, width), BF)]
    share = features // len(CYCLE)
    sizes = [share] * 4 + [share // 2] * 2 + [share] * 3
    return [struct((n, width), BF) for n in sizes]


def ffn_grad_kernel(units, n_blocks, starts, *refs):
    hidden, g, (grads, inner) = refs[:2], refs[2:4], refs[4:6]
    outs, held = refs[6 : 6 + n_blocks], refs[6 + n_blocks]
    own = hidden[0].shape[0]
    turned = stacked(hidden, own).T
    for t in range(0, 2 * units, units):
        held[:, t : t + units] = dot(turned, grads[:, t : t + units], NN).astype(BF)
    held[:, 2 * units :] = dot(stacked(g, own).T, inner[...], NN).astype(BF)
    write_blocks(held, starts, outs)


def prepare_kernel(heads, taken, *refs):
    pieces, (w_out, context, log_total, package) = refs[:2], refs[2:]
    g = stacked(pieces, taken)
    rows = HEAD + AUX
    grad = dot(w_out[...], g, NT).astype(BF)
    index = lax.broadcasted_iota(jnp.int32, (AUX, g.shape[0]), 0)
    for h in range(heads):
        part = grad[h * HEAD : (h + 1) * HEAD]
        package[h * rows : h * rows + HEAD] = part
        delta = jnp.sum(part.astype(F32) * context[h], axis=0, keepdims=True)
        tail = jnp.zeros(index.shape, F32)
        for at, value in ((8, -log_total[h : h + 1]), (11, -delta)):
            for j in range(3):
                high = value.astype(BF).astype(F32)
                tail = jnp.where(index == at + j, high, tail)
                value = value - high
        package[h * rows + HEAD : (h + 1) * rows] = tail.astype(BF)

    def sums(piece):
        both = piece[taken : taken + 16].astype(F32)
        return both[:4] + both[4:8]

    total = sums(pieces[0]) + sums(pieces[1])
    high = total.astype(BF).astype(F32)
    both = jnp.concatenate([high, total - high], axis=0)
    base = heads * rows
    package[base:, NORM_LANES:] = jnp.zeros((package.shape[0] - base, package.shape[1] - NORM_LANES), BF)
    parts = [both[:, i * NORM_LANES : (i + 1) * NORM_LANES] for i in range(both.shape[1] // NORM_LANES)]
    parts.append(jnp.zeros((package.shape[0] - base - 8 * len(parts), NORM_LANES), F32))
    package[base:, :NORM_LANES] = jnp.concatenate(parts, axis=0).astype(BF)


def turn_back(first, second, cosine, sine):
    return jnp.concatenate([first * cosine + second * sine, second * cosine - first * sine], axis=0)


def early_grad_kernel(heads, taken, n_x, slots, *refs):
    x_refs, g_refs, refs = refs[:n_x], refs[n_x : n_x + 2], refs[n_x + 2 :]
    grad_query, turn, context, mixed, held = refs
    half = HEAD // 2
    scale = 1.0 / math.sqrt(HEAD)
    for h in range(heads):
        value = grad_query[h] * scale
        mixed[h * HEAD : (h + 1) * HEAD] = turn_back(value[:half], value[half:], turn[:half], turn[half:]).astype(BF)
    x = stacked(x_refs, x_refs[0].shape[0])
    width = heads * HEAD
    held[:, :width] = dot(mixed[...], x, NN).T.astype(BF)
    held[:, width:] = dot(context[...], stacked(g_refs, taken), NN).T.astype(BF)


def late_grad_kernel(heads, n_x, n_blocks, slots, starts, *refs):
    x_refs, refs = refs[:n_x], refs[n_x:]
    mixed_q, grad_key, grad_value, early, turn, weight, near, far, *refs = refs
    outs, held, mixed = refs[:n_blocks], refs[n_blocks], refs[n_blocks + 1]
    half = HEAD // 2
    width = heads * HEAD
    mixed[:width] = mixed_q[...]
    for h in range(heads):
        value = grad_key[h]
        mixed[width + h * HEAD : width + (h + 1) * HEAD] = turn_back(
            value[:half], value[half:], turn[:half], turn[half:]
        ).astype(BF)
        mixed[2 * width + h * HEAD : 2 * width + (h + 1) * HEAD] = grad_value[h].astype(BF)
    back = dot(mixed[...], weight[...], TN)
    size = near.shape[0]
    near[...] = back[:size].astype(BF)
    far[...] = back[size:].astype(BF)
    x = stacked(x_refs, x_refs[0].shape[0])
    held[:, : 2 * width] = early[...]
    held[:, 2 * width :] = dot(mixed[width:], x, NN).T.astype(BF)
    write_blocks(held, starts, outs)


def finish_ffn_kernel(units, block, ahead, back, gu, dn):
    total = block[...].astype(F32) + ahead[...].astype(F32) + back[...].astype(F32)
    gu[:, 0, :] = total[:, :units]
    gu[:, 1, :] = total[:, units : 2 * units]
    dn[...] = total[:, 2 * units :].T


def finish_mix_kernel(width, block, ahead, back, mix, out):
    total = block[...].astype(F32) + ahead[...].astype(F32) + back[...].astype(F32)
    mix[0] = total[:, :width]
    mix[1] = total[:, 2 * width : 3 * width]
    mix[2] = total[:, 3 * width :]
    out[...] = total[:, width : 2 * width].T


NORM_ROWS = 24


def norm_total_kernel(rows, *refs):
    pieces, (out, held) = refs[:-2], refs[-2:]
    at = 0
    for piece in pieces:
        for i in range(piece.shape[0]):
            held[rows[at]] = piece[i]
            at += 1
    total = held[0]
    for r in range(1, at):
        total = total + held[r]
    for i in range(NORM_ROWS // 8):
        part = total[8 * i : 8 * i + 8]
        out[:, i * NORM_LANES : (i + 1) * NORM_LANES] = part[:4] + part[4:]


def slot_tables(seq_lengths, packed_order, wanted, local, waits):
    blocks = packed_order.reshape(-1, local)
    index = jnp.arange(blocks.shape[0], dtype=jnp.int32)
    slots = jnp.sum(
        jnp.where(wanted[:, None, None] == index[None, :, None], blocks[None], 0), axis=1
    ).reshape(1, -1)
    count = seq_lengths.shape[0]
    seq = jnp.zeros_like(slots)
    start = jnp.zeros_like(slots)
    end = jnp.int32(0)
    for s in range(count):
        end = end + seq_lengths[s]
        passed = slots >= end
        seq = seq + passed.astype(jnp.int32)
        start = jnp.where(passed, end, start)
    positions = after((slots - start).astype(F32), waits[0])
    half = HEAD // 2
    freqs = ROPE_BASE ** (-jnp.arange(half, dtype=F32) * 2.0 / HEAD)
    angles = positions * freqs[:, None]
    turn = jnp.concatenate([jnp.cos(angles), jnp.sin(angles)], axis=0)
    line = jnp.arange(3 * AUX, dtype=jnp.int32)[:, None]
    member = lax.rem(line, AUX) == after(seq, waits[1])
    ones = ((line >= 8) & (line < 11)) | ((line >= 2 * AUX + 11) & (line < 2 * AUX + 14))
    marks = jnp.where(ones, 1.0, 0.0)
    marks = jnp.where((line < 8) & member, 1.0, marks)
    marks = jnp.where((line >= AUX) & (line < AUX + 8) & ~member, FAR, marks)
    return turn, marks.astype(BF)


def local(
    tokens,
    w_qkv,
    w_out,
    w_gate_up,
    w_down,
    gain1,
    bias1,
    gain2,
    bias2,
    cotangent,
    seq_lengths,
    packed_order,
):
    rows = lax.axis_size("row")
    row, col = lax.axis_index("row"), lax.axis_index("col")
    ring = rows == len(CYCLE)
    own, features = tokens.shape
    group = own * lax.axis_size("col")
    total = group * rows
    share = w_qkv.shape[0]
    width = w_qkv.shape[2]
    heads = width // HEAD
    units = w_gate_up.shape[2]
    gains = [v.reshape(1, features) for v in (gain1, bias1, gain2, bias2)]

    early = jnp.concatenate([w_qkv.reshape(share, 3 * width), w_out.T], axis=1)
    late = jnp.concatenate([w_gate_up.reshape(share, 2 * units), w_down.T], axis=1)

    pair = tokens_pair = jnp.concatenate([tokens, col_swap(tokens, 2)], axis=0)
    taken = pair.shape[0]
    if ring:
        place = cycle_place()
        half = share // 2
        starts = cycle_rows(place, (0, *ROUND_STEPS)) * share + jnp.array([0] * 8 + [half], jnp.int32)
        block_starts = cycle_rows(place, BLOCK_STEPS) * share + jnp.array([0] * 5 + [half] + [0] * 3, jnp.int32)
        layout = [(ROUND_STEPS[2 * i + j], o) for i in range(3) for o in OFFSETS for j in range(2)]
        layout += [(step, o) for step in (0, 4) for o in OFFSETS]
        wanted = cycle_rows(place, [step for step, _ in layout]) * len(OFFSETS)
        wanted = wanted + (col ^ jnp.array([o for _, o in layout], jnp.int32))
        token_half = own // 2
        (packed,) = call(
            functools.partial(pack_kernel, 2),
            "pack",
            [w_qkv.transpose(1, 0, 2), w_out, tokens],
            [struct((share + own, features), BF)],
        )
        ring_early = Rounds(packed, 0)
        waits = [ring_early.step(), ring_early.step()]
        ring_early.step()
        ring_early.step()
        packed_order = after(packed_order, waits[0])

        def token_rows(v):
            step = half + token_half
            return [v[i + half : i + step] for i in range(0, v.shape[0], step)]

    else:
        starts = block_starts = jnp.zeros((1,), jnp.int32)
        wanted = jnp.arange(rows, dtype=jnp.int32)[:, None] * len(OFFSETS)
        wanted = (wanted + (col ^ jnp.array(OFFSETS, jnp.int32))[None, :]).reshape(-1)
        waits = (), ()
        early_full = lax.all_gather(early, "row", axis=0, tiled=True)
        w_mix, full_out = assemble([early_full], [[(0, features, 0)]], starts, 3 * width)

    turn, marks = slot_tables(seq_lengths, packed_order, wanted, own, waits)
    if ring:
        cuts = [[(0, half, 0), (half + token_half, half, half)]] * 7 + [[(0, half, 0)]] * 2
        w_mix, full_out = assemble([ring_early.block, *ring_early.pieces()], cuts, starts, 3 * width)
    fixed = (w_mix, turn, marks, heads, total, group)
    if ring:
        pair = after(pair, ring_early.done[3])
    x_pieces = [pair, col_swap(pair, 1)]

    def at(slot):
        return jnp.asarray(slot, jnp.int32).reshape(1)

    own_slot = at(6) if ring else at(row)
    keys, values, queries, own_q, *state = attend("first", x_pieces, own_slot, *fixed)
    if ring:
        late_ring = Rounds(late, 0)
        rounds = ring_early.done

        def side(held):
            both = jnp.concatenate([rows for v in held for rows in token_rows(v)], axis=0)
            return jnp.concatenate([both, col_swap(both, 2)], axis=0)

        def middle(i, chunk):
            return attend(
                "middle",
                [chunk, col_swap(chunk, 1)],
                at(i),
                *fixed,
                (own_q, *state, keys, values, queries),
            )

        one = side(rounds[0])
        two = side(after(rounds[1], one))
        three = side(after(rounds[2], two))
        late_ring.step(rounds[2])
        two = after(two, state[0])
        keys, values, queries, *state = middle(0, after(one, rounds[3]))
        both = [rows for v in after(rounds[3], three) for rows in token_rows(v)]
        both = jnp.concatenate([*both, cotangent], axis=0)
        swapped = col_swap(both, 2)
        far = jnp.concatenate([both[:own], swapped[:own]], axis=0)
        other_cotangent = swapped[own:]
        three = after(three, state[0])
        keys, values, queries, *state = middle(1, after(two, late_ring.done[0]))
        late_ring.step()
        far = after(far, state[0])
        keys, values, queries, *state = middle(2, three)
        far = after(far, late_ring.done[1])
        keys, values, queries, *finished = attend(
            "last",
            [far, col_swap(far, 1)],
            at(7),
            *fixed,
            (own_q, *state, keys, values, queries),
            full_out,
        )
    else:
        blocks = lax.all_gather(jnp.concatenate(x_pieces, axis=0), "row", axis=0, tiled=False)

        def block(i):
            slot = lax.rem(row + i, rows)
            return [lax.dynamic_index_in_dim(blocks, slot, 0, keepdims=False)], at(slot)

        def step(i, carried):
            *state, keys, values, queries = carried
            keys, values, queries, *state = attend(
                "middle", *block(i), *fixed, (own_q, *state, keys, values, queries)
            )
            return (*state, keys, values, queries)

        *state, keys, values, queries = lax.fori_loop(1, rows - 1, step, (*state, keys, values, queries))
        keys, values, queries, *finished = attend(
            "last", *block(rows - 1), *fixed, (own_q, *state, keys, values, queries), full_out
        )
    near, far, context_bf, context, log_total = finished

    if ring:
        late_ring.step()
        near = after(near, late_ring.done[2])
        late_ring.step()
    else:
        late_pieces = [lax.all_gather(late, "row", axis=0, tiled=True)]

    if not ring:
        other_cotangent = col_swap(cotangent, 2)
    cotangent_pair = jnp.concatenate([cotangent, other_cotangent], axis=0)
    part = struct((group // 2, features), BF)
    flat, flat_bf = struct((taken, features), F32), struct((taken, features), BF)
    residual1, hidden = call(
        first_norm_kernel,
        "first_norm",
        [*col_exchange(near, far), after(tokens_pair, late_ring.done[3]) if ring else tokens_pair, *gains[:2]],
        [flat, flat_bf],
    )
    if ring:
        late_pieces = [late, *late_ring.pieces()]
    hidden_pieces = [hidden, col_swap(hidden, 1)]
    w_gu, w_dn, gate_up, inner, near, far = call(
        functools.partial(forward_kernel, len(late_pieces), units),
        "ffn_forward",
        [*late_pieces, *hidden_pieces],
        [
            struct((features, 2 * units), BF),
            struct((features, units), BF),
            struct((group, 2 * units), F32),
            struct((group, units), BF),
            part,
            part,
        ],
        prefetch=[starts],
        scratch=[pltpu.VMEM((group, features), BF)],
        flops=6 * group * features * units,
    )
    result, grad_res2, grad_bf, sums2 = call(
        second_norm_kernel,
        "second_norm",
        [*col_exchange(near, far), residual1, *gains, cotangent_pair],
        [struct((own, features), BF), flat, flat_bf, struct((8, features), F32)],
    )
    grad_pieces = [grad_bf, col_swap(grad_bf, 1)]
    grad_gate_up, near, far = call(
        functools.partial(backward_kernel, units),
        "ffn_backward",
        [*grad_pieces, w_gu, w_dn, gate_up],
        [struct((group, 2 * units), BF), part, part],
        scratch=[pltpu.VMEM((group, features), BF)],
        flops=6 * group * features * units,
    )
    exchanged = col_exchange(near, far)
    outs = block_structs(features, 3 * units, ring)
    blocks = call(
        functools.partial(ffn_grad_kernel, units, len(outs)),
        "ffn_grad",
        [*hidden_pieces, *grad_pieces, grad_gate_up, inner],
        outs,
        prefetch=[block_starts],
        scratch=[pltpu.VMEM((features, 3 * units), BF)],
        flops=6 * group * features * units,
    )
    residual1 = after(residual1, blocks)
    ffn_sum = RowSum(blocks)
    sent = ffn_sum.step()
    grad_res1, package = call(
        first_norm_back_kernel,
        "first_norm_back",
        [*exchanged, residual1, gains[0], grad_res2, sums2],
        [struct((own, features), F32), struct((taken + 16, features), BF)],
    )
    attn_pieces = after([package, col_swap(package, 1)], sent)
    (package,) = call(
        functools.partial(prepare_kernel, heads, taken),
        "prepare",
        [*attn_pieces, full_out, context, log_total],
        [struct((heads * (HEAD + AUX) + 32, group), BF)],
        flops=2 * width * features * group,
    )
    span = min(2 * group, total)
    steps_all = total // span
    grad_query = jnp.zeros((heads, HEAD, group), F32)
    if ring:
        package_ring = Rounds(package, 1)
        package_ring.step()
        sent = ffn_sum.step()
    grad_query = query_grad(own_q, package, keys, values, heads, span, 0, steps_all, grad_query)
    own_turn = pl.BlockSpec((HEAD, group), lambda i, s, *_: (0, s[0]))
    args = [*x_pieces, *attn_pieces, grad_query, turn, context_bf]
    specs = [whole(a.shape) for a in args]
    specs[-2] = own_turn
    mixed_q, early_grad = call(
        functools.partial(early_grad_kernel, heads, taken, len(x_pieces)),
        "early_grad",
        args,
        [struct((width, group), BF), struct((features, 2 * width), BF)],
        prefetch=[own_slot],
        specs=specs,
        flops=4 * width * features * group,
    )

    def key_step(pieces, chunks, slot, sums):
        slots = jnp.where(jnp.arange(2) == 0, at(slot), own_slot)
        step = own if chunks == 2 else pieces[0].shape[1]
        *sums, norms = key_grad(
            pieces, chunks, step, slots, queries, keys, values, heads, group, tuple(sums)
        )
        return sums, norms

    norm_out = struct((4, features), F32)
    if ring:
        package_ring.step(early_grad)
        sums, norms = key_step([after(package, early_grad, package_ring.done[0], sent)], 1, 6, ())
        norm_pieces = [norms]
        for i in range(3):
            sums, norms = key_step(package_ring.done[i], 2, i, sums)
            norm_pieces.append(norms)
            if i < 2:
                package_ring.step(norms)
        ffn_sum.moving = after(ffn_sum.moving, norms)
        sums, norms = key_step(package_ring.done[3], 1, 7, sums)
        norm_pieces.append(norms)
        (norm_sums,) = call(
            norm_total_kernel,
            "norm_total",
            norm_pieces,
            [norm_out],
            prefetch=[cycle_rows(place, (0, *ROUND_STEPS[:7]))],
            scratch=[pltpu.VMEM((rows, NORM_ROWS, NORM_LANES), F32)],
        )
    else:
        packages = lax.all_gather(package, "row", axis=0, tiled=False)

        def step(i, carried):
            sums, norms = carried
            piece = lax.dynamic_index_in_dim(packages, i, 0, keepdims=False)
            sums, more = key_step([piece], 1, i, sums)
            return tuple(sums), norms + more

        zeros = jnp.zeros((heads, HEAD, group), F32)
        sums, norms = lax.fori_loop(
            0, rows, step, ((zeros, zeros), jnp.zeros((1, NORM_ROWS, NORM_LANES), F32))
        )
        (norm_sums,) = call(
            norm_total_kernel,
            "norm_total",
            [norms],
            [norm_out],
            prefetch=[jnp.zeros((1,), jnp.int32)],
            scratch=[pltpu.VMEM((1, NORM_ROWS, NORM_LANES), F32)],
        )
    args = [*x_pieces, mixed_q, *sums, early_grad, turn, w_mix]
    specs = [whole(a.shape) for a in args]
    specs[-2] = own_turn
    outs = block_structs(features, 4 * width, ring)
    near, far, *blocks = call(
        functools.partial(late_grad_kernel, heads, len(x_pieces), len(outs)),
        "late_grad",
        args,
        [part, part, *outs],
        prefetch=[own_slot, block_starts],
        scratch=[pltpu.VMEM((features, 4 * width), BF), pltpu.VMEM((3 * width, group), BF)],
        specs=specs,
        flops=10 * width * features * group,
    )
    late_sum = RowSum(blocks)
    late_sum = late_sum.terms()
    grad_gu, grad_dn = call(
        functools.partial(finish_ffn_kernel, units),
        "finish_ffn",
        ffn_sum.terms(),
        [struct((share, 2, units), F32), struct((units, share), F32)],
        cost=20.0,
    )
    grad_tokens = grad_res1 + col_sum(near, far)
    grad_mix, grad_out = call(
        functools.partial(finish_mix_kernel, width),
        "finish_mix",
        late_sum,
        [struct((3, share, width), F32), struct((width, share), F32)],
        cost=20.0,
    )
    return (
        result,
        grad_tokens,
        grad_mix.transpose(1, 0, 2),
        grad_out,
        grad_gu,
        grad_dn,
        norm_sums[0],
        norm_sums[1],
        norm_sums[2],
        norm_sums[3],
    )


def solution(mesh):
    placed = (
        P(("row", "col"), None),
        P("row", None, "col"),
        P("col", "row"),
        P("row", None, "col"),
        P("col", "row"),
        P(),
        P(),
        P(),
        P(),
        P(("row", "col"), None),
        P(),
        P(),
    )
    return jax.shard_map(
        local,
        mesh=mesh,
        in_specs=placed,
        out_specs=(
            P(("row", "col"), None),
            P(("row", "col"), None),
            P("row", None, "col"),
            P("col", "row"),
            P("row", None, "col"),
            P("col", "row"),
            P(),
            P(),
            P(),
            P(),
        ),
        check_vma=False,
    )
```

```python
import functools
import math

import jax
import jax.numpy as jnp
from jax import lax
from jax.experimental import pallas as pl
from jax.experimental.pallas import tpu as pltpu
from jax.sharding import PartitionSpec as P

HEAD = 64
ROPE_BASE = 1000.0
NORM_EPS = 1e-12
FAR = -(2.0**100)
LOWEST = -1e30
AUX = 16
BF = jnp.bfloat16
F32 = jnp.float32

CYCLE = (0, 2, 4, 6, 7, 5, 3, 1)
OFFSETS = (0, 2, 1, 3)


def dot(a, b, contract, out=F32):
    return lax.dot_general(a, b, (contract, ((), ())), preferred_element_type=out)


COST = 0.02

NN = ((1,), (0,))
NT = ((1,), (1,))
TN = ((0,), (0,))


def forward_hop(v):
    n = len(CYCLE)
    return lax.ppermute(v, "row", [(CYCLE[i], CYCLE[(i + 1) % n]) for i in range(n)])


def backward_hop(v):
    n = len(CYCLE)
    return lax.ppermute(v, "row", [(CYCLE[(i + 1) % n], CYCLE[i]) for i in range(n)])


def col_swap(v, mask):
    count = lax.axis_size("col")
    return lax.ppermute(v, "col", [(i, i ^ mask) for i in range(count)])


def cycle_place():
    row = lax.axis_index("row")
    return sum(jnp.where(row == CYCLE[i], i, 0) for i in range(len(CYCLE))).astype(jnp.int32)


def cycle_rows(place, steps):
    places = lax.rem(place + jnp.array([s + len(CYCLE) for s in steps], jnp.int32), len(CYCLE))
    return sum(jnp.where(places == i, CYCLE[i], 0) for i in range(len(CYCLE))).astype(jnp.int32)


def after(value, *first):
    return lax.optimization_barrier((value, first))[0]


class Rounds:
    def __init__(self, block, axis):
        self.block, self.held, self.axis, self.done = block, (block, block), axis, []

    def step(self, *first):
        behind, ahead = after(self.held, first) if first else self.held
        if len(self.done) == 3:
            half = behind.shape[self.axis] // 2
            behind = lax.slice_in_dim(behind, 0, half, axis=self.axis)
            ahead = lax.slice_in_dim(ahead, half, 2 * half, axis=self.axis)
        self.held = forward_hop(behind), backward_hop(ahead)
        self.done.append(self.held)
        return self.held

    def pieces(self):
        while len(self.done) < 4:
            self.step()
        return [p for r in self.done for p in r]


ROUND_STEPS = (-1, 1, -2, 2, -3, 3, 4, 4)
BLOCK_STEPS = (0, 1, 2, 3, 4, 4, 5, 6, 7)


class RowSum:
    def __init__(self, blocks):
        self.blocks, self.hops, self.moving = blocks, 0, None
        if len(blocks) > 1:
            self.moving = blocks[4], blocks[5]

    def step(self):
        if len(self.blocks) == 1:
            return ()
        half = self.blocks[4].shape[0]

        def add(v, block):
            return (v.astype(F32) + block.astype(F32)).astype(BF)

        ahead, back = forward_hop(self.moving[0]), backward_hop(self.moving[1])
        up = (self.blocks[3], self.blocks[2], self.blocks[1], None)[self.hops]
        down = (self.blocks[6], self.blocks[7], self.blocks[8], None)[self.hops]
        if self.hops == 0:
            ahead = jnp.concatenate([add(ahead, up[:half]), up[half:]], axis=0)
            back = jnp.concatenate([down[:half], add(back, down[half:])], axis=0)
        elif up is not None:
            ahead, back = add(ahead, up), add(back, down)
        self.hops += 1
        self.moving = ahead, back
        return self.moving

    def terms(self):
        if len(self.blocks) == 1:
            full = lax.psum_scatter(self.blocks[0].astype(F32), "row", scatter_dimension=0, tiled=True)
            return [full, jnp.zeros_like(full), jnp.zeros_like(full)]
        while self.hops < 4:
            self.step()
        return [self.blocks[0], *self.moving]


def core_sum(near, far):
    return (near.astype(F32) + col_swap(far, 1).astype(F32)).astype(BF)


def col_exchange(near, far):
    mine = core_sum(near, far)
    return [mine, col_swap(mine, 2)]


def col_sum(near, far):
    mine = core_sum(near, far)
    own = mine.shape[0] // 2
    return mine[:own].astype(F32) + col_swap(mine[own:], 2).astype(F32)


def whole(shape):
    return pl.BlockSpec(shape, lambda *_: (0,) * len(shape))


ANY = pl.BlockSpec(memory_space=pl.ANY)


def call(kernel, name, args, outs, prefetch=(), scratch=(), specs=None, out_specs=None, aliases=None, grid=(1,), flops=0, exps=0, limit=20, cost=COST):
    args, outs = list(args), list(outs)
    moved = sum(a.size * a.dtype.itemsize for a in args) + sum(
        math.prod(o.shape) * o.dtype.itemsize for o in outs
    )
    return pl.pallas_call(
        kernel,
        grid_spec=pltpu.PrefetchScalarGridSpec(
            num_scalar_prefetch=len(prefetch),
            grid=grid,
            in_specs=specs or [whole(a.shape) for a in args],
            out_specs=out_specs or [whole(o.shape) for o in outs],
            scratch_shapes=list(scratch),
        ),
        out_shape=outs,
        input_output_aliases=aliases or {},
        cost_estimate=pl.CostEstimate(flops=int(flops * cost), bytes_accessed=int(moved * cost), transcendentals=int(exps * cost)),
        compiler_params=pltpu.CompilerParams(vmem_limit_bytes=limit << 20),
        name=name,
    )(*prefetch, *args)


def struct(shape, kind):
    return jax.ShapeDtypeStruct(tuple(shape), kind)


def rows_at(start, count):
    return pl.ds(pl.multiple_of(start, 4), count)


def pack_kernel(parts, weights, w_out, tokens, out):
    early = jnp.concatenate([*(weights[c] for c in range(3)), w_out[...].T], axis=1)
    half, token_half = early.shape[0] // parts, tokens.shape[0] // parts
    for i in range(parts):
        at = i * (half + token_half)
        out[at : at + half] = early[i * half : (i + 1) * half]
        out[at + half : at + half + token_half] = tokens[i * token_half : (i + 1) * token_half]


def assemble_kernel(split, cuts, starts, *refs):
    pieces, (mix, out, held) = refs[:-3], refs[-3:]
    for i, piece in enumerate(pieces):
        for begin, count, shift in cuts[i]:
            held[pl.ds(pl.multiple_of(starts[i] + shift, 16), count), :] = piece[begin : begin + count]
    mix[...] = held[:, :split].T
    out[...] = held[:, split:].T


def assemble(pieces, cuts, starts, split):
    width = pieces[0].shape[1]
    total = sum(c[1] for cut in cuts for c in cut)
    return call(
        functools.partial(assemble_kernel, split, cuts),
        "assemble",
        pieces,
        [struct((split, total), BF), struct((width - split, total), BF)],
        prefetch=[starts],
        scratch=[pltpu.VMEM((total, width), BF)],
    )


def project_into(pieces, weight, turn, marks, q_out, k_out, v_out, heads):
    half = HEAD // 2
    width = heads * HEAD
    begin = 0
    for piece in pieces:
        count = piece.shape[0]
        lanes = slice(begin, begin + count)
        begin += count
        mixed = dot(weight[...], piece[...], NT)
        cosine, sine = turn[:half, lanes], turn[half:, lanes]
        for h in range(heads):
            for base, out, scale, tail in (
                (0, q_out, 1.0 / math.sqrt(HEAD), AUX),
                (width, k_out, None, 0),
            ):
                at = base + h * HEAD
                first, second = mixed[at : at + half], mixed[at + half : at + HEAD]
                turned = jnp.concatenate(
                    [first * cosine - second * sine, second * cosine + first * sine], axis=0
                )
                if scale is not None:
                    turned = turned * scale
                out[h, :HEAD, lanes] = turned.astype(BF)
                out[h, HEAD:, lanes] = marks[tail : tail + AUX, lanes]
            at = 2 * width + h * HEAD
            v_out[h, :HEAD, lanes] = mixed[at : at + HEAD].astype(BF)
            v_out[h, HEAD:, lanes] = marks[2 * AUX : 3 * AUX, lanes]


def attend_kernel(mode, heads, count, slot, *refs):
    pieces, refs = refs[:count], refs[count:]
    weight, turn, marks = refs[:3]
    refs = refs[3:]
    if mode != "first":
        q_own, top_in, sum_in, acc_in = refs[:4]
        refs = refs[7:]
    if mode == "last":
        w_out, refs = refs[0], refs[1:]
    k, v, q = refs[:3]
    refs = refs[3:]
    project_into(pieces, weight, turn, marks, q, k, v, heads)
    if mode == "first":
        q_own, refs = refs[0], refs[1:]
        q_own[...] = q[...]
    if mode == "last":
        near, far, context_bf, context, log_total = refs
    else:
        top, total, acc = refs

    @pl.loop(0, heads)
    def _(h):
        one = pl.ds(h, 1)
        scores = dot(k[h], q_own[h], TN)
        new = jnp.max(scores, axis=0, keepdims=True)
        if mode != "first":
            old = top_in[one, :]
            new = jnp.maximum(old, new)
            keep = jnp.exp(old - new)
        weights = jnp.exp(scores - new)
        count = jnp.sum(weights, axis=0, keepdims=True)
        value = dot(v[h, :HEAD, :], weights.astype(BF), NN)
        if mode != "first":
            count = sum_in[one, :] * keep + count
            value = acc_in[h] * keep + value
        if mode == "last":
            value = value / count
            context[h] = value
            context_bf[pl.ds(pl.multiple_of(h * HEAD, HEAD), HEAD), :] = value.astype(BF)
            log_total[one, :] = new + jnp.log(count)
        else:
            top[one, :] = new
            total[one, :] = count
            acc[h] = value

    if mode == "last":
        attn = dot(context_bf[...], w_out[...], TN)
        half = near.shape[0]
        near[...] = attn[:half].astype(BF)
        far[...] = attn[half:].astype(BF)


def attend(mode, pieces, slot, weight, turn, marks, heads, total, group, carried=(), w_out=None):
    width = sum(p.shape[0] for p in pieces)
    rows = HEAD + AUX

    def lanes(*lead):
        return pl.BlockSpec((*lead, width), lambda i, s: (*(0,) * len(lead), s[0]))

    args = [*pieces, weight, turn, marks, *carried]
    specs = [whole(p.shape) for p in pieces]
    specs += [whole(weight.shape), lanes(turn.shape[0]), lanes(marks.shape[0])]
    buffers = [struct((heads, rows, total), BF)] * 3
    outs, out_specs = list(buffers), [lanes(heads, rows)] * 3
    aliases = {}
    if mode != "first":
        specs += [whole(c.shape) for c in carried[:4]] + [ANY] * 3
        base = 1 + len(pieces) + 3 + 4
        aliases = {base: 0, base + 1: 1, base + 2: 2}
    features = weight.shape[1]
    if mode == "last":
        args.append(w_out)
        specs.append(whole(w_out.shape))
        extra = [
            struct((group // 2, features), BF),
            struct((group // 2, features), BF),
            struct((heads * HEAD, group), BF),
            struct((heads, HEAD, group), F32),
            struct((heads, group), F32),
        ]
    else:
        extra = [
            struct((heads, group), F32),
            struct((heads, group), F32),
            struct((heads, HEAD, group), F32),
        ]
        if mode == "first":
            extra = [struct((heads, rows, group), BF)] + extra
    outs += extra
    out_specs += [whole(e.shape) for e in extra]
    scores = heads * width * group
    return call(
        functools.partial(attend_kernel, mode, heads, len(pieces)),
        "attend",
        args,
        outs,
        prefetch=[slot],
        specs=specs,
        out_specs=out_specs,
        aliases=aliases,
        flops=scores * 512,
        exps=scores,
    )


def with_terms(q, g):
    extra = g[HEAD:].astype(F32)
    row = lax.broadcasted_iota(jnp.int32, extra.shape, 0)
    extra = q[HEAD:].astype(F32) + jnp.where(row < 8, 0.0, extra)
    return jnp.concatenate([q[:HEAD], extra.astype(BF)], axis=0)


def query_grad_kernel(heads, q, g, k, v, out_in, out):
    @pl.when(pl.program_id(0) == 0)
    def _():
        out[...] = out_in[...]

    rows = HEAD + AUX

    @pl.loop(0, heads)
    def _(h):
        terms = g[pl.ds(pl.multiple_of(h * rows, 16), rows), :]
        probs = jnp.exp(dot(k[h], with_terms(q[h], terms), TN))
        grads = (probs * dot(v[h], terms, TN)).astype(BF)
        out[h] += dot(k[h, :HEAD, :], grads, NN)


def query_grad(q, g, keys, values, heads, width, begin, steps, carried):
    rows = keys.shape[1]
    group = q.shape[2]
    each = pl.BlockSpec((heads, rows, width), lambda i: (0, 0, i + begin))
    scores = heads * group * steps * width
    return call(
        functools.partial(query_grad_kernel, heads),
        "query_grad",
        [q, g, keys, values, carried],
        [struct((heads, HEAD, group), F32)],
        specs=[whole(q.shape), whole(g.shape), each, each, whole(carried.shape)],
        grid=(steps,),
        flops=scores * 768,
        exps=scores,
    )[0]


def key_grad_kernel(heads, count, step, carried, slots, *refs):
    pieces, (q, k, v), refs = refs[:count], refs[count : count + 3], refs[count + 3 :]
    rows = HEAD + AUX
    if carried:
        dk_in, dv_in = refs[:2]
        refs = refs[2:]
    dk, dv, norms = refs

    @pl.loop(0, heads)
    def _(h):
        mine = pl.ds(pl.multiple_of(h * rows, 16), rows)
        lanes = [slice(i, i + step) for i in range(0, pieces[0].shape[1], step)]
        parts = [p[mine, n] for n in lanes for p in pieces]
        terms = parts[0] if len(parts) == 1 else jnp.concatenate(parts, axis=1)
        probs = jnp.exp(dot(with_terms(q[h], terms), k[h], TN))
        grads = (probs * dot(terms, v[h], TN)).astype(BF)
        value = dot(terms[:HEAD], probs.astype(BF), NN)
        key = dot(q[h, :HEAD, :], grads, NN)
        dv[h] = dv_in[h] + value if carried else value
        dk[h] = dk_in[h] + key if carried else key

    for i in range(norms.shape[0]):
        for h in range(heads):
            norms[i, 8 * h : 8 * h + 8, :] = pieces[i][h * rows + HEAD : h * rows + HEAD + 8, :NORM_LANES].astype(F32)


NORM_LANES = 256


def key_grad(pieces, chunks, step, slots, q, keys, values, heads, group, sums=()):
    width = sum(p.shape[1] for p in pieces)
    rows = HEAD + AUX
    own = pl.BlockSpec((heads, rows, group), lambda i, s: (0, 0, s[1]))
    specs = [whole(p.shape) for p in pieces]
    specs += [pl.BlockSpec((heads, rows, width), lambda i, s: (0, 0, s[0])), own, own]
    specs += [whole(s.shape) for s in sums]
    scores = heads * group * width
    return call(
        functools.partial(key_grad_kernel, heads, len(pieces), step, bool(sums)),
        "key_grad",
        [*pieces, q, keys, values, *sums],
        [struct((heads, HEAD, group), F32)] * 2 + [struct((chunks, NORM_ROWS, NORM_LANES), F32)],
        prefetch=[slots],
        specs=specs,
        flops=scores * 1024,
        exps=scores,
    )


def norm_parts(values):
    centered = values - jnp.mean(values, axis=-1, keepdims=True)
    inverse = lax.rsqrt(jnp.mean(centered * centered, axis=-1, keepdims=True) + NORM_EPS)
    return centered * inverse, inverse


def norm_back(grad_out, normed, inverse, gain):
    scaled = grad_out * gain
    grad_in = inverse * (
        scaled
        - jnp.mean(scaled, axis=-1, keepdims=True)
        - normed * jnp.mean(scaled * normed, axis=-1, keepdims=True)
    )
    own = grad_out.shape[0] // 2

    def total(v):
        return jnp.sum(v[:own], axis=0, keepdims=True) + jnp.sum(v[own:], axis=0, keepdims=True)

    return grad_in, (total(grad_out * normed), total(grad_out))


def col_total(mine, other):
    own = mine.shape[0] // 2
    return mine[...].astype(F32) + jnp.concatenate([other[own:], other[:own]], axis=0).astype(F32)


def first_norm_kernel(mine, other, tokens, gain, bias, residual, hidden):
    value = tokens[...].astype(F32) + col_total(mine, other)
    residual[...] = value
    normed, _ = norm_parts(value)
    hidden[...] = (normed * gain[...] + bias[...]).astype(BF)


def second_norm_kernel(mine, other, residual, gain1, bias1, gain2, bias2, cotangent, result, grad, grad_bf, sums):
    hidden = norm_parts(residual[...])[0] * gain1[...] + bias1[...]
    normed, inverse = norm_parts(hidden + col_total(mine, other))
    own = result.shape[0]
    result[...] = (normed[:own] * gain2[...] + bias2[...]).astype(BF)
    value, (dgain, dbias) = norm_back(cotangent[...].astype(F32), normed, inverse, gain2[...])
    grad[...] = value
    grad_bf[...] = value.astype(BF)
    sums[0:1] = dgain
    sums[1:2] = dbias


def first_norm_back_kernel(mine, other, residual, gain, grad2, sums2, grad, package):
    normed, inverse = norm_parts(residual[...])
    grad_out = grad2[...] + col_total(mine, other)
    value, (dgain, dbias) = norm_back(grad_out, normed, inverse, gain[...])
    grad[...] = value[: grad.shape[0]]
    rows = value.shape[0]
    package[:rows] = value.astype(BF)
    sums = jnp.concatenate([dgain, dbias, sums2[0:1], sums2[1:2]], axis=0)
    high = sums.astype(BF)
    low = (sums - high.astype(F32)).astype(BF)
    blank = jnp.zeros((8, sums.shape[1]), F32)
    package[rows:] = jnp.concatenate([high.astype(F32), low.astype(F32), blank], axis=0).astype(BF)


def stacked(refs, rows):
    return jnp.concatenate([r[:rows] for r in refs], axis=0)


def forward_kernel(count, units, starts, *refs):
    pieces, hidden, (gu, dn, gate_up, inner, near, far, held) = refs[:count], refs[count:-7], refs[-7:]
    for i, piece in enumerate(pieces):
        rows = pl.ds(pl.multiple_of(starts[i], 16), piece.shape[0])
        gu[rows, :] = piece[:, : 2 * units]
        dn[rows, :] = piece[:, 2 * units :]
    held[...] = stacked(hidden, hidden[0].shape[0])
    size = held.shape[0] // 2

    @pl.loop(0, 2)
    def _(i):
        rows = pl.ds(pl.multiple_of(i * size, 128), size)
        both = dot(held[rows, :], gu[...], NN)
        gate_up[rows, :] = both
        up, gate = both[:, :units], both[:, units:]
        value = (gate * jax.nn.sigmoid(gate) * up).astype(BF)
        inner[rows, :] = value
        part = dot(value, dn[...], NT).astype(BF)
        for j, out in enumerate((near, far)):

            @pl.when(i == j)
            def _():
                out[...] = part


def backward_kernel(units, *refs):
    pieces, (gu, dn, gate_up, grads, near, far, held) = refs[:-7], refs[-7:]
    held[...] = stacked(pieces, pieces[0].shape[0])
    size = held.shape[0] // 2

    @pl.loop(0, 2)
    def _(i):
        rows = pl.ds(pl.multiple_of(i * size, 128), size)
        grad_inner = dot(held[rows, :], dn[...], NN)
        up, gate = gate_up[rows, :units], gate_up[rows, units:]
        sigma = jax.nn.sigmoid(gate)
        grads[rows, :units] = (grad_inner * gate * sigma).astype(BF)
        grads[rows, units:] = (grad_inner * up * sigma * (1.0 + gate * (1.0 - sigma))).astype(BF)
        part = dot(grads[rows, :], gu[...], NT).astype(BF)
        for j, out in enumerate((near, far)):

            @pl.when(i == j)
            def _():
                out[...] = part


def write_blocks(held, starts, outs):
    for i, out in enumerate(outs):
        out[...] = held[pl.ds(pl.multiple_of(starts[i], 16), out.shape[0]), :]


def block_structs(features, width, ring):
    if not ring:
        return [struct((features, width), BF)]
    share = features // len(CYCLE)
    sizes = [share] * 4 + [share // 2] * 2 + [share] * 3
    return [struct((n, width), BF) for n in sizes]


def ffn_grad_kernel(units, n_blocks, starts, *refs):
    hidden, g, (grads, inner) = refs[:2], refs[2:4], refs[4:6]
    outs, held = refs[6 : 6 + n_blocks], refs[6 + n_blocks]
    own = hidden[0].shape[0]
    turned = stacked(hidden, own).T
    for t in range(0, 2 * units, units):
        held[:, t : t + units] = dot(turned, grads[:, t : t + units], NN).astype(BF)
    held[:, 2 * units :] = dot(stacked(g, own).T, inner[...], NN).astype(BF)
    write_blocks(held, starts, outs)


def prepare_kernel(heads, taken, *refs):
    pieces, (w_out, context, log_total, package) = refs[:2], refs[2:]
    g = stacked(pieces, taken)
    rows = HEAD + AUX
    grad = dot(w_out[...], g, NT).astype(BF)

    def sums(piece):
        both = piece[taken : taken + 16].astype(F32)
        return both[:4] + both[4:8]

    total = sums(pieces[0]) + sums(pieces[1])
    high = total.astype(BF).astype(F32)
    both = jnp.concatenate([high, total - high], axis=0)
    index = lax.broadcasted_iota(jnp.int32, (AUX - 8, g.shape[0]), 0)
    for h in range(heads):
        part = grad[h * HEAD : (h + 1) * HEAD]
        package[h * rows : h * rows + HEAD] = part
        delta = jnp.sum(part.astype(F32) * context[h], axis=0, keepdims=True)
        tail = jnp.zeros(index.shape, F32)
        for at, value in ((0, -log_total[h : h + 1]), (3, -delta)):
            for j in range(3):
                high = value.astype(BF).astype(F32)
                tail = jnp.where(index == at + j, high, tail)
                value = value - high
        norm = both[:, h * NORM_LANES : (h + 1) * NORM_LANES]
        norm = jnp.concatenate([norm, jnp.zeros((8, g.shape[0] - NORM_LANES), F32)], axis=1)
        package[h * rows + HEAD : (h + 1) * rows] = jnp.concatenate([norm, tail], axis=0).astype(BF)


def turn_back(first, second, cosine, sine):
    return jnp.concatenate([first * cosine + second * sine, second * cosine - first * sine], axis=0)


def early_grad_kernel(heads, taken, n_x, slots, *refs):
    x_refs, g_refs, refs = refs[:n_x], refs[n_x : n_x + 2], refs[n_x + 2 :]
    grad_query, turn, context, mixed, held = refs
    half = HEAD // 2
    scale = 1.0 / math.sqrt(HEAD)
    for h in range(heads):
        value = grad_query[h] * scale
        mixed[h * HEAD : (h + 1) * HEAD] = turn_back(value[:half], value[half:], turn[:half], turn[half:]).astype(BF)
    x = stacked(x_refs, x_refs[0].shape[0])
    width = heads * HEAD
    held[:, :width] = dot(mixed[...], x, NN).T.astype(BF)
    held[:, width:] = dot(context[...], stacked(g_refs, taken), NN).T.astype(BF)


def late_grad_kernel(heads, n_x, n_blocks, slots, starts, *refs):
    x_refs, refs = refs[:n_x], refs[n_x:]
    mixed_q, grad_key, grad_value, early, turn, weight, near, far, *refs = refs
    outs, held, mixed = refs[:n_blocks], refs[n_blocks], refs[n_blocks + 1]
    half = HEAD // 2
    width = heads * HEAD
    mixed[:width] = mixed_q[...]
    for h in range(heads):
        value = grad_key[h]
        mixed[width + h * HEAD : width + (h + 1) * HEAD] = turn_back(
            value[:half], value[half:], turn[:half], turn[half:]
        ).astype(BF)
        mixed[2 * width + h * HEAD : 2 * width + (h + 1) * HEAD] = grad_value[h].astype(BF)
    back = dot(mixed[...], weight[...], TN)
    size = near.shape[0]
    near[...] = back[:size].astype(BF)
    far[...] = back[size:].astype(BF)
    x = stacked(x_refs, x_refs[0].shape[0])
    held[:, : 2 * width] = early[...]
    held[:, 2 * width :] = dot(mixed[width:], x, NN).T.astype(BF)
    write_blocks(held, starts, outs)


def finish_ffn_kernel(units, block, ahead, back, gu, dn):
    total = block[...].astype(F32) + ahead[...].astype(F32) + back[...].astype(F32)
    gu[:, 0, :] = total[:, :units]
    gu[:, 1, :] = total[:, units : 2 * units]
    dn[...] = total[:, 2 * units :]


def finish_mix_kernel(width, block, ahead, back, mix, out):
    total = block[...].astype(F32) + ahead[...].astype(F32) + back[...].astype(F32)
    mix[0] = total[:, :width]
    mix[1] = total[:, 2 * width : 3 * width]
    mix[2] = total[:, 3 * width :]
    out[...] = total[:, width : 2 * width].T


NORM_ROWS = 24


def norm_total_kernel(rows, *refs):
    pieces, (out, held) = refs[:-2], refs[-2:]
    at = 0
    for piece in pieces:
        for i in range(piece.shape[0]):
            held[rows[at]] = piece[i]
            at += 1
    total = held[0]
    for r in range(1, at):
        total = total + held[r]
    for i in range(NORM_ROWS // 8):
        part = total[8 * i : 8 * i + 8]
        out[:, i * NORM_LANES : (i + 1) * NORM_LANES] = part[:4] + part[4:]


def slot_tables(seq_lengths, packed_order, wanted, local, waits):
    blocks = packed_order.reshape(-1, local)
    index = jnp.arange(blocks.shape[0], dtype=jnp.int32)
    slots = jnp.sum(
        jnp.where(wanted[:, None, None] == index[None, :, None], blocks[None], 0), axis=1
    ).reshape(1, -1)
    count = seq_lengths.shape[0]
    seq = jnp.zeros_like(slots)
    start = jnp.zeros_like(slots)
    end = jnp.int32(0)
    for s in range(count):
        end = end + seq_lengths[s]
        passed = slots >= end
        seq = seq + passed.astype(jnp.int32)
        start = jnp.where(passed, end, start)
    positions = after((slots - start).astype(F32), waits[0])
    half = HEAD // 2
    freqs = ROPE_BASE ** (-jnp.arange(half, dtype=F32) * 2.0 / HEAD)
    angles = positions * freqs[:, None]
    turn = jnp.concatenate([jnp.cos(angles), jnp.sin(angles)], axis=0)
    line = jnp.arange(3 * AUX, dtype=jnp.int32)[:, None]
    member = lax.rem(line, AUX) == after(seq, waits[1])
    ones = ((line >= 8) & (line < 11)) | ((line >= 2 * AUX + 11) & (line < 2 * AUX + 14))
    marks = jnp.where(ones, 1.0, 0.0)
    marks = jnp.where((line < 8) & member, 1.0, marks)
    marks = jnp.where((line >= AUX) & (line < AUX + 8) & ~member, FAR, marks)
    return turn, marks.astype(BF)


def local(
    tokens,
    w_qkv,
    w_out,
    w_gate_up,
    w_down,
    gain1,
    bias1,
    gain2,
    bias2,
    cotangent,
    seq_lengths,
    packed_order,
):
    rows = lax.axis_size("row")
    row, col = lax.axis_index("row"), lax.axis_index("col")
    ring = rows == len(CYCLE)
    own, features = tokens.shape
    group = own * lax.axis_size("col")
    total = group * rows
    share = w_qkv.shape[0]
    width = w_qkv.shape[2]
    heads = width // HEAD
    units = w_gate_up.shape[2]
    gains = [v.reshape(1, features) for v in (gain1, bias1, gain2, bias2)]

    early = jnp.concatenate([w_qkv.reshape(share, 3 * width), w_out.T], axis=1)
    late = jnp.concatenate([w_gate_up.reshape(share, 2 * units), w_down.T], axis=1)

    pair = tokens_pair = jnp.concatenate([tokens, col_swap(tokens, 2)], axis=0)
    taken = pair.shape[0]
    if ring:
        place = cycle_place()
        half = share // 2
        starts = cycle_rows(place, (0, *ROUND_STEPS)) * share + jnp.array([0] * 8 + [half], jnp.int32)
        block_starts = cycle_rows(place, BLOCK_STEPS) * share + jnp.array([0] * 5 + [half] + [0] * 3, jnp.int32)
        layout = [(ROUND_STEPS[2 * i + j], o) for i in range(3) for o in OFFSETS for j in range(2)]
        layout += [(step, o) for step in (0, 4) for o in OFFSETS]
        wanted = cycle_rows(place, [step for step, _ in layout]) * len(OFFSETS)
        wanted = wanted + (col ^ jnp.array([o for _, o in layout], jnp.int32))
        token_half = own // 2
        (packed,) = call(
            functools.partial(pack_kernel, 2),
            "pack",
            [w_qkv.transpose(1, 0, 2), w_out, tokens],
            [struct((share + own, features), BF)],
        )
        ring_early = Rounds(packed, 0)
        waits = [ring_early.step(), ring_early.step()]
        ring_early.step()
        ring_early.step()
        packed_order = after(packed_order, waits[0])

        def token_rows(v):
            step = half + token_half
            return [v[i + half : i + step] for i in range(0, v.shape[0], step)]

    else:
        starts = block_starts = jnp.zeros((1,), jnp.int32)
        wanted = jnp.arange(rows, dtype=jnp.int32)[:, None] * len(OFFSETS)
        wanted = (wanted + (col ^ jnp.array(OFFSETS, jnp.int32))[None, :]).reshape(-1)
        waits = (), ()
        early_full = lax.all_gather(early, "row", axis=0, tiled=True)
        w_mix, full_out = assemble([early_full], [[(0, features, 0)]], starts, 3 * width)

    turn, marks = slot_tables(seq_lengths, packed_order, wanted, own, waits)
    if ring:
        cuts = [[(0, half, 0), (half + token_half, half, half)]] * 7 + [[(0, half, 0)]] * 2
        w_mix, full_out = assemble([ring_early.block, *ring_early.pieces()], cuts, starts, 3 * width)
    fixed = (w_mix, turn, marks, heads, total, group)
    if ring:
        pair = after(pair, ring_early.done[3])
    x_pieces = [pair, col_swap(pair, 1)]

    def at(slot):
        return jnp.asarray(slot, jnp.int32).reshape(1)

    own_slot = at(6) if ring else at(row)
    keys, values, queries, own_q, *state = attend("first", x_pieces, own_slot, *fixed)
    if ring:
        late_ring = Rounds(late, 0)
        rounds = ring_early.done

        def side(held):
            both = jnp.concatenate([rows for v in held for rows in token_rows(v)], axis=0)
            return jnp.concatenate([both, col_swap(both, 2)], axis=0)

        def middle(i, chunk):
            return attend(
                "middle",
                [chunk, col_swap(chunk, 1)],
                at(i),
                *fixed,
                (own_q, *state, keys, values, queries),
            )

        one = side(rounds[0])
        two = side(after(rounds[1], one))
        three = side(after(rounds[2], two))
        late_ring.step(rounds[2])
        two = after(two, state[0])
        keys, values, queries, *state = middle(0, after(one, rounds[3]))
        both = [rows for v in after(rounds[3], three) for rows in token_rows(v)]
        both = jnp.concatenate([*both, cotangent], axis=0)
        swapped = col_swap(both, 2)
        far = jnp.concatenate([both[:own], swapped[:own]], axis=0)
        other_cotangent = swapped[own:]
        three = after(three, state[0])
        keys, values, queries, *state = middle(1, after(two, late_ring.done[0]))
        late_ring.step()
        far = after(far, state[0])
        keys, values, queries, *state = middle(2, three)
        far = after(far, late_ring.done[1])
        keys, values, queries, *finished = attend(
            "last",
            [far, col_swap(far, 1)],
            at(7),
            *fixed,
            (own_q, *state, keys, values, queries),
            full_out,
        )
    else:
        blocks = lax.all_gather(jnp.concatenate(x_pieces, axis=0), "row", axis=0, tiled=False)

        def block(i):
            slot = lax.rem(row + i, rows)
            return [lax.dynamic_index_in_dim(blocks, slot, 0, keepdims=False)], at(slot)

        def step(i, carried):
            *state, keys, values, queries = carried
            keys, values, queries, *state = attend(
                "middle", *block(i), *fixed, (own_q, *state, keys, values, queries)
            )
            return (*state, keys, values, queries)

        *state, keys, values, queries = lax.fori_loop(1, rows - 1, step, (*state, keys, values, queries))
        keys, values, queries, *finished = attend(
            "last", *block(rows - 1), *fixed, (own_q, *state, keys, values, queries), full_out
        )
    near, far, context_bf, context, log_total = finished

    if ring:
        late_ring.step()
        near = after(near, late_ring.done[2])
        late_ring.step()
    else:
        late_pieces = [lax.all_gather(late, "row", axis=0, tiled=True)]

    if not ring:
        other_cotangent = col_swap(cotangent, 2)
    cotangent_pair = jnp.concatenate([cotangent, other_cotangent], axis=0)
    part = struct((group // 2, features), BF)
    flat, flat_bf = struct((taken, features), F32), struct((taken, features), BF)
    residual1, hidden = call(
        first_norm_kernel,
        "first_norm",
        [*col_exchange(near, far), after(tokens_pair, late_ring.done[3]) if ring else tokens_pair, *gains[:2]],
        [flat, flat_bf],
    )
    if ring:
        late_pieces = [late, *late_ring.pieces()]
    hidden_pieces = [hidden, col_swap(hidden, 1)]
    w_gu, w_dn, gate_up, inner, near, far = call(
        functools.partial(forward_kernel, len(late_pieces), units),
        "ffn_forward",
        [*late_pieces, *hidden_pieces],
        [
            struct((features, 2 * units), BF),
            struct((features, units), BF),
            struct((group, 2 * units), F32),
            struct((group, units), BF),
            part,
            part,
        ],
        prefetch=[starts],
        scratch=[pltpu.VMEM((group, features), BF)],
        flops=6 * group * features * units,
    )
    result, grad_res2, grad_bf, sums2 = call(
        second_norm_kernel,
        "second_norm",
        [*col_exchange(near, far), residual1, *gains, cotangent_pair],
        [struct((own, features), BF), flat, flat_bf, struct((8, features), F32)],
    )
    grad_pieces = [grad_bf, col_swap(grad_bf, 1)]
    grad_gate_up, near, far = call(
        functools.partial(backward_kernel, units),
        "ffn_backward",
        [*grad_pieces, w_gu, w_dn, gate_up],
        [struct((group, 2 * units), BF), part, part],
        scratch=[pltpu.VMEM((group, features), BF)],
        flops=6 * group * features * units,
    )
    exchanged = col_exchange(near, far)
    outs = block_structs(features, 3 * units, ring)
    blocks = call(
        functools.partial(ffn_grad_kernel, units, len(outs)),
        "ffn_grad",
        [*hidden_pieces, *grad_pieces, grad_gate_up, inner],
        outs,
        prefetch=[block_starts],
        scratch=[pltpu.VMEM((features, 3 * units), BF)],
        flops=6 * group * features * units,
    )
    residual1 = after(residual1, blocks)
    ffn_sum = RowSum(blocks)
    sent = ffn_sum.step()
    grad_res1, package = call(
        first_norm_back_kernel,
        "first_norm_back",
        [*exchanged, residual1, gains[0], grad_res2, sums2],
        [struct((own, features), F32), struct((taken + 16, features), BF)],
    )
    attn_pieces = after([package, col_swap(package, 1)], sent)
    (package,) = call(
        functools.partial(prepare_kernel, heads, taken),
        "prepare",
        [*attn_pieces, full_out, context, log_total],
        [struct((heads * (HEAD + AUX), group), BF)],
        flops=2 * width * features * group,
    )
    span = min(2 * group, total)
    steps_all = total // span
    grad_query = jnp.zeros((heads, HEAD, group), F32)
    if ring:
        package_ring = Rounds(package, 1)
        package_ring.step()
        sent = ffn_sum.step()
    grad_query = query_grad(own_q, package, keys, values, heads, span, 0, steps_all, grad_query)
    own_turn = pl.BlockSpec((HEAD, group), lambda i, s, *_: (0, s[0]))
    args = [*x_pieces, *attn_pieces, grad_query, turn, context_bf]
    specs = [whole(a.shape) for a in args]
    specs[-2] = own_turn
    mixed_q, early_grad = call(
        functools.partial(early_grad_kernel, heads, taken, len(x_pieces)),
        "early_grad",
        args,
        [struct((width, group), BF), struct((features, 2 * width), BF)],
        prefetch=[own_slot],
        specs=specs,
        flops=4 * width * features * group,
    )

    def key_step(pieces, chunks, slot, sums):
        slots = jnp.where(jnp.arange(2) == 0, at(slot), own_slot)
        step = own if chunks == 2 else pieces[0].shape[1]
        *sums, norms = key_grad(
            pieces, chunks, step, slots, queries, keys, values, heads, group, tuple(sums)
        )
        return sums, norms

    norm_out = struct((4, features), F32)
    if ring:
        package_ring.step(early_grad)
        sums, norms = key_step([after(package, early_grad, package_ring.done[0])], 1, 6, ())
        sums = after(sums, sent)
        norm_pieces = [norms]
        for i in range(3):
            sums, norms = key_step(package_ring.done[i], 2, i, sums)
            norm_pieces.append(norms)
            if i < 2:
                package_ring.step(norms)
        ffn_sum.moving = after(ffn_sum.moving, norms)
        sums, norms = key_step(package_ring.done[3], 1, 7, sums)
        norm_pieces.append(norms)
        (norm_sums,) = call(
            norm_total_kernel,
            "norm_total",
            norm_pieces,
            [norm_out],
            prefetch=[cycle_rows(place, (0, *ROUND_STEPS[:7]))],
            scratch=[pltpu.VMEM((rows, NORM_ROWS, NORM_LANES), F32)],
        )
    else:
        packages = lax.all_gather(package, "row", axis=0, tiled=False)

        def step(i, carried):
            sums, norms = carried
            piece = lax.dynamic_index_in_dim(packages, i, 0, keepdims=False)
            sums, more = key_step([piece], 1, i, sums)
            return tuple(sums), norms + more

        zeros = jnp.zeros((heads, HEAD, group), F32)
        sums, norms = lax.fori_loop(
            0, rows, step, ((zeros, zeros), jnp.zeros((1, NORM_ROWS, NORM_LANES), F32))
        )
        (norm_sums,) = call(
            norm_total_kernel,
            "norm_total",
            [norms],
            [norm_out],
            prefetch=[jnp.zeros((1,), jnp.int32)],
            scratch=[pltpu.VMEM((1, NORM_ROWS, NORM_LANES), F32)],
        )
    args = [*x_pieces, mixed_q, *sums, early_grad, turn, w_mix]
    specs = [whole(a.shape) for a in args]
    specs[-2] = own_turn
    outs = block_structs(features, 4 * width, ring)
    near, far, *blocks = call(
        functools.partial(late_grad_kernel, heads, len(x_pieces), len(outs)),
        "late_grad",
        args,
        [part, part, *outs],
        prefetch=[own_slot, block_starts],
        scratch=[pltpu.VMEM((features, 4 * width), BF), pltpu.VMEM((3 * width, group), BF)],
        specs=specs,
        flops=10 * width * features * group,
    )
    late_sum = RowSum(blocks)
    late_sum = late_sum.terms()
    grad_gu, grad_dn = call(
        functools.partial(finish_ffn_kernel, units),
        "finish_ffn",
        ffn_sum.terms(),
        [struct((share, 2, units), F32), struct((share, units), F32)],
        cost=20.0,
    )
    grad_tokens = grad_res1 + col_sum(near, far)
    grad_mix, grad_out = call(
        functools.partial(finish_mix_kernel, width),
        "finish_mix",
        late_sum,
        [struct((3, share, width), F32), struct((width, share), F32)],
        cost=20.0,
    )
    return (
        result,
        grad_tokens,
        grad_mix.transpose(1, 0, 2),
        grad_out,
        grad_gu,
        grad_dn.T,
        norm_sums[0],
        norm_sums[1],
        norm_sums[2],
        norm_sums[3],
    )


def solution(mesh):
    placed = (
        P(("row", "col"), None),
        P("row", None, "col"),
        P("col", "row"),
        P("row", None, "col"),
        P("col", "row"),
        P(),
        P(),
        P(),
        P(),
        P(("row", "col"), None),
        P(),
        P(),
    )
    return jax.shard_map(
        local,
        mesh=mesh,
        in_specs=placed,
        out_specs=(
            P(("row", "col"), None),
            P(("row", "col"), None),
            P("row", None, "col"),
            P("col", "row"),
            P("row", None, "col"),
            P("col", "row"),
            P(),
            P(),
            P(),
            P(),
        ),
        check_vma=False,
    )
```
